32 devices in a mesh: req: 16 (over z, y, core), tp: 2 (over x).
Axes of the slice: x: 2, y: 2, z: 4, core: 2. Of those that a mesh axis runs over, the one named last changes fastest.
Arguments:
- queries: bfloat16 [1024, 2048], P('req', 'tp'), may hold values from -18 to 18
- fresh_key_value: bfloat16 [1024, 1024], P('req', 'tp'), may hold values from -6 to 6
- key_value_cache: bfloat16 [64, 128, 1024], P('req', None, 'tp'), may hold values from -12.2 to 12.2
- request_page_index: int32 [144, 4], P('req'), may hold values from 0 to 3
- cache_length_rows: int32 [144], P('req'), may hold values from 2 to 512, as said below
- residual: bfloat16 [1024, 2048], P('req'), may hold values from -12.8 to 12.8
- w_out: bfloat16 [2048, 2048], P('tp'), may hold values from -0.125 to 0.125
- gain_in: float32 [2048], replicated, may hold values from 0.5 to 1.5
- route_ids: int32 [1024, 8], P('req'), may hold values from 0 to 15, all different within a row; in each aligned block of 32 rows (0 to 31, 32 to 63, ...) at most 32 rows name the same one
- route_weights: float32 [1024, 8], P('req'), may hold values from 0.1 to 1
- expert_home: int32 [16], replicated, may hold values from 0 to 15, each once
- w_gate: bfloat16 [16, 2048, 768], P('req', None, 'tp'), may hold values from -0.125 to 0.125
- w_up: bfloat16 [16, 2048, 768], P('req', None, 'tp'), may hold values from -0.125 to 0.125
- w_down: bfloat16 [16, 768, 2048], P('req', 'tp'), may hold values from -0.21875 to 0.21875
- gain_out: float32 [2048], replicated, may hold values from 0.5 to 1.5
Outputs:
- normed: bfloat16 [1024, 2048], P(('req', 'tp'))
The draws below stay inside these ranges and needn't reach their ends.
Inputs may be any that keep to these rules, and one draw needn't show every extreme that they name: `route_ids`: each row names 8 different experts; in each aligned block of 32 rows no expert is named by more than 32 rows, and in some block some expert by exactly 32. `expert_home`: each expert is held by exactly one group. `request_page_index`: entries number pages among the 4 pages of the request's own group; a page may be named by several requests and entries. `cache_length_rows`: in every group one request has exactly 512 cached tokens.
All inputs are finite; a program needn't handle non-finite values.
Results may differ from the reference program's by a relative error of at most 0.0058.
Values may be sent and summed in bfloat16 or wider, within the bound.
No kernel may reach another device: no remote copies, remote signals or barrier semaphores. Data moves between devices by JAX's collectives and lax.ppermute only.
A program may use at most 64 MiB of HBM per device.

```python
import math
import jax
import jax.numpy as jnp
import numpy as np
from jax import lax

D = 2048
QUERY_HEADS = 16
KEY_VALUE_HEADS = 4
HEAD_WIDTH = 128
FF = 768
TOPK = 8
PAGE_TOKENS = 128
PRE_DEV = 56
REQUEST_PAGES = 4
GROUP_PAGES = 4
EXPERTS = 16
GROUP_TOKENS = 64
TQ = 32
MOST = 32
GROUP_REQUESTS = 9
TOKEN_TOTAL = 1024
REQ_ALL = 144
TOTAL_PAGES = 64
N_REQ = 16
N_TP = 2


def draw_queries(key, part):
    value_rows = jnp.clip(jax.random.normal(jax.random.fold_in(key, 11), (TOKEN_TOTAL, QUERY_HEADS, HEAD_WIDTH), jnp.float32), -6.0, 6.0)
    return value_rows.reshape(TOKEN_TOTAL, QUERY_HEADS * HEAD_WIDTH).astype(jnp.bfloat16)


def draw_key_value_cache(key, part):
    full_shape_tuple = (TOTAL_PAGES, PAGE_TOKENS, KEY_VALUE_HEADS, 2, HEAD_WIDTH)
    value_rows = jnp.clip(jax.random.normal(jax.random.fold_in(key, 23), full_shape_tuple, jnp.float32), -6.0, 6.0)
    return value_rows.reshape(TOTAL_PAGES, PAGE_TOKENS, KEY_VALUE_HEADS * 2 * HEAD_WIDTH).astype(jnp.bfloat16)


def draw_residual(key, part):
    value_rows = 0.3 * jnp.clip(jax.random.normal(jax.random.fold_in(key, 37), (TOKEN_TOTAL, D), jnp.float32), -6.0, 6.0)
    return value_rows.astype(jnp.bfloat16)


def draw_cache_length_rows(key, part):
    groups_all = TOKEN_TOTAL // GROUP_TOKENS
    lengths = jax.random.randint(jax.random.fold_in(key, 51), (groups_all, GROUP_REQUESTS), 2, REQUEST_PAGES * PAGE_TOKENS + 1)
    longest = jax.random.randint(jax.random.fold_in(key, 52), (groups_all,), 0, GROUP_REQUESTS)
    lengths = jnp.where(jnp.arange(GROUP_REQUESTS)[None, :] == longest[:, None], REQUEST_PAGES * PAGE_TOKENS, lengths)
    return lengths.reshape(-1).astype(jnp.int32)


def with_ends(values, rng, least, top_value):
    spot = [jax.random.randint(jax.random.fold_in(rng, axis), (), 0, length) for axis, length in enumerate(values.shape)]
    widest = values.shape.index(max(values.shape))
    beside = spot[:widest] + [(spot[widest] + 1) % values.shape[widest]] + spot[widest + 1:]
    return values.at[tuple(spot)].set(least).at[tuple(beside)].set(top_value)


def levels(stream_key, extent, cuts, least, high):
    def one(dim, blocks):
        steps = jax.random.uniform(jax.random.fold_in(jax.random.fold_in(stream_key, 6), dim), (blocks,), jnp.float32, least / len(cuts), high / len(cuts))
        return jnp.repeat(jnp.exp(steps), extent[dim] // blocks).reshape((-1,) + (1,) * (len(extent) - dim - 1))

    factor_of = one(*cuts[0])
    for cut in cuts[1:]:
        factor_of = factor_of * one(*cut)
    return factor_of


def shared_out(stream_key, own, number, rows, number_of, top, limit, skew):
    ranking = jax.random.permutation(stream_key, number_of)
    packed, common = portions_of(number_of, rows * top, limit, skew, True), portions_of(number_of, rows * top, limit, skew, False)
    places = jnp.arange(number_of)

    def named(sizes, offset_by):
        used = int((sizes > 0).sum())
        fixed = max(1, used // 4)
        shifted = fixed + (places - fixed + offset_by * (used - fixed)) % max(1, number_of - fixed)
        return jnp.zeros((number_of,), jnp.int32).at[ranking[jnp.where(places < fixed, places, shifted)]].set(jnp.asarray(sizes, jnp.int32))

    sizes = jnp.where(number % 4 == 0, named(packed, number // 4), named(common, number - number // 4 - 1))
    mixed = jax.random.permutation(jax.random.fold_in(own, 3), number_of)
    giver, receiver = mixed[0:number_of // 2 * 2:2], mixed[1:number_of // 2 * 2:2]
    room = jnp.minimum(sizes[giver] - 1, limit - sizes[receiver]) // 2
    room = jnp.where((giver == ranking[0]) | (receiver == ranking[0]) | (sizes[receiver] == 0), 0, jnp.maximum(room, 0))
    shifted = jax.random.randint(jax.random.fold_in(own, 4), (number_of // 2,), 0, 1 << 20) % (room + 1)
    sizes = sizes.at[giver].add(-shifted).at[receiver].add(shifted)
    items = jnp.searchsorted(jnp.cumsum(sizes), jnp.arange(rows * top), side="right").astype(jnp.int32)
    listing = items.reshape(top, rows).T
    listing = listing[jax.random.permutation(jax.random.fold_in(own, 1), rows)]
    offset_by = jax.random.randint(jax.random.fold_in(own, 2), (rows, 1), 0, top)
    return jnp.take_along_axis(listing, (jnp.arange(top)[None, :] + offset_by) % top, axis=1)


def portions_of(number_of, total, bound, skew, full):
    portions = [(1 << 20) // math.isqrt(rank ** skew) + 1 for rank in range(1, number_of + 1)]
    largest = bound if full else min(bound, max(-(-total // number_of), total * portions[0] // sum(portions)))
    least = 1 if total - largest >= number_of - 1 else 0
    counts, spare = [largest] + [least] * (number_of - 1), total - largest - least * (number_of - 1)
    while spare > 0:
        movable = [i for i in range(1, number_of) if counts[i] < largest] or [i for i in range(1, number_of) if counts[i] < bound]
        pool, remaining = sum([portions[i] for i in movable]), spare
        for i in movable:
            addition = min(bound - counts[i], max(1, remaining * portions[i] // pool), spare)
            counts[i] = counts[i] + addition
            spare = spare - addition
    return np.array(counts)


def noise(key, dims, deviation, reach, cuts=(), held_as=jnp.bfloat16):
    drawn = jax.random.normal(key, dims, jnp.float32) * deviation
    if len(cuts) > 0:
        drawn = levels(key, dims, cuts, -0.22, 0.18) * drawn
    return jnp.clip(drawn, min=-reach, max=reach).astype(held_as)


def setup_inputs(seed: int = 0) -> dict:
    key_of = jax.random.split(jax.random.key(seed), 16)
    queries = draw_queries(jax.random.fold_in(key_of[15], 71), 0)
    fresh_key_value = noise(key_of[1], (TOKEN_TOTAL, KEY_VALUE_HEADS * 2 * HEAD_WIDTH), 1.0, 6.0, ((0, 16), (1, 2)))
    key_value_cache = draw_key_value_cache(jax.random.fold_in(key_of[15], 71), 0)
    request_page_index = with_ends(jax.random.randint(key_of[3], (REQ_ALL, REQUEST_PAGES), 0, GROUP_PAGES), jax.random.fold_in(key_of[3], 1), 0, GROUP_PAGES - 1).astype(jnp.int32)
    cache_length_rows = draw_cache_length_rows(jax.random.fold_in(key_of[15], 71), 0)
    residual = draw_residual(jax.random.fold_in(key_of[15], 71), 0)
    w_out = noise(key_of[6], (QUERY_HEADS * HEAD_WIDTH, D), (QUERY_HEADS * HEAD_WIDTH) ** -0.5, 0.125, ((0, 2),))
    gain_in = jnp.clip(1.0 + 0.1 * jax.random.normal(key_of[7], (D,), jnp.float32), 0.5, 1.5)
    route_ids_keys = jax.random.split(jax.random.fold_in(key_of[8], 1), TOKEN_TOTAL // TQ)
    route_ids_turns = jax.random.permutation(jax.random.fold_in(key_of[8], 3), TOKEN_TOTAL // TQ)
    route_ids = jax.vmap(lambda own, number: shared_out(jax.random.fold_in(key_of[8], 2), own, number, TQ, EXPERTS, TOPK, MOST, 2))(route_ids_keys, route_ids_turns).reshape((TOKEN_TOTAL, TOPK))
    route_weights = jnp.clip(jnp.exp(math.log(1.0) - 2.3025851 * jax.random.uniform(key_of[9], (TOKEN_TOTAL, TOPK), jnp.float32) ** levels(key_of[9], (TOKEN_TOTAL, TOPK), ((0, 16),), -0.2, 0.2)), 0.1, 1.0)
    expert_home = jax.random.permutation(key_of[10], EXPERTS).astype(jnp.int32)
    w_gate = noise(key_of[11], (EXPERTS, D, FF), D ** -0.5, 0.125, ((0, 16), (2, 2)))
    w_up = noise(key_of[12], (EXPERTS, D, FF), D ** -0.5, 0.125, ((0, 16), (2, 2)))
    w_down = noise(key_of[13], (EXPERTS, FF, D), FF ** -0.5, 0.21875, ((0, 16), (1, 2)))
    gain_out = jnp.clip(1.0 + 0.1 * jax.random.normal(key_of[14], (D,), jnp.float32), 0.5, 1.5)
    return {"queries": queries, "fresh_key_value": fresh_key_value, "key_value_cache": key_value_cache, "request_page_index": request_page_index, "cache_length_rows": cache_length_rows, "residual": residual, "w_out": w_out, "gain_in": gain_in, "route_ids": route_ids, "route_weights": route_weights, "expert_home": expert_home, "w_gate": w_gate, "w_up": w_up, "w_down": w_down, "gain_out": gain_out}


EPSILON = 1e-06

def rms_scale(value_rows, gain_row):
    mean_square = lax.optimization_barrier(jnp.mean(value_rows * value_rows, axis=-1, keepdims=True))
    return value_rows * lax.rsqrt(mean_square + EPSILON) * gain_row

def softmax_rounded(scores):
    row_peak = lax.optimization_barrier(jnp.max(scores, axis=-1, keepdims=True))
    weights = jnp.exp(scores - row_peak)
    return (weights / lax.optimization_barrier(jnp.sum(weights, axis=-1, keepdims=True))).astype(jnp.bfloat16)

def group_attention(queries, fresh_key_value, page_pool, page_rows, lengths):
    tokens_here = queries.shape[0]
    kv_heads = fresh_key_value.shape[1] // (2 * HEAD_WIDTH)
    group_size = queries.shape[1] // (HEAD_WIDTH * kv_heads)
    score_scale = HEAD_WIDTH ** (-0.5)
    split_query = queries.reshape(tokens_here, kv_heads, group_size, HEAD_WIDTH).astype(jnp.float32)
    fresh_kv = fresh_key_value.reshape(tokens_here, kv_heads, 2, HEAD_WIDTH).astype(jnp.float32)
    gathered_pages = page_pool[page_rows]
    cached = gathered_pages.reshape(page_rows.shape[0], -1, kv_heads, 2, HEAD_WIDTH).astype(jnp.float32)
    places = jnp.arange(cached.shape[1], dtype=jnp.int32)
    prefill_query = split_query[:PRE_DEV]
    prefill_fresh = fresh_kv[:PRE_DEV]
    cache_scores = jnp.einsum('ikgd,ckd->kgic', prefill_query, cached[0, :, :, 0]) * score_scale
    cache_scores = jnp.where(places < lengths[0], cache_scores, -jnp.inf)
    block_scores = jnp.einsum('ikgd,jkd->kgij', prefill_query, prefill_fresh[:, :, 0]) * score_scale
    causal = jnp.arange(PRE_DEV)[:, None] >= jnp.arange(PRE_DEV)[None, :]
    block_scores = jnp.where(causal, block_scores, -jnp.inf)
    prefill_probs = softmax_rounded(jnp.concatenate([cache_scores, block_scores], axis=3))
    prefill_values = jnp.concatenate([cached[0, :, :, 1], prefill_fresh[:, :, 1]], axis=0)
    prefill_out = jnp.einsum('kgic,ckd->ikgd', prefill_probs.astype(jnp.float32), prefill_values)
    decode_query = split_query[PRE_DEV:]
    decode_fresh = fresh_kv[PRE_DEV:]
    decode_scores = jnp.einsum('rkgd,rckd->rkgc', decode_query, cached[1:, :, :, 0]) * score_scale
    decode_scores = jnp.where(places[None, None, None, :] < lengths[1:, None, None, None], decode_scores, -jnp.inf)
    own_scores = jnp.einsum('rkgd,rkd->rkg', decode_query, decode_fresh[:, :, 0])[..., None] * score_scale
    decode_probs = softmax_rounded(jnp.concatenate([decode_scores, own_scores], axis=3))
    decode_values = jnp.concatenate([cached[1:, :, :, 1], decode_fresh[:, None, :, 1]], axis=1)
    decode_out = jnp.einsum('rkgc,rckd->rkgd', decode_probs.astype(jnp.float32), decode_values)
    joined = jnp.concatenate([prefill_out, decode_out], axis=0)
    return joined.reshape(tokens_here, -1).astype(jnp.bfloat16)

def reference(queries, fresh_key_value, key_value_cache, request_page_index, cache_length_rows, residual, w_out, gain_in, route_ids, route_weights, expert_home, w_gate, w_up, w_down, gain_out):
    grouped_heads = (queries.reshape(N_REQ, GROUP_TOKENS, QUERY_HEADS * HEAD_WIDTH), fresh_key_value.reshape(N_REQ, GROUP_TOKENS, KEY_VALUE_HEADS * 2 * HEAD_WIDTH), key_value_cache.reshape(N_REQ, GROUP_PAGES, PAGE_TOKENS, KEY_VALUE_HEADS * 2 * HEAD_WIDTH), request_page_index.reshape(N_REQ, GROUP_REQUESTS, REQUEST_PAGES), cache_length_rows.reshape(N_REQ, GROUP_REQUESTS))
    context = lax.map(lambda pieces: group_attention(*pieces), grouped_heads).reshape(TOKEN_TOTAL, QUERY_HEADS * HEAD_WIDTH)
    state = residual.astype(jnp.float32) + jnp.dot(context, w_out, preferred_element_type=jnp.float32)
    normed_in = rms_scale(state, gain_in).astype(jnp.bfloat16)
    owner = expert_home[route_ids].reshape(-1).astype(jnp.int32)
    shares = (route_weights / lax.optimization_barrier(jnp.sum(route_weights, axis=1, keepdims=True))).reshape(-1)
    padded_rows = jnp.concatenate([normed_in, jnp.zeros((1, D), jnp.bfloat16)], axis=0)
    padded_shares = jnp.concatenate([shares, jnp.zeros((1,), jnp.float32)], axis=0)
    capacity = N_TP * N_REQ * MOST

    def expert_step(mixture, holder):
        picks = jnp.nonzero(owner == holder, size=capacity, fill_value=TOKEN_TOTAL * TOPK)[0].astype(jnp.int32)
        token_index = (picks // TOPK).astype(jnp.int32)
        expert_rows = padded_rows[token_index].astype(jnp.float32)
        gate_proj = jnp.dot(expert_rows, w_gate[holder].astype(jnp.float32))
        up_proj = jnp.dot(expert_rows, w_up[holder].astype(jnp.float32))
        hidden = (jax.nn.silu(gate_proj) * up_proj).astype(jnp.bfloat16)
        hidden = lax.optimization_barrier(hidden).astype(jnp.float32)
        down_parts = w_down[holder].astype(jnp.float32).reshape(N_TP, FF // N_TP, D)
        partial_value = jnp.einsum('rqf,qfd->qrd', hidden.reshape(capacity, N_TP, FF // N_TP), down_parts)
        partial_value = lax.optimization_barrier(partial_value.astype(jnp.bfloat16)).astype(jnp.float32)
        expert_out = lax.optimization_barrier(jnp.sum(partial_value, axis=0)).astype(jnp.bfloat16)
        expert_out = lax.optimization_barrier(expert_out).astype(jnp.float32)
        mixture = mixture.at[token_index].add(padded_shares[picks][:, None] * expert_out)
        return (mixture, None)
    mixture, _ = lax.scan(expert_step, jnp.zeros((TOKEN_TOTAL + 1, D), jnp.float32), jnp.arange(EXPERTS, dtype=jnp.int32))
    total = state + mixture[:TOKEN_TOTAL]
    return rms_scale(total, gain_out).astype(jnp.bfloat16)
```

```python
import functools

import jax
import jax.numpy as jnp
from jax import lax
from jax.experimental import pallas as pl
from jax.experimental.pallas import tpu as pltpu
from jax.sharding import PartitionSpec as P

HEAD_WIDTH = 128
TOPK = 8
PRE_DEV = 56


EPSILON = 1e-06


def rms_scale(value_rows, gain_row):
    mean_square = jnp.mean(value_rows * value_rows, axis=-1, keepdims=True)
    return value_rows * lax.rsqrt(mean_square + EPSILON) * gain_row


def softmax_rounded(scores):
    row_peak = jnp.max(scores, axis=-1, keepdims=True)
    weights = jnp.exp(scores - row_peak)
    return (weights / jnp.sum(weights, axis=-1, keepdims=True)).astype(jnp.bfloat16)


def group_attention(queries, fresh_key_value, page_pool, page_rows, lengths):
    tokens_here = queries.shape[0]
    kv_heads = fresh_key_value.shape[1] // (2 * HEAD_WIDTH)
    group_size = queries.shape[1] // (HEAD_WIDTH * kv_heads)
    score_scale = HEAD_WIDTH ** (-0.5)
    split_query = queries.reshape(tokens_here, kv_heads, group_size, HEAD_WIDTH)
    fresh_kv = fresh_key_value.reshape(tokens_here, kv_heads, 2, HEAD_WIDTH)
    gathered_pages = page_pool[page_rows]
    cached = gathered_pages.reshape(page_rows.shape[0], -1, kv_heads, 2, HEAD_WIDTH)
    places = jnp.arange(cached.shape[1], dtype=jnp.int32)
    prefill_query = split_query[:PRE_DEV]
    prefill_fresh = fresh_kv[:PRE_DEV]
    cache_scores = (
        jnp.einsum(
            "ikgd,ckd->kgic", prefill_query, cached[0, :, :, 0], preferred_element_type=jnp.float32
        )
        * score_scale
    )
    cache_scores = jnp.where(places < lengths[0], cache_scores, -jnp.inf)
    block_scores = (
        jnp.einsum(
            "ikgd,jkd->kgij",
            prefill_query,
            prefill_fresh[:, :, 0],
            preferred_element_type=jnp.float32,
        )
        * score_scale
    )
    causal = jnp.arange(PRE_DEV)[:, None] >= jnp.arange(PRE_DEV)[None, :]
    block_scores = jnp.where(causal, block_scores, -jnp.inf)
    prefill_probs = softmax_rounded(jnp.concatenate([cache_scores, block_scores], axis=3))
    prefill_values = jnp.concatenate([cached[0, :, :, 1], prefill_fresh[:, :, 1]], axis=0)
    prefill_out = jnp.einsum(
        "kgic,ckd->ikgd", prefill_probs, prefill_values, preferred_element_type=jnp.float32
    )
    decode_query = split_query[PRE_DEV:]
    decode_fresh = fresh_kv[PRE_DEV:]
    decode_scores = (
        jnp.einsum(
            "rkgd,rckd->rkgc", decode_query, cached[1:, :, :, 0], preferred_element_type=jnp.float32
        )
        * score_scale
    )
    decode_scores = jnp.where(
        places[None, None, None, :] < lengths[1:, None, None, None], decode_scores, -jnp.inf
    )
    own_scores = (
        jnp.einsum(
            "rkgd,rkd->rkg", decode_query, decode_fresh[:, :, 0], preferred_element_type=jnp.float32
        )[..., None]
        * score_scale
    )
    decode_probs = softmax_rounded(jnp.concatenate([decode_scores, own_scores], axis=3))
    decode_values = jnp.concatenate([cached[1:, :, :, 1], decode_fresh[:, None, :, 1]], axis=1)
    decode_out = jnp.einsum(
        "rkgc,rckd->rkgd", decode_probs, decode_values, preferred_element_type=jnp.float32
    )
    joined = jnp.concatenate([prefill_out, decode_out], axis=0)
    return joined.reshape(tokens_here, -1).astype(jnp.bfloat16)


def slot_positions(block_owner, experts, capacity):
    flat_owner = block_owner.reshape(-1)
    onehot = (flat_owner[:, None] == jnp.arange(experts, dtype=jnp.int32)[None, :]).astype(
        jnp.int32
    )
    earlier = jnp.cumsum(onehot, axis=0) - onehot
    slot_index = jnp.sum(earlier * onehot, axis=1)
    return (flat_owner * capacity + slot_index).reshape(block_owner.shape)


def place_matrix(positions, slots_total):
    matches = positions[None, :, :] == jnp.arange(slots_total, dtype=jnp.int32)[:, None, None]
    return jnp.any(matches, axis=2).astype(jnp.bfloat16)


def local_sparse(
    queries,
    fresh_key_value,
    key_value_cache,
    request_page_index,
    cache_length_rows,
    residual,
    w_out,
    gain_in,
    route_ids,
    route_weights,
    expert_home,
    w_gate,
    w_up,
    w_down,
    gain_out,
):
    tp_size = lax.axis_size("tp")
    req_size = lax.axis_size("req")
    tp_index = lax.axis_index("tp")
    model_width = residual.shape[1]
    tokens_here = residual.shape[0]
    quarter = tokens_here // tp_size
    experts = expert_home.shape[0]
    capacity = min(quarter, max(2, 2 * quarter * TOPK // experts))
    context = group_attention(
        queries, fresh_key_value, key_value_cache, request_page_index, cache_length_rows
    )
    head_terms = jnp.dot(context, w_out, preferred_element_type=jnp.float32)
    state = residual.astype(jnp.float32) + lax.psum(head_terms, "tp")
    owners = jnp.sum(
        jnp.where(
            route_ids[:, :, None] == jnp.arange(experts, dtype=jnp.int32)[None, None, :],
            expert_home[None, None, :],
            0,
        ),
        axis=2,
    )
    shares = route_weights / jnp.sum(route_weights, axis=1, keepdims=True)
    own_start = tp_index * quarter
    own_state = lax.dynamic_slice_in_dim(state, own_start, quarter, 0)
    own_shares = lax.dynamic_slice_in_dim(shares, own_start, quarter, 0)
    normed_all = rms_scale(state, gain_in).astype(jnp.bfloat16)
    positions_all = jax.vmap(lambda block_owner: slot_positions(block_owner, experts, capacity))(
        owners.reshape(tp_size, quarter, TOPK)
    )
    placing = jax.vmap(lambda positions: place_matrix(positions, experts * capacity))(positions_all)
    outgoing = jnp.einsum(
        "qmi,qid->qmd",
        placing,
        normed_all.reshape(tp_size, quarter, model_width),
        preferred_element_type=jnp.float32,
    )
    outgoing = outgoing.astype(jnp.bfloat16).reshape(tp_size, experts, capacity, model_width)
    incoming = lax.all_to_all(outgoing, "req", split_axis=1, concat_axis=1, tiled=True)
    own_positions = lax.dynamic_index_in_dim(positions_all, tp_index, 0, keepdims=False)
    expert_rows = incoming.reshape(-1, model_width)
    gate_proj = jnp.dot(expert_rows, w_gate[0], preferred_element_type=jnp.float32)
    up_proj = jnp.dot(expert_rows, w_up[0], preferred_element_type=jnp.float32)
    inner_units = (jax.nn.silu(gate_proj) * up_proj).astype(jnp.bfloat16)
    summed = lax.psum_scatter(
        jnp.dot(inner_units, w_down[0], preferred_element_type=jnp.float32).astype(jnp.bfloat16),
        "tp",
        scatter_dimension=0,
        tiled=True,
    )
    results = summed.reshape(req_size, capacity, model_width)
    returned = lax.all_to_all(results, "req", split_axis=0, concat_axis=0, tiled=True).reshape(
        -1, model_width
    )
    picked = returned[own_positions]
    mixture = jnp.sum(own_shares[:, :, None] * picked.astype(jnp.float32), axis=1)
    return rms_scale(own_state + mixture, gain_out).astype(jnp.bfloat16)


ALL = ("req", "tp")
MASKED = -1e30
VMEM_BYTES = 40 * 1024 * 1024


def vmem():
    return pl.BlockSpec(memory_space=pltpu.VMEM)


def smem():
    return pl.BlockSpec(memory_space=pltpu.SMEM)


def multiplicity(page_rows, length, pool_pages, page_tokens):
    rows = page_rows[0].shape[0]
    lane = lax.broadcasted_iota(jnp.int32, (rows, page_tokens), 1)
    parts = []
    for page in range(pool_pages):
        count = jnp.zeros((rows, page_tokens), jnp.float32)
        for slot, named in enumerate(page_rows):
            hit = (named == page) & (lane + slot * page_tokens < length)
            count = count + jnp.where(hit, 1.0, 0.0)
        parts.append(count)
    return jnp.concatenate(parts, axis=1)


def attention_kernel(
    pages_ref, lengths_ref, tp_ref, q_ref, fresh_ref, cache_ref, residual_ref, w_hbm,
    own_ref, send_ref, w_ref, context_ref, terms_ref, w_sem,
):
    fetch = pltpu.make_async_copy(w_hbm, w_ref, w_sem)
    fetch.start()
    tokens = q_ref.shape[0]
    pool_pages, page_tokens, _ = cache_ref.shape
    requests, slots = pages_ref.shape
    kv_heads = fresh_ref.shape[1] // (2 * HEAD_WIDTH)
    group = q_ref.shape[1] // (HEAD_WIDTH * kv_heads)
    decodes = requests - 1
    row = lax.broadcasted_iota(jnp.int32, (decodes, page_tokens), 0)

    def by_row(read):
        value = jnp.zeros((decodes, page_tokens), jnp.int32)
        for j in range(decodes):
            value = jnp.where(row == j, read(j + 1), value)
        return value

    full = lambda scalar: jnp.full((decodes, page_tokens), scalar, jnp.int32)
    first = multiplicity(
        [full(pages_ref[0, s]) for s in range(slots)], full(lengths_ref[0]), pool_pages, page_tokens
    )
    later = multiplicity(
        [by_row(lambda j, s=s: pages_ref[j, s]) for s in range(slots)],
        by_row(lambda j: lengths_ref[j]),
        pool_pages,
        page_tokens,
    )
    count = jnp.concatenate([first] * (PRE_DEV // decodes) + [later], axis=0)
    query_place = lax.broadcasted_iota(jnp.int32, (tokens, tokens), 0)
    key_place = lax.broadcasted_iota(jnp.int32, (tokens, tokens), 1)
    seen = (key_place == query_place) | ((key_place <= query_place) & (query_place < PRE_DEV))
    visible = jnp.concatenate([count] * group, axis=0)
    seen = jnp.concatenate([jnp.where(seen, 1.0, 0.0)] * group, axis=0)
    scale = HEAD_WIDTH**-0.5
    contract_last = (((1,), (1,)), ((), ()))
    for k in range(kv_heads):
        key_at, value_at = 2 * k * HEAD_WIDTH, (2 * k + 1) * HEAD_WIDTH
        query = jnp.concatenate(
            [
                q_ref[:, (k * group + g) * HEAD_WIDTH : (k * group + g + 1) * HEAD_WIDTH]
                for g in range(group)
            ],
            axis=0,
        )
        keys = cache_ref[:, :, key_at : key_at + HEAD_WIDTH].reshape(-1, HEAD_WIDTH)
        values = cache_ref[:, :, value_at : value_at + HEAD_WIDTH].reshape(-1, HEAD_WIDTH)
        old = lax.dot_general(query, keys, contract_last, preferred_element_type=jnp.float32)
        new = lax.dot_general(
            query,
            fresh_ref[:, key_at : key_at + HEAD_WIDTH],
            contract_last,
            preferred_element_type=jnp.float32,
        )
        old = jnp.where(visible > 0, old * scale, MASKED)
        new = jnp.where(seen > 0, new * scale, MASKED)
        peak = jnp.maximum(
            jnp.max(old, axis=1, keepdims=True), jnp.max(new, axis=1, keepdims=True)
        )
        old = jnp.exp(old - peak) * visible
        new = jnp.exp(new - peak) * seen
        inverse = 1.0 / (
            jnp.sum(old, axis=1, keepdims=True) + jnp.sum(new, axis=1, keepdims=True)
        )
        mixed = jnp.dot(
            (old * inverse).astype(jnp.bfloat16), values, preferred_element_type=jnp.float32
        ) + jnp.dot(
            (new * inverse).astype(jnp.bfloat16),
            fresh_ref[:, value_at : value_at + HEAD_WIDTH],
            preferred_element_type=jnp.float32,
        )
        mixed = mixed.astype(jnp.bfloat16)
        for g in range(group):
            h = k * group + g
            context_ref[:, h * HEAD_WIDTH : (h + 1) * HEAD_WIDTH] = mixed[
                g * tokens : (g + 1) * tokens
            ]
    fetch.wait()
    half = tokens // 2
    width = terms_ref.shape[1]
    block = 512
    own_at = pl.multiple_of(tp_ref[0] * half, half)
    other_at = pl.multiple_of((1 - tp_ref[0]) * half, half)
    for at in range(0, width, block):
        cols = slice(at, at + block)
        terms_ref[:, cols] = jnp.dot(
            context_ref[...], w_ref[:, cols], preferred_element_type=jnp.float32
        )
    own_ref[...] = terms_ref[pl.ds(own_at, half), :] + residual_ref[
        pl.ds(own_at, half), :
    ].astype(jnp.float32)
    send_ref[...] = terms_ref[pl.ds(other_at, half), :].astype(jnp.bfloat16)


def attention_terms(pages, lengths, tp_index, queries, fresh, cache, residual, w_out):
    tokens, width = residual.shape
    half = tokens // 2
    return pl.pallas_call(
        attention_kernel,
        out_shape=(
            jax.ShapeDtypeStruct((half, width), jnp.float32),
            jax.ShapeDtypeStruct((half, width), jnp.bfloat16),
        ),
        in_specs=[smem(), smem(), smem(), vmem(), vmem(), vmem(), vmem(),
                  pl.BlockSpec(memory_space=pl.ANY)],
        out_specs=(vmem(), vmem()),
        scratch_shapes=[
            pltpu.VMEM(w_out.shape, jnp.bfloat16),
            pltpu.VMEM(queries.shape, jnp.bfloat16),
            pltpu.VMEM((tokens, width), jnp.float32),
            pltpu.SemaphoreType.DMA,
        ],
        compiler_params=pltpu.CompilerParams(vmem_limit_bytes=VMEM_BYTES),
        name="attention_terms",
    )(pages, lengths, tp_index, queries, fresh, cache, residual, w_out)


def norm_kernel(own_ref, got_ref, gain_ref, state_ref, a_ref, b_ref):
    state = own_ref[...] + got_ref[...].astype(jnp.float32)
    state_ref[...] = state
    normed = rms_scale(state, gain_ref[...]).astype(jnp.bfloat16)
    wide = a_ref.shape[1]
    a_ref[...] = normed[:, :wide]
    b_ref[...] = normed[:, wide:]


def norm_rows(own, got, gain, wide):
    rows, width = own.shape
    return pl.pallas_call(
        norm_kernel,
        out_shape=(
            jax.ShapeDtypeStruct((rows, width), jnp.float32),
            jax.ShapeDtypeStruct((rows, wide), jnp.bfloat16),
            jax.ShapeDtypeStruct((rows, width - wide), jnp.bfloat16),
        ),
        in_specs=[vmem()] * 3,
        out_specs=(vmem(),) * 3,
        name="norm_rows",
    )(own, got, gain)


def expert_kernel(*refs):
    (a0, a1, a2, a3, b0, b1, b2, b3, share_ref, wg0, wu0, wd0, wg1, wu1, wd1) = refs[:15]
    (oa0, oa1, oa2, oa3, ob0, ob1, ob2, ob3, x_ref, h0_ref, h1_ref) = refs[15:]
    a_in, b_in = (a0, a1, a2, a3), (b0, b1, b2, b3)
    a_out, b_out = (oa0, oa1, oa2, oa3), (ob0, ob1, ob2, ob3)
    rows, width = x_ref.shape
    wide = a0.shape[1]
    quad = rows // 4
    unit = quad // 4
    for i in range(4):
        x_ref[i * quad : (i + 1) * quad, :wide] = a_in[i][...]
        for j in range(4):
            at = i * quad + j * unit
            x_ref[at : at + unit, wide:] = b_in[j][i * unit : (i + 1) * unit, :]
    for wg, wu, h_ref in ((wg0, wu0, h0_ref), (wg1, wu1, h1_ref)):
        gate = jnp.dot(x_ref[...], wg[...], preferred_element_type=jnp.float32)
        up = jnp.dot(x_ref[...], wu[...], preferred_element_type=jnp.float32)
        h_ref[...] = (gate / (1.0 + jnp.exp(-gate)) * up).astype(jnp.bfloat16)
    share0, share1 = share_ref[:, 0:1], share_ref[:, 1:2]
    block = 128
    for at in range(0, width, block):
        cols = slice(at, at + block)
        down = share0 * jnp.dot(h0_ref[...], wd0[:, cols], preferred_element_type=jnp.float32)
        down = down + share1 * jnp.dot(
            h1_ref[...], wd1[:, cols], preferred_element_type=jnp.float32
        )
        if at < wide:
            for i in range(4):
                a_out[i][:, cols] = down[i * quad : (i + 1) * quad].astype(a_out[i].dtype)
        else:
            there = slice(at - wide, at - wide + block)
            for i in range(4):
                for j in range(4):
                    row = i * quad + j * unit
                    b_out[j][i * unit : (i + 1) * unit, there] = down[row : row + unit].astype(
                        b_out[j].dtype
                    )


def expert_rows(a_parts, b_parts, shares, weights, partner_weights):
    quad, wide = a_parts[0].shape
    narrow = b_parts[0].shape[1]
    width = wide + narrow
    rows = 4 * quad
    hidden = weights[0].shape[1]
    kinds = (jnp.float32, jnp.bfloat16, jnp.bfloat16, jnp.bfloat16)
    return pl.pallas_call(
        expert_kernel,
        out_shape=tuple(jax.ShapeDtypeStruct((quad, wide), kind) for kind in kinds)
        + tuple(jax.ShapeDtypeStruct((quad, narrow), kind) for kind in kinds),
        in_specs=[vmem()] * 15,
        out_specs=(vmem(),) * 8,
        scratch_shapes=[
            pltpu.VMEM((rows, width), jnp.bfloat16),
            pltpu.VMEM((rows, hidden), jnp.bfloat16),
            pltpu.VMEM((rows, hidden), jnp.bfloat16),
        ],
        compiler_params=pltpu.CompilerParams(vmem_limit_bytes=VMEM_BYTES),
        cost_estimate=pl.CostEstimate(
            flops=12 * rows * width * hidden, bytes_accessed=16 * rows * width, transcendentals=0
        ),
        name="expert_rows",
    )(*a_parts, *b_parts, shares, *weights, *partner_weights)


def sum_kernel(own_ref, g1, g2, g3, o0, o1, o2, o3):
    unit = o0.shape[0]
    for i, out in enumerate((o0, o1, o2, o3)):
        rows = slice(i * unit, (i + 1) * unit)
        total = own_ref[rows, :]
        for got in (g1, g2, g3):
            total = total + got[rows, :].astype(jnp.float32)
        out[...] = total.astype(out.dtype)


def sum_rows(own, got):
    quad, width = own.shape
    unit = quad // 4
    kinds = (jnp.float32, jnp.bfloat16, jnp.bfloat16, jnp.bfloat16)
    return pl.pallas_call(
        sum_kernel,
        out_shape=tuple(jax.ShapeDtypeStruct((unit, width), kind) for kind in kinds),
        in_specs=[vmem()] * 4,
        out_specs=(vmem(),) * 4,
        name="sum_rows",
    )(own, *got)


def final_kernel(state_ref, a0, a1, a2, a3, b0, b1, b2, b3, gain_ref, out_ref):
    wide = a0.shape[1]
    mixed_a = a0[...]
    for got in (a1, a2, a3):
        mixed_a = mixed_a + got[...].astype(jnp.float32)
    mixed_b = b0[...]
    for got in (b1, b2, b3):
        mixed_b = mixed_b + got[...].astype(jnp.float32)
    total = state_ref[...] + jnp.concatenate([mixed_a, mixed_b], axis=1)
    out_ref[...] = rms_scale(total, gain_ref[...]).astype(jnp.bfloat16)


def final_rows(state, a_parts, b_parts, gain):
    return pl.pallas_call(
        final_kernel,
        out_shape=jax.ShapeDtypeStruct(state.shape, jnp.bfloat16),
        in_specs=[vmem()] * 10,
        out_specs=vmem(),
        name="final_rows",
    )(state, *a_parts, *b_parts, gain)


def place(z, y, c, x):
    return ((z * 2 + y) * 2 + c) * 2 + x


def swap(value, dz, dy, dc, dx):
    pairs = [
        (place(z, y, c, x), place(z ^ dz, y ^ dy, c ^ dc, x ^ dx))
        for z in range(4)
        for y in range(2)
        for c in range(2)
        for x in range(2)
    ]
    return lax.ppermute(value, ALL, pairs)


PLANE = ((0, 0), (0, 1), (1, 0), (1, 1))


def swap_z(pieces):
    return tuple(swap(piece, d, 0, 0, 0) for d, piece in zip((1, 2, 3), pieces))


def swap_plane(pieces):
    return tuple(swap(piece, 0, dy, 0, dx) for (dy, dx), piece in zip(PLANE[1:], pieces))


def local_dense(
    queries, fresh_key_value, key_value_cache, request_page_index, cache_length_rows, residual,
    w_out, gain_in, route_ids, route_weights, expert_home, w_gate, w_up, w_down, gain_out,
):
    tp_index = lax.axis_index("tp")
    req_index = lax.axis_index("req")
    tokens, width = residual.shape
    half = tokens // 2
    wide = (width * 11 // 16) // 128 * 128
    groups = expert_home.shape[0]
    weights = (w_gate[0], w_up[0], w_down[0])
    partner_weights = tuple(swap(w, 0, 0, 1, 0) for w in weights)
    own_start = tp_index * half
    ids = lax.dynamic_slice_in_dim(route_ids, own_start, half, 0)
    routed = lax.dynamic_slice_in_dim(route_weights, own_start, half, 0)
    shares = routed / jnp.sum(routed, axis=1, keepdims=True)
    by_expert = jnp.sum(
        jnp.where(
            ids[:, :, None] == jnp.arange(groups, dtype=jnp.int32)[None, None, :],
            shares[:, :, None],
            0.0,
        ),
        axis=1,
    )
    homes = expert_home[:, None] == jnp.arange(groups, dtype=jnp.int32)[None, :]
    by_home = jnp.sum(jnp.where(homes[None], by_expert[:, :, None], 0.0), axis=1)
    every_share = lax.all_gather(by_home, ALL, axis=0, tiled=False)
    core = req_index % 2
    spots = [
        (((req_index // 4) ^ dz) * 2 + (((req_index // 2) % 2) ^ dy)) * 4 + core * 2 + (tp_index ^ dx)
        for dy, dx in PLANE
        for dz in range(4)
    ]
    near_share = every_share[jnp.stack(spots)].reshape(16 * half, groups)
    column = jnp.arange(groups, dtype=jnp.int32)[None, :]
    pair_share = jnp.stack(
        [
            jnp.sum(jnp.where(column == req_index, near_share, 0.0), axis=1),
            jnp.sum(jnp.where(column == (req_index ^ 1), near_share, 0.0), axis=1),
        ],
        axis=1,
    )

    own_state, sent = attention_terms(
        request_page_index, cache_length_rows, tp_index.reshape(1).astype(jnp.int32),
        queries, fresh_key_value, key_value_cache, residual, w_out,
    )
    got = swap(sent, 0, 0, 0, 1)
    state, rows_a, rows_b = norm_rows(own_state, got, gain_in[None, :], wide)
    column_a = jnp.concatenate((rows_a,) + swap_z((rows_a,) * 3), axis=0)
    column_b = jnp.concatenate((rows_b,) + swap_plane((rows_b,) * 3), axis=0)
    all_a = (column_a,) + swap_plane((column_a,) * 3)
    all_b = (column_b,) + swap_z((column_b,) * 3)
    parts = expert_rows(all_a, all_b, pair_share, weights, partner_weights)
    part_a, part_b = parts[:4], parts[4:]
    near_a = sum_rows(part_a[0], swap_plane(part_a[1:]))
    near_b = sum_rows(part_b[0], swap_z(part_b[1:]))
    last_a = (near_a[0],) + swap_z(near_a[1:])
    last_b = (near_b[0],) + swap_plane(near_b[1:])
    return final_rows(state, last_a, last_b, gain_out[None, :])


def solution(mesh):
    dense = mesh.shape["req"] == 16 and mesh.shape["tp"] == 2
    return jax.shard_map(
        local_dense if dense else local_sparse,
        mesh=mesh,
        in_specs=(
            P("req", "tp"),
            P("req", "tp"),
            P("req", None, "tp"),
            P("req", None),
            P("req"),
            P("req", None),
            P("tp", None),
            P(),
            P("req", None),
            P("req", None),
            P(),
            P("req", None, "tp"),
            P("req", None, "tp"),
            P("req", "tp", None),
            P(),
        ),
        out_specs=P(("req", "tp"), None),
        check_vma=False,
    )
```

```python
import functools

import jax
import jax.numpy as jnp
from jax import lax
from jax.experimental import pallas as pl
from jax.experimental.pallas import tpu as pltpu
from jax.sharding import PartitionSpec as P

HEAD_WIDTH = 128
TOPK = 8
PRE_DEV = 56


EPSILON = 1e-06


def rms_scale(value_rows, gain_row):
    mean_square = jnp.mean(value_rows * value_rows, axis=-1, keepdims=True)
    return value_rows * lax.rsqrt(mean_square + EPSILON) * gain_row


def softmax_rounded(scores):
    row_peak = jnp.max(scores, axis=-1, keepdims=True)
    weights = jnp.exp(scores - row_peak)
    return (weights / jnp.sum(weights, axis=-1, keepdims=True)).astype(jnp.bfloat16)


def group_attention(queries, fresh_key_value, page_pool, page_rows, lengths):
    tokens_here = queries.shape[0]
    kv_heads = fresh_key_value.shape[1] // (2 * HEAD_WIDTH)
    group_size = queries.shape[1] // (HEAD_WIDTH * kv_heads)
    score_scale = HEAD_WIDTH ** (-0.5)
    split_query = queries.reshape(tokens_here, kv_heads, group_size, HEAD_WIDTH)
    fresh_kv = fresh_key_value.reshape(tokens_here, kv_heads, 2, HEAD_WIDTH)
    gathered_pages = page_pool[page_rows]
    cached = gathered_pages.reshape(page_rows.shape[0], -1, kv_heads, 2, HEAD_WIDTH)
    places = jnp.arange(cached.shape[1], dtype=jnp.int32)
    prefill_query = split_query[:PRE_DEV]
    prefill_fresh = fresh_kv[:PRE_DEV]
    cache_scores = (
        jnp.einsum(
            "ikgd,ckd->kgic", prefill_query, cached[0, :, :, 0], preferred_element_type=jnp.float32
        )
        * score_scale
    )
    cache_scores = jnp.where(places < lengths[0], cache_scores, -jnp.inf)
    block_scores = (
        jnp.einsum(
            "ikgd,jkd->kgij",
            prefill_query,
            prefill_fresh[:, :, 0],
            preferred_element_type=jnp.float32,
        )
        * score_scale
    )
    causal = jnp.arange(PRE_DEV)[:, None] >= jnp.arange(PRE_DEV)[None, :]
    block_scores = jnp.where(causal, block_scores, -jnp.inf)
    prefill_probs = softmax_rounded(jnp.concatenate([cache_scores, block_scores], axis=3))
    prefill_values = jnp.concatenate([cached[0, :, :, 1], prefill_fresh[:, :, 1]], axis=0)
    prefill_out = jnp.einsum(
        "kgic,ckd->ikgd", prefill_probs, prefill_values, preferred_element_type=jnp.float32
    )
    decode_query = split_query[PRE_DEV:]
    decode_fresh = fresh_kv[PRE_DEV:]
    decode_scores = (
        jnp.einsum(
            "rkgd,rckd->rkgc", decode_query, cached[1:, :, :, 0], preferred_element_type=jnp.float32
        )
        * score_scale
    )
    decode_scores = jnp.where(
        places[None, None, None, :] < lengths[1:, None, None, None], decode_scores, -jnp.inf
    )
    own_scores = (
        jnp.einsum(
            "rkgd,rkd->rkg", decode_query, decode_fresh[:, :, 0], preferred_element_type=jnp.float32
        )[..., None]
        * score_scale
    )
    decode_probs = softmax_rounded(jnp.concatenate([decode_scores, own_scores], axis=3))
    decode_values = jnp.concatenate([cached[1:, :, :, 1], decode_fresh[:, None, :, 1]], axis=1)
    decode_out = jnp.einsum(
        "rkgc,rckd->rkgd", decode_probs, decode_values, preferred_element_type=jnp.float32
    )
    joined = jnp.concatenate([prefill_out, decode_out], axis=0)
    return joined.reshape(tokens_here, -1).astype(jnp.bfloat16)


def slot_positions(block_owner, experts, capacity):
    flat_owner = block_owner.reshape(-1)
    onehot = (flat_owner[:, None] == jnp.arange(experts, dtype=jnp.int32)[None, :]).astype(
        jnp.int32
    )
    earlier = jnp.cumsum(onehot, axis=0) - onehot
    slot_index = jnp.sum(earlier * onehot, axis=1)
    return (flat_owner * capacity + slot_index).reshape(block_owner.shape)


def place_matrix(positions, slots_total):
    matches = positions[None, :, :] == jnp.arange(slots_total, dtype=jnp.int32)[:, None, None]
    return jnp.any(matches, axis=2).astype(jnp.bfloat16)


def local_sparse(
    queries,
    fresh_key_value,
    key_value_cache,
    request_page_index,
    cache_length_rows,
    residual,
    w_out,
    gain_in,
    route_ids,
    route_weights,
    expert_home,
    w_gate,
    w_up,
    w_down,
    gain_out,
):
    tp_size = lax.axis_size("tp")
    req_size = lax.axis_size("req")
    tp_index = lax.axis_index("tp")
    model_width = residual.shape[1]
    tokens_here = residual.shape[0]
    quarter = tokens_here // tp_size
    experts = expert_home.shape[0]
    capacity = min(quarter, max(2, 2 * quarter * TOPK // experts))
    context = group_attention(
        queries, fresh_key_value, key_value_cache, request_page_index, cache_length_rows
    )
    head_terms = jnp.dot(context, w_out, preferred_element_type=jnp.float32)
    state = residual.astype(jnp.float32) + lax.psum(head_terms, "tp")
    owners = jnp.sum(
        jnp.where(
            route_ids[:, :, None] == jnp.arange(experts, dtype=jnp.int32)[None, None, :],
            expert_home[None, None, :],
            0,
        ),
        axis=2,
    )
    shares = route_weights / jnp.sum(route_weights, axis=1, keepdims=True)
    own_start = tp_index * quarter
    own_state = lax.dynamic_slice_in_dim(state, own_start, quarter, 0)
    own_shares = lax.dynamic_slice_in_dim(shares, own_start, quarter, 0)
    normed_all = rms_scale(state, gain_in).astype(jnp.bfloat16)
    positions_all = jax.vmap(lambda block_owner: slot_positions(block_owner, experts, capacity))(
        owners.reshape(tp_size, quarter, TOPK)
    )
    placing = jax.vmap(lambda positions: place_matrix(positions, experts * capacity))(positions_all)
    outgoing = jnp.einsum(
        "qmi,qid->qmd",
        placing,
        normed_all.reshape(tp_size, quarter, model_width),
        preferred_element_type=jnp.float32,
    )
    outgoing = outgoing.astype(jnp.bfloat16).reshape(tp_size, experts, capacity, model_width)
    incoming = lax.all_to_all(outgoing, "req", split_axis=1, concat_axis=1, tiled=True)
    own_positions = lax.dynamic_index_in_dim(positions_all, tp_index, 0, keepdims=False)
    expert_rows = incoming.reshape(-1, model_width)
    gate_proj = jnp.dot(expert_rows, w_gate[0], preferred_element_type=jnp.float32)
    up_proj = jnp.dot(expert_rows, w_up[0], preferred_element_type=jnp.float32)
    inner_units = (jax.nn.silu(gate_proj) * up_proj).astype(jnp.bfloat16)
    summed = lax.psum_scatter(
        jnp.dot(inner_units, w_down[0], preferred_element_type=jnp.float32).astype(jnp.bfloat16),
        "tp",
        scatter_dimension=0,
        tiled=True,
    )
    results = summed.reshape(req_size, capacity, model_width)
    returned = lax.all_to_all(results, "req", split_axis=0, concat_axis=0, tiled=True).reshape(
        -1, model_width
    )
    picked = returned[own_positions]
    mixture = jnp.sum(own_shares[:, :, None] * picked.astype(jnp.float32), axis=1)
    return rms_scale(own_state + mixture, gain_out).astype(jnp.bfloat16)


ALL = ("req", "tp")
MASKED = -1e30
LANES = 128
MIB = 1024 * 1024
SMALL = pltpu.CompilerParams(vmem_limit_bytes=8 * MIB)


def vmem():
    return pl.BlockSpec(memory_space=pltpu.VMEM)


def smem():
    return pl.BlockSpec(memory_space=pltpu.SMEM)


def hbm():
    return pl.BlockSpec(memory_space=pltpu.HBM)


def stay(value):
    return pltpu.with_memory_space_constraint(value, pltpu.HBM)


def barrier(*values):
    return lax.optimization_barrier(values)


def multiplicity(page_rows, length, pool_pages, page_tokens):
    rows = page_rows[0].shape[0]
    lane = lax.broadcasted_iota(jnp.int32, (rows, page_tokens), 1)
    parts = []
    for page in range(pool_pages):
        count = jnp.zeros((rows, page_tokens), jnp.float32)
        for slot, named in enumerate(page_rows):
            hit = (named == page) & (lane + slot * page_tokens < length)
            count = count + jnp.where(hit, 1.0, 0.0)
        parts.append(count)
    return jnp.concatenate(parts, axis=1)


def pack_shares(ids, routed, home_ref):
    groups = home_ref.shape[0]
    rows = ids.shape[0]
    lane = lax.broadcasted_iota(jnp.int32, (rows, LANES), 1)
    shares = routed / jnp.sum(routed, axis=1, keepdims=True)
    by_expert = jnp.zeros((rows, LANES), jnp.float32)
    for k in range(ids.shape[1]):
        by_expert = by_expert + jnp.where(lane == ids[:, k : k + 1], shares[:, k : k + 1], 0.0)
    by_home = jnp.zeros((rows, LANES), jnp.float32)
    for e in range(groups):
        mine = (lane == home_ref[e]) | (lane == home_ref[e] + groups)
        by_home = by_home + jnp.where(mine, by_expert[:, e : e + 1], 0.0)
    rounded = by_home.astype(jnp.bfloat16).astype(jnp.float32)
    return jnp.where(lane < groups, rounded, by_home - rounded).astype(jnp.bfloat16)


def attention_kernel(
    pages_ref, lengths_ref, tp_ref, home_ref, q_hbm, fresh_hbm, cache_hbm, residual_hbm, ids_hbm,
    routed_hbm, w_hbm, own_ref, send_ref, pack_ref,
    q_ref, fresh_ref, cache_ref, residual_ref, ids_ref, routed_ref, w_ref, context_ref, terms_ref,
    sems,
):
    fetches = [
        pltpu.make_async_copy(source, target, sems.at[i])
        for i, (source, target) in enumerate(
            (
                (q_hbm, q_ref),
                (cache_hbm, cache_ref),
                (fresh_hbm, fresh_ref),
                (ids_hbm, ids_ref),
                (routed_hbm, routed_ref),
                (residual_hbm, residual_ref),
                (w_hbm, w_ref),
            )
        )
    ]
    for fetch in fetches:
        fetch.start()
    tokens = q_ref.shape[0]
    pool_pages, page_tokens, _ = cache_ref.shape
    requests, slots = pages_ref.shape
    kv_heads = fresh_ref.shape[1] // (2 * HEAD_WIDTH)
    group = q_ref.shape[1] // (HEAD_WIDTH * kv_heads)
    decodes = requests - 1
    row = lax.broadcasted_iota(jnp.int32, (decodes, page_tokens), 0)

    def by_row(read):
        value = jnp.zeros((decodes, page_tokens), jnp.int32)
        for j in range(decodes):
            value = jnp.where(row == j, read(j + 1), value)
        return value

    full = lambda scalar: jnp.full((decodes, page_tokens), scalar, jnp.int32)
    first = multiplicity(
        [full(pages_ref[0, s]) for s in range(slots)], full(lengths_ref[0]), pool_pages, page_tokens
    )
    later = multiplicity(
        [by_row(lambda j, s=s: pages_ref[j, s]) for s in range(slots)],
        by_row(lambda j: lengths_ref[j]),
        pool_pages,
        page_tokens,
    )
    count = jnp.concatenate([first] * (PRE_DEV // decodes) + [later], axis=0)
    query_place = lax.broadcasted_iota(jnp.int32, (tokens, tokens), 0)
    key_place = lax.broadcasted_iota(jnp.int32, (tokens, tokens), 1)
    seen = (key_place == query_place) | ((key_place <= query_place) & (query_place < PRE_DEV))
    visible = jnp.concatenate([count] * group, axis=0)
    seen = jnp.concatenate([jnp.where(seen, 1.0, 0.0)] * group, axis=0)
    scale = HEAD_WIDTH**-0.5
    for fetch in fetches[:3]:
        fetch.wait()
    contract_last = (((1,), (1,)), ((), ()))
    for k in range(kv_heads):
        key_at, value_at = 2 * k * HEAD_WIDTH, (2 * k + 1) * HEAD_WIDTH
        query = jnp.concatenate(
            [
                q_ref[:, (k * group + g) * HEAD_WIDTH : (k * group + g + 1) * HEAD_WIDTH]
                for g in range(group)
            ],
            axis=0,
        )
        keys = cache_ref[:, :, key_at : key_at + HEAD_WIDTH].reshape(-1, HEAD_WIDTH)
        values = cache_ref[:, :, value_at : value_at + HEAD_WIDTH].reshape(-1, HEAD_WIDTH)
        old = lax.dot_general(query, keys, contract_last, preferred_element_type=jnp.float32)
        new = lax.dot_general(
            query,
            fresh_ref[:, key_at : key_at + HEAD_WIDTH],
            contract_last,
            preferred_element_type=jnp.float32,
        )
        old = jnp.where(visible > 0, old * scale, MASKED)
        new = jnp.where(seen > 0, new * scale, MASKED)
        peak = jnp.maximum(
            jnp.max(old, axis=1, keepdims=True), jnp.max(new, axis=1, keepdims=True)
        )
        old = jnp.exp(old - peak) * visible
        new = jnp.exp(new - peak) * seen
        inverse = 1.0 / (
            jnp.sum(old, axis=1, keepdims=True) + jnp.sum(new, axis=1, keepdims=True)
        )
        mixed = jnp.dot(
            (old * inverse).astype(jnp.bfloat16), values, preferred_element_type=jnp.float32
        ) + jnp.dot(
            (new * inverse).astype(jnp.bfloat16),
            fresh_ref[:, value_at : value_at + HEAD_WIDTH],
            preferred_element_type=jnp.float32,
        )
        mixed = mixed.astype(jnp.bfloat16)
        for g in range(group):
            h = k * group + g
            context_ref[:, h * HEAD_WIDTH : (h + 1) * HEAD_WIDTH] = mixed[
                g * tokens : (g + 1) * tokens
            ]
    half = tokens // 2
    width = terms_ref.shape[1]
    block = 512
    own_at = pl.multiple_of(tp_ref[0] * half, half)
    other_at = pl.multiple_of((1 - tp_ref[0]) * half, half)
    for fetch in fetches[3:5]:
        fetch.wait()
    pack_ref[...] = pack_shares(
        ids_ref[pl.ds(own_at, half), :], routed_ref[pl.ds(own_at, half), :], home_ref
    )
    for fetch in fetches[5:]:
        fetch.wait()
    for at in range(0, width, block):
        cols = slice(at, at + block)
        terms_ref[:, cols] = jnp.dot(
            context_ref[...], w_ref[:, cols], preferred_element_type=jnp.float32
        )
    own_ref[...] = terms_ref[pl.ds(own_at, half), :] + residual_ref[
        pl.ds(own_at, half), :
    ].astype(jnp.float32)
    send_ref[...] = terms_ref[pl.ds(other_at, half), :].astype(jnp.bfloat16)


def attention_terms(
    pages, lengths, tp_index, home, queries, fresh, cache, residual, ids, routed, w_out
):
    tokens, width = residual.shape
    half = tokens // 2
    moved = (queries, fresh, cache, residual, ids, routed, w_out)
    return pl.pallas_call(
        attention_kernel,
        out_shape=(
            jax.ShapeDtypeStruct((half, width), jnp.float32),
            jax.ShapeDtypeStruct((half, width), jnp.bfloat16),
            jax.ShapeDtypeStruct((half, LANES), jnp.bfloat16),
        ),
        in_specs=[smem()] * 4 + [hbm()] * 7,
        out_specs=(vmem(),) * 3,
        scratch_shapes=[pltpu.VMEM(v.shape, v.dtype) for v in moved]
        + [
            pltpu.VMEM(queries.shape, jnp.bfloat16),
            pltpu.VMEM((tokens, width), jnp.float32),
            pltpu.SemaphoreType.DMA((7,)),
        ],
        compiler_params=pltpu.CompilerParams(vmem_limit_bytes=40 * MIB),
        name="attention_terms",
    )(stay(pages), stay(lengths), tp_index, stay(home), *[stay(v) for v in moved])


def norm_kernel(own_ref, got_ref, pack_ref, gain_ref, state_ref, a_ref, b_ref):
    state = own_ref[...] + got_ref[...].astype(jnp.float32)
    state_ref[...] = state
    normed = rms_scale(state, gain_ref[...]).astype(jnp.bfloat16)
    wide = a_ref.shape[1] - LANES
    a_ref[:, :wide] = normed[:, :wide]
    a_ref[:, wide:] = pack_ref[...]
    b_ref[...] = normed[:, wide:]


def norm_rows(own, got, pack, gain, wide):
    rows, width = own.shape
    return pl.pallas_call(
        norm_kernel,
        out_shape=(
            jax.ShapeDtypeStruct((rows, width), jnp.float32),
            jax.ShapeDtypeStruct((rows, wide + LANES), jnp.bfloat16),
            jax.ShapeDtypeStruct((rows, width - wide), jnp.bfloat16),
        ),
        in_specs=[vmem()] * 4,
        out_specs=(vmem(),) * 3,
        compiler_params=SMALL,
        name="norm_rows",
    )(own, got, pack, gain)


def expert_kernel(
    group_ref, a0, a1, a2, a3, b0, b1, b2, b3, wg0, wu0, wd0, wg1, wu1, wd1,
    oa0, oa1, oa2, oa3, ob0, ob1, ob2, ob3,
    x_ref, w0_ref, w1_ref, down_ref, h_ref, sems,
):
    a_in, b_in = (a0, a1, a2, a3), (b0, b1, b2, b3)
    a_out, b_out = (oa0, oa1, oa2, oa3), (ob0, ob1, ob2, ob3)
    rows, width = x_ref.shape
    hidden = wg0.shape[1]
    wide = oa0.shape[1]
    quad = rows // 4
    unit = quad // 4
    fetches = [
        pltpu.make_async_copy(source, target, sems.at[i])
        for i, (source, target) in enumerate(
            (
                (wg0, w0_ref.at[:, :hidden]),
                (wu0, w0_ref.at[:, hidden:]),
                (wg1, w1_ref.at[:, :hidden]),
                (wu1, w1_ref.at[:, hidden:]),
                (wd0, down_ref.at[:hidden, :]),
                (wd1, down_ref.at[hidden:, :]),
            )
        )
    ]
    for fetch in fetches:
        fetch.start()
    lane = lax.broadcasted_iota(jnp.int32, (rows, LANES), 1)
    packed = jnp.concatenate([a[:, wide:] for a in a_in], axis=0).astype(jnp.float32)
    groups = group_ref[2]
    for i in range(4):
        x_ref[i * quad : (i + 1) * quad, :wide] = a_in[i][:, :wide]
        for j in range(4):
            at = i * quad + j * unit
            x_ref[at : at + unit, wide:] = b_in[j][i * unit : (i + 1) * unit, :]
    for e, w_ref in enumerate((w0_ref, w1_ref)):
        group = group_ref[e]
        share = jnp.sum(
            jnp.where((lane == group) | (lane == group + groups), packed, 0.0),
            axis=1,
            keepdims=True,
        )
        fetches[2 * e].wait()
        fetches[2 * e + 1].wait()
        both = jnp.dot(x_ref[...], w_ref[...], preferred_element_type=jnp.float32)
        gate, up = both[:, :hidden], both[:, hidden:]
        h_ref[:, e * hidden : (e + 1) * hidden] = (
            share * up * (gate / (1.0 + jnp.exp(-gate)))
        ).astype(jnp.bfloat16)
    fetches[4].wait()
    fetches[5].wait()
    block = 256
    for at in range(0, width, block):
        cols = slice(at, at + block)
        down = jnp.dot(h_ref[...], down_ref[:, cols], preferred_element_type=jnp.float32)
        if at < wide:
            for i in range(4):
                a_out[i][:, cols] = down[i * quad : (i + 1) * quad].astype(a_out[i].dtype)
        else:
            there = slice(at - wide, at - wide + block)
            for i in range(4):
                for j in range(4):
                    row = i * quad + j * unit
                    b_out[j][i * unit : (i + 1) * unit, there] = down[row : row + unit].astype(
                        b_out[j].dtype
                    )


def expert_rows(group, a_parts, b_parts, weights, partner_weights):
    quad, narrow = b_parts[0].shape
    wide = a_parts[0].shape[1] - LANES
    width = wide + narrow
    rows = 4 * quad
    hidden = weights[0].shape[1]
    kinds = (jnp.float32, jnp.bfloat16, jnp.bfloat16, jnp.bfloat16)
    return pl.pallas_call(
        expert_kernel,
        out_shape=tuple(jax.ShapeDtypeStruct((quad, wide), kind) for kind in kinds)
        + tuple(jax.ShapeDtypeStruct((quad, narrow), kind) for kind in kinds),
        in_specs=[smem()] + [vmem()] * 8 + [hbm()] * 6,
        out_specs=(vmem(),) * 8,
        scratch_shapes=[
            pltpu.VMEM((rows, width), jnp.bfloat16),
            pltpu.VMEM((width, 2 * hidden), jnp.bfloat16),
            pltpu.VMEM((width, 2 * hidden), jnp.bfloat16),
            pltpu.VMEM((2 * hidden, width), jnp.bfloat16),
            pltpu.VMEM((rows, 2 * hidden), jnp.bfloat16),
            pltpu.SemaphoreType.DMA((6,)),
        ],
        compiler_params=pltpu.CompilerParams(vmem_limit_bytes=40 * MIB),
        cost_estimate=pl.CostEstimate(
            flops=12 * rows * width * hidden, bytes_accessed=16 * rows * width, transcendentals=0
        ),
        name="expert_rows",
    )(group, *a_parts, *b_parts, *[stay(w) for w in weights + partner_weights])


def sum_kernel(own_ref, g1, g2, g3, o0, o1, o2, o3):
    unit = o0.shape[0]
    for i, out in enumerate((o0, o1, o2, o3)):
        rows = slice(i * unit, (i + 1) * unit)
        total = own_ref[rows, :]
        for got in (g1, g2, g3):
            total = total + got[rows, :].astype(jnp.float32)
        out[...] = total.astype(out.dtype)


def sum_rows(own, got):
    quad, width = own.shape
    unit = quad // 4
    kinds = (jnp.float32, jnp.bfloat16, jnp.bfloat16, jnp.bfloat16)
    return pl.pallas_call(
        sum_kernel,
        out_shape=tuple(jax.ShapeDtypeStruct((unit, width), kind) for kind in kinds),
        in_specs=[vmem()] * 4,
        out_specs=(vmem(),) * 4,
        compiler_params=SMALL,
        name="sum_rows",
    )(own, *got)


def final_kernel(state_ref, a0, a1, a2, a3, b0, b1, b2, b3, gain_ref, out_ref):
    wide = a0.shape[1]
    mixed_a = a0[...]
    for got in (a1, a2, a3):
        mixed_a = mixed_a + got[...].astype(jnp.float32)
    mixed_b = b0[...]
    for got in (b1, b2, b3):
        mixed_b = mixed_b + got[...].astype(jnp.float32)
    total = state_ref[...] + jnp.concatenate([mixed_a, mixed_b], axis=1)
    out_ref[...] = rms_scale(total, gain_ref[...]).astype(jnp.bfloat16)


def final_rows(state, a_parts, b_parts, gain):
    return pl.pallas_call(
        final_kernel,
        out_shape=jax.ShapeDtypeStruct(state.shape, jnp.bfloat16),
        in_specs=[vmem()] * 10,
        out_specs=vmem(),
        compiler_params=SMALL,
        name="final_rows",
    )(state, *a_parts, *b_parts, gain)


def place(z, y, c, x):
    return ((z * 2 + y) * 2 + c) * 2 + x


def swap(value, dz, dy, dc, dx):
    pairs = [
        (place(z, y, c, x), place(z ^ dz, y ^ dy, c ^ dc, x ^ dx))
        for z in range(4)
        for y in range(2)
        for c in range(2)
        for x in range(2)
    ]
    return lax.ppermute(value, ALL, pairs)


PLANE = ((0, 0), (0, 1), (1, 0), (1, 1))


def swap_z(pieces):
    return tuple(swap(piece, d, 0, 0, 0) for d, piece in zip((1, 2, 3), pieces))


def swap_plane(pieces):
    return tuple(swap(piece, 0, dy, 0, dx) for (dy, dx), piece in zip(PLANE[1:], pieces))


def local_dense(
    queries, fresh_key_value, key_value_cache, request_page_index, cache_length_rows, residual,
    w_out, gain_in, route_ids, route_weights, expert_home, w_gate, w_up, w_down, gain_out,
):
    tp_index = lax.axis_index("tp")
    req_index = lax.axis_index("req")
    tokens, width = residual.shape
    half = tokens // 2
    wide = width * 5 // 8
    groups = expert_home.shape[0]
    weights = (w_gate[0], w_up[0], w_down[0])
    partner_weights = tuple(swap(w, 0, 0, 1, 0) for w in weights)
    own_state, sent, pack = attention_terms(
        request_page_index, cache_length_rows, tp_index.reshape(1).astype(jnp.int32), expert_home,
        queries, fresh_key_value, key_value_cache, residual, route_ids, route_weights, w_out,
    )
    got = swap(sent, 0, 0, 0, 1)
    state, rows_a, rows_b = norm_rows(own_state, got, pack, gain_in[None, :], wide)
    more_a, more_b, partner_weights = barrier(
        swap_z((rows_a,) * 3), swap_plane((rows_b,) * 3), partner_weights
    )
    column_a, column_b = barrier(
        jnp.concatenate((rows_a,) + more_a, axis=0), jnp.concatenate((rows_b,) + more_b, axis=0)
    )
    more_a, more_b = barrier(swap_plane((column_a,) * 3), swap_z((column_b,) * 3))
    group = jnp.stack([req_index, req_index ^ 1, groups]).astype(jnp.int32)
    parts = expert_rows(
        group, (column_a,) + more_a, (column_b,) + more_b, weights, partner_weights
    )
    part_a, part_b = parts[:4], parts[4:]
    more_a, more_b = barrier(swap_plane(part_a[1:]), swap_z(part_b[1:]))
    near_a, near_b = barrier(sum_rows(part_a[0], more_a), sum_rows(part_b[0], more_b))
    more_a, more_b = barrier(swap_z(near_a[1:]), swap_plane(near_b[1:]))
    return final_rows(state, (near_a[0],) + more_a, (near_b[0],) + more_b, gain_out[None, :])


def solution(mesh):
    dense = mesh.shape["req"] == 16 and mesh.shape["tp"] == 2
    return jax.shard_map(
        local_dense if dense else local_sparse,
        mesh=mesh,
        in_specs=(
            P("req", "tp"),
            P("req", "tp"),
            P("req", None, "tp"),
            P("req", None),
            P("req"),
            P("req", None),
            P("tp", None),
            P(),
            P("req", None),
            P("req", None),
            P(),
            P("req", None, "tp"),
            P("req", None, "tp"),
            P("req", "tp", None),
            P(),
        ),
        out_specs=P(("req", "tp"), None),
        check_vma=False,
    )
```

```python
import functools

import jax
import jax.numpy as jnp
from jax import lax
from jax.experimental import pallas as pl
from jax.experimental.pallas import tpu as pltpu
from jax.sharding import PartitionSpec as P

HEAD_WIDTH = 128
TOPK = 8
PRE_DEV = 56


EPSILON = 1e-06


def rms_scale(value_rows, gain_row):
    mean_square = jnp.mean(value_rows * value_rows, axis=-1, keepdims=True)
    return value_rows * lax.rsqrt(mean_square + EPSILON) * gain_row


def softmax_rounded(scores):
    row_peak = jnp.max(scores, axis=-1, keepdims=True)
    weights = jnp.exp(scores - row_peak)
    return (weights / jnp.sum(weights, axis=-1, keepdims=True)).astype(jnp.bfloat16)


def group_attention(queries, fresh_key_value, page_pool, page_rows, lengths):
    tokens_here = queries.shape[0]
    kv_heads = fresh_key_value.shape[1] // (2 * HEAD_WIDTH)
    group_size = queries.shape[1] // (HEAD_WIDTH * kv_heads)
    score_scale = HEAD_WIDTH ** (-0.5)
    split_query = queries.reshape(tokens_here, kv_heads, group_size, HEAD_WIDTH)
    fresh_kv = fresh_key_value.reshape(tokens_here, kv_heads, 2, HEAD_WIDTH)
    gathered_pages = page_pool[page_rows]
    cached = gathered_pages.reshape(page_rows.shape[0], -1, kv_heads, 2, HEAD_WIDTH)
    places = jnp.arange(cached.shape[1], dtype=jnp.int32)
    prefill_query = split_query[:PRE_DEV]
    prefill_fresh = fresh_kv[:PRE_DEV]
    cache_scores = (
        jnp.einsum(
            "ikgd,ckd->kgic", prefill_query, cached[0, :, :, 0], preferred_element_type=jnp.float32
        )
        * score_scale
    )
    cache_scores = jnp.where(places < lengths[0], cache_scores, -jnp.inf)
    block_scores = (
        jnp.einsum(
            "ikgd,jkd->kgij",
            prefill_query,
            prefill_fresh[:, :, 0],
            preferred_element_type=jnp.float32,
        )
        * score_scale
    )
    causal = jnp.arange(PRE_DEV)[:, None] >= jnp.arange(PRE_DEV)[None, :]
    block_scores = jnp.where(causal, block_scores, -jnp.inf)
    prefill_probs = softmax_rounded(jnp.concatenate([cache_scores, block_scores], axis=3))
    prefill_values = jnp.concatenate([cached[0, :, :, 1], prefill_fresh[:, :, 1]], axis=0)
    prefill_out = jnp.einsum(
        "kgic,ckd->ikgd", prefill_probs, prefill_values, preferred_element_type=jnp.float32
    )
    decode_query = split_query[PRE_DEV:]
    decode_fresh = fresh_kv[PRE_DEV:]
    decode_scores = (
        jnp.einsum(
            "rkgd,rckd->rkgc", decode_query, cached[1:, :, :, 0], preferred_element_type=jnp.float32
        )
        * score_scale
    )
    decode_scores = jnp.where(
        places[None, None, None, :] < lengths[1:, None, None, None], decode_scores, -jnp.inf
    )
    own_scores = (
        jnp.einsum(
            "rkgd,rkd->rkg", decode_query, decode_fresh[:, :, 0], preferred_element_type=jnp.float32
        )[..., None]
        * score_scale
    )
    decode_probs = softmax_rounded(jnp.concatenate([decode_scores, own_scores], axis=3))
    decode_values = jnp.concatenate([cached[1:, :, :, 1], decode_fresh[:, None, :, 1]], axis=1)
    decode_out = jnp.einsum(
        "rkgc,rckd->rkgd", decode_probs, decode_values, preferred_element_type=jnp.float32
    )
    joined = jnp.concatenate([prefill_out, decode_out], axis=0)
    return joined.reshape(tokens_here, -1).astype(jnp.bfloat16)


def slot_positions(block_owner, experts, capacity):
    flat_owner = block_owner.reshape(-1)
    onehot = (flat_owner[:, None] == jnp.arange(experts, dtype=jnp.int32)[None, :]).astype(
        jnp.int32
    )
    earlier = jnp.cumsum(onehot, axis=0) - onehot
    slot_index = jnp.sum(earlier * onehot, axis=1)
    return (flat_owner * capacity + slot_index).reshape(block_owner.shape)


def place_matrix(positions, slots_total):
    matches = positions[None, :, :] == jnp.arange(slots_total, dtype=jnp.int32)[:, None, None]
    return jnp.any(matches, axis=2).astype(jnp.bfloat16)


def local_sparse(
    queries,
    fresh_key_value,
    key_value_cache,
    request_page_index,
    cache_length_rows,
    residual,
    w_out,
    gain_in,
    route_ids,
    route_weights,
    expert_home,
    w_gate,
    w_up,
    w_down,
    gain_out,
):
    tp_size = lax.axis_size("tp")
    req_size = lax.axis_size("req")
    tp_index = lax.axis_index("tp")
    model_width = residual.shape[1]
    tokens_here = residual.shape[0]
    quarter = tokens_here // tp_size
    experts = expert_home.shape[0]
    capacity = min(quarter, max(2, 2 * quarter * TOPK // experts))
    context = group_attention(
        queries, fresh_key_value, key_value_cache, request_page_index, cache_length_rows
    )
    head_terms = jnp.dot(context, w_out, preferred_element_type=jnp.float32)
    state = residual.astype(jnp.float32) + lax.psum(head_terms, "tp")
    owners = jnp.sum(
        jnp.where(
            route_ids[:, :, None] == jnp.arange(experts, dtype=jnp.int32)[None, None, :],
            expert_home[None, None, :],
            0,
        ),
        axis=2,
    )
    shares = route_weights / jnp.sum(route_weights, axis=1, keepdims=True)
    own_start = tp_index * quarter
    own_state = lax.dynamic_slice_in_dim(state, own_start, quarter, 0)
    own_shares = lax.dynamic_slice_in_dim(shares, own_start, quarter, 0)
    normed_all = rms_scale(state, gain_in).astype(jnp.bfloat16)
    positions_all = jax.vmap(lambda block_owner: slot_positions(block_owner, experts, capacity))(
        owners.reshape(tp_size, quarter, TOPK)
    )
    placing = jax.vmap(lambda positions: place_matrix(positions, experts * capacity))(positions_all)
    outgoing = jnp.einsum(
        "qmi,qid->qmd",
        placing,
        normed_all.reshape(tp_size, quarter, model_width),
        preferred_element_type=jnp.float32,
    )
    outgoing = outgoing.astype(jnp.bfloat16).reshape(tp_size, experts, capacity, model_width)
    incoming = lax.all_to_all(outgoing, "req", split_axis=1, concat_axis=1, tiled=True)
    own_positions = lax.dynamic_index_in_dim(positions_all, tp_index, 0, keepdims=False)
    expert_rows = incoming.reshape(-1, model_width)
    gate_proj = jnp.dot(expert_rows, w_gate[0], preferred_element_type=jnp.float32)
    up_proj = jnp.dot(expert_rows, w_up[0], preferred_element_type=jnp.float32)
    inner_units = (jax.nn.silu(gate_proj) * up_proj).astype(jnp.bfloat16)
    summed = lax.psum_scatter(
        jnp.dot(inner_units, w_down[0], preferred_element_type=jnp.float32).astype(jnp.bfloat16),
        "tp",
        scatter_dimension=0,
        tiled=True,
    )
    results = summed.reshape(req_size, capacity, model_width)
    returned = lax.all_to_all(results, "req", split_axis=0, concat_axis=0, tiled=True).reshape(
        -1, model_width
    )
    picked = returned[own_positions]
    mixture = jnp.sum(own_shares[:, :, None] * picked.astype(jnp.float32), axis=1)
    return rms_scale(own_state + mixture, gain_out).astype(jnp.bfloat16)


ALL = ("req", "tp")
MASKED = -1e30
LANES = 128
MIB = 1024 * 1024
SMALL = pltpu.CompilerParams(vmem_limit_bytes=8 * MIB)


def vmem():
    return pl.BlockSpec(memory_space=pltpu.VMEM)


def smem():
    return pl.BlockSpec(memory_space=pltpu.SMEM)


def hbm():
    return pl.BlockSpec(memory_space=pltpu.HBM)


def stay(value):
    return pltpu.with_memory_space_constraint(value, pltpu.HBM)


def barrier(*values):
    return lax.optimization_barrier(values)


def multiplicity(page_rows, length, pool_pages, page_tokens):
    rows = page_rows[0].shape[0]
    lane = lax.broadcasted_iota(jnp.int32, (rows, page_tokens), 1)
    parts = []
    for page in range(pool_pages):
        count = jnp.zeros((rows, page_tokens), jnp.float32)
        for slot, named in enumerate(page_rows):
            hit = (named == page) & (lane + slot * page_tokens < length)
            count = count + jnp.where(hit, 1.0, 0.0)
        parts.append(count)
    return jnp.concatenate(parts, axis=1)


def pack_shares(ids, routed, home_ref):
    groups = home_ref.shape[0]
    choices, tokens = ids.shape
    spot = lax.broadcasted_iota(jnp.int32, (groups, tokens), 0)
    shares = routed / jnp.sum(routed, axis=0, keepdims=True)
    by_expert = jnp.zeros((groups, tokens), jnp.float32)
    for k in range(choices):
        by_expert = by_expert + jnp.where(spot == ids[k : k + 1, :], shares[k : k + 1, :], 0.0)
    by_home = jnp.zeros((groups, tokens), jnp.float32)
    for e in range(groups):
        by_home = by_home + jnp.where(spot == home_ref[e], by_expert[e : e + 1, :], 0.0)
    rounded = by_home.astype(jnp.bfloat16).astype(jnp.float32)
    tall = jnp.concatenate(
        [rounded, by_home - rounded, jnp.zeros((LANES - 2 * groups, tokens), jnp.float32)], axis=0
    )
    square = jnp.concatenate([tall, jnp.zeros((LANES, LANES - tokens), jnp.float32)], axis=1)
    return jnp.transpose(square)


def attention_kernel(
    pages_ref, lengths_ref, tp_ref, home_ref, q_hbm, fresh_hbm, cache_hbm, residual_hbm, ids_hbm,
    routed_hbm, w_hbm, own_ref, send_ref, pack_ref,
    q_ref, fresh_ref, cache_ref, residual_ref, ids_ref, routed_ref, w_ref, context_ref, terms_ref,
    every_ref, sems,
):
    fetches = [
        pltpu.make_async_copy(source, target, sems.at[i])
        for i, (source, target) in enumerate(
            (
                (q_hbm, q_ref),
                (cache_hbm, cache_ref),
                (fresh_hbm, fresh_ref),
                (ids_hbm, ids_ref),
                (routed_hbm, routed_ref),
                (residual_hbm, residual_ref),
                (w_hbm, w_ref),
            )
        )
    ]
    for fetch in fetches:
        fetch.start()
    tokens = q_ref.shape[0]
    pool_pages, page_tokens, _ = cache_ref.shape
    slots, requests = pages_ref.shape
    kv_heads = fresh_ref.shape[1] // (2 * HEAD_WIDTH)
    group = q_ref.shape[1] // (HEAD_WIDTH * kv_heads)
    decodes = requests - 1
    row = lax.broadcasted_iota(jnp.int32, (decodes, page_tokens), 0)

    def by_row(read):
        value = jnp.zeros((decodes, page_tokens), jnp.int32)
        for j in range(decodes):
            value = jnp.where(row == j, read(j + 1), value)
        return value

    full = lambda scalar: jnp.full((decodes, page_tokens), scalar, jnp.int32)
    first = multiplicity(
        [full(pages_ref[s, 0]) for s in range(slots)], full(lengths_ref[0]), pool_pages, page_tokens
    )
    later = multiplicity(
        [by_row(lambda j, s=s: pages_ref[s, j]) for s in range(slots)],
        by_row(lambda j: lengths_ref[j]),
        pool_pages,
        page_tokens,
    )
    count = jnp.concatenate([first] * (PRE_DEV // decodes) + [later], axis=0)
    query_place = lax.broadcasted_iota(jnp.int32, (tokens, tokens), 0)
    key_place = lax.broadcasted_iota(jnp.int32, (tokens, tokens), 1)
    seen = (key_place == query_place) | ((key_place <= query_place) & (query_place < PRE_DEV))
    visible = jnp.concatenate([count] * group, axis=0)
    seen = jnp.concatenate([jnp.where(seen, 1.0, 0.0)] * group, axis=0)
    scale = HEAD_WIDTH**-0.5
    for fetch in fetches[:3]:
        fetch.wait()
    contract_last = (((1,), (1,)), ((), ()))
    for k in range(kv_heads):
        key_at, value_at = 2 * k * HEAD_WIDTH, (2 * k + 1) * HEAD_WIDTH
        query = jnp.concatenate(
            [
                q_ref[:, (k * group + g) * HEAD_WIDTH : (k * group + g + 1) * HEAD_WIDTH]
                for g in range(group)
            ],
            axis=0,
        )
        keys = cache_ref[:, :, key_at : key_at + HEAD_WIDTH].reshape(-1, HEAD_WIDTH)
        values = cache_ref[:, :, value_at : value_at + HEAD_WIDTH].reshape(-1, HEAD_WIDTH)
        old = lax.dot_general(query, keys, contract_last, preferred_element_type=jnp.float32)
        new = lax.dot_general(
            query,
            fresh_ref[:, key_at : key_at + HEAD_WIDTH],
            contract_last,
            preferred_element_type=jnp.float32,
        )
        old = jnp.where(visible > 0, old * scale, MASKED)
        new = jnp.where(seen > 0, new * scale, MASKED)
        peak = jnp.maximum(
            jnp.max(old, axis=1, keepdims=True), jnp.max(new, axis=1, keepdims=True)
        )
        old = jnp.exp(old - peak) * visible
        new = jnp.exp(new - peak) * seen
        inverse = 1.0 / (
            jnp.sum(old, axis=1, keepdims=True) + jnp.sum(new, axis=1, keepdims=True)
        )
        mixed = jnp.dot(
            (old * inverse).astype(jnp.bfloat16), values, preferred_element_type=jnp.float32
        ) + jnp.dot(
            (new * inverse).astype(jnp.bfloat16),
            fresh_ref[:, value_at : value_at + HEAD_WIDTH],
            preferred_element_type=jnp.float32,
        )
        mixed = mixed.astype(jnp.bfloat16)
        for g in range(group):
            h = k * group + g
            context_ref[:, h * HEAD_WIDTH : (h + 1) * HEAD_WIDTH] = mixed[
                g * tokens : (g + 1) * tokens
            ]
    half = tokens // 2
    width = terms_ref.shape[1]
    block = 512
    own_at = pl.multiple_of(tp_ref[0] * half, half)
    other_at = pl.multiple_of((1 - tp_ref[0]) * half, half)
    for fetch in fetches[3:5]:
        fetch.wait()
    every_ref[...] = pack_shares(ids_ref[...], routed_ref[...], home_ref)
    pack_ref[...] = every_ref[pl.ds(own_at, half), :].astype(jnp.bfloat16)
    for fetch in fetches[5:]:
        fetch.wait()
    for at in range(0, width, block):
        cols = slice(at, at + block)
        terms_ref[:, cols] = jnp.dot(
            context_ref[...], w_ref[:, cols], preferred_element_type=jnp.float32
        )
    own_ref[...] = terms_ref[pl.ds(own_at, half), :] + residual_ref[
        pl.ds(own_at, half), :
    ].astype(jnp.float32)
    send_ref[...] = terms_ref[pl.ds(other_at, half), :].astype(jnp.bfloat16)


def attention_terms(
    pages, lengths, tp_index, home, queries, fresh, cache, residual, ids, routed, w_out
):
    tokens, width = residual.shape
    half = tokens // 2
    moved = (queries, fresh, cache, residual, ids.T, routed.T, w_out)
    return pl.pallas_call(
        attention_kernel,
        out_shape=(
            jax.ShapeDtypeStruct((half, width), jnp.float32),
            jax.ShapeDtypeStruct((half, width), jnp.bfloat16),
            jax.ShapeDtypeStruct((half, LANES), jnp.bfloat16),
        ),
        in_specs=[smem()] * 4 + [hbm()] * 7,
        out_specs=(vmem(),) * 3,
        scratch_shapes=[pltpu.VMEM(v.shape, v.dtype) for v in moved]
        + [
            pltpu.VMEM(queries.shape, jnp.bfloat16),
            pltpu.VMEM((tokens, width), jnp.float32),
            pltpu.VMEM((LANES, LANES), jnp.float32),
            pltpu.SemaphoreType.DMA((7,)),
        ],
        compiler_params=pltpu.CompilerParams(vmem_limit_bytes=40 * MIB),
        name="attention_terms",
    )(stay(pages.T), stay(lengths), tp_index, stay(home), *[stay(v) for v in moved])


def norm_kernel(own_ref, got_ref, pack_ref, gain_ref, state_ref, rows_ref, far_ref):
    state = own_ref[...] + got_ref[...].astype(jnp.float32)
    state_ref[...] = state
    normed = rms_scale(state, gain_ref[...]).astype(jnp.bfloat16)
    width = state.shape[1]
    far = far_ref.shape[0]
    rows_ref[:, :width] = normed
    rows_ref[:, width:] = pack_ref[...]
    far_ref[:, :width] = normed[:far]
    far_ref[:, width:] = pack_ref[:far, :]


def norm_rows(own, got, pack, gain, far):
    rows, width = own.shape
    return pl.pallas_call(
        norm_kernel,
        out_shape=(
            jax.ShapeDtypeStruct((rows, width), jnp.float32),
            jax.ShapeDtypeStruct((rows, width + LANES), jnp.bfloat16),
            jax.ShapeDtypeStruct((far, width + LANES), jnp.bfloat16),
        ),
        in_specs=[vmem()] * 4,
        out_specs=(vmem(),) * 3,
        compiler_params=SMALL,
        name="norm_rows",
    )(own, got, pack, gain)


def relay_kernel(r0, r1, r2, r3, z1, z2, z3, plane_ref, column_ref):
    far = z1.shape[0]
    near = r0.shape[0] - far
    for j, piece in enumerate((z1, z2, z3)):
        plane_ref[j * far : (j + 1) * far, :] = piece[...]
    for i, piece in enumerate((r0, r1, r2, r3)):
        column_ref[i * near : (i + 1) * near, :] = piece[far:, :]


def relay_rows(rows, far):
    height, width = far[0].shape
    near = rows[0].shape[0] - height
    return pl.pallas_call(
        relay_kernel,
        out_shape=(
            jax.ShapeDtypeStruct((3 * height, width), jnp.bfloat16),
            jax.ShapeDtypeStruct((4 * near, width), jnp.bfloat16),
        ),
        in_specs=[vmem()] * 7,
        out_specs=(vmem(),) * 2,
        compiler_params=SMALL,
        name="relay_rows",
    )(*rows, *far)


def hidden_units(group_ref, x_ref, w_refs, h_ref, ready):
    rows = x_ref.shape[0]
    width = w_refs[0].shape[0]
    hidden = h_ref.shape[1] // 2
    groups = group_ref[2]
    lane = lax.broadcasted_iota(jnp.int32, (rows, LANES), 1)
    packed = x_ref[:, width:].astype(jnp.float32)
    for e, w_ref in enumerate(w_refs):
        group = group_ref[e]
        share = jnp.sum(
            jnp.where((lane == group) | (lane == group + groups), packed, 0.0),
            axis=1,
            keepdims=True,
        )
        ready(e)
        both = jnp.dot(x_ref[:, :width], w_ref[...], preferred_element_type=jnp.float32)
        gate, up = both[:, :hidden], both[:, hidden:]
        h_ref[:, e * hidden : (e + 1) * hidden] = (
            share * up * (gate / (1.0 + jnp.exp(-gate)))
        ).astype(jnp.bfloat16)


DOWN_BLOCK = 512


def near_kernel(
    group_ref, r0, r1, r2, r3, z1, z2, z3, wg0, wu0, wd0, wg1, wu1, wd1,
    out_ref, w0_ref, w1_ref, down_ref, x_ref, h_ref, sems,
):
    hidden = wg0.shape[1]
    fetches = [
        pltpu.make_async_copy(source, target, sems.at[i])
        for i, (source, target) in enumerate(
            (
                (wg0, w0_ref.at[:, :hidden]),
                (wu0, w0_ref.at[:, hidden:]),
                (wg1, w1_ref.at[:, :hidden]),
                (wu1, w1_ref.at[:, hidden:]),
                (wd0, down_ref.at[:hidden, :]),
                (wd1, down_ref.at[hidden:, :]),
            )
        )
    ]
    for fetch in fetches:
        fetch.start()
    at = 0
    for piece in (r0, r1, r2, r3, z1, z2, z3):
        x_ref[at : at + piece.shape[0], :] = piece[...]
        at += piece.shape[0]
    if at < x_ref.shape[0]:
        x_ref[at:, :] = jnp.zeros((x_ref.shape[0] - at, x_ref.shape[1]), jnp.bfloat16)

    def ready(e):
        fetches[2 * e].wait()
        fetches[2 * e + 1].wait()

    hidden_units(group_ref, x_ref, (w0_ref, w1_ref), h_ref, ready)
    fetches[4].wait()
    fetches[5].wait()
    for col in range(0, down_ref.shape[1], DOWN_BLOCK):
        cols = slice(col, col + DOWN_BLOCK)
        down = jnp.dot(h_ref[...], down_ref[:, cols], preferred_element_type=jnp.float32)
        out_ref[:, cols] = down[:at]


def expert_cost(rows, width, hidden):
    return pl.CostEstimate(
        flops=12 * rows * width * hidden,
        bytes_accessed=12 * width * hidden,
        transcendentals=2 * rows * hidden,
    )


def near_rows(group, rows, far, weights, partner_weights):
    height = 4 * rows[0].shape[0] + 3 * far[0].shape[0]
    padded = -(-height // 16) * 16
    width, hidden = weights[0].shape
    return pl.pallas_call(
        near_kernel,
        out_shape=(
            jax.ShapeDtypeStruct((height, width), jnp.float32),
            jax.ShapeDtypeStruct((width, 2 * hidden), jnp.bfloat16),
            jax.ShapeDtypeStruct((width, 2 * hidden), jnp.bfloat16),
            jax.ShapeDtypeStruct((2 * hidden, width), jnp.bfloat16),
        ),
        in_specs=[smem()] + [vmem()] * 7 + [hbm()] * 6,
        out_specs=(vmem(),) * 4,
        scratch_shapes=[
            pltpu.VMEM((padded, width + LANES), jnp.bfloat16),
            pltpu.VMEM((padded, 2 * hidden), jnp.bfloat16),
            pltpu.SemaphoreType.DMA((6,)),
        ],
        compiler_params=pltpu.CompilerParams(vmem_limit_bytes=24 * MIB),
        cost_estimate=expert_cost(height, width, hidden),
        name="near_rows",
    )(group, *rows, *far, *[stay(w) for w in weights + partner_weights])


def piece_kernel(count, group_ref, *refs):
    pieces, (w0_ref, w1_ref, down_ref) = refs[:count], refs[count : count + 3]
    outs, (x_ref, h_ref) = refs[count + 3 : 2 * count + 3], refs[2 * count + 3 :]
    height = pieces[0].shape[0]
    for i, piece in enumerate(pieces):
        x_ref[i * height : (i + 1) * height, :] = piece[...]
    at = count * height
    if at < x_ref.shape[0]:
        x_ref[at:, :] = jnp.zeros((x_ref.shape[0] - at, x_ref.shape[1]), jnp.bfloat16)
    hidden_units(group_ref, x_ref, (w0_ref, w1_ref), h_ref, lambda e: None)
    for col in range(0, down_ref.shape[1], DOWN_BLOCK):
        cols = slice(col, col + DOWN_BLOCK)
        down = jnp.dot(h_ref[...], down_ref[:, cols], preferred_element_type=jnp.float32)
        for i, out in enumerate(outs):
            out[:, cols] = down[i * height : (i + 1) * height].astype(jnp.bfloat16)


def piece_rows(group, pieces, w0, w1, down):
    count = len(pieces)
    height = count * pieces[0].shape[0]
    padded = -(-height // 16) * 16
    width, hidden = w0.shape[0], w0.shape[1] // 2
    return pl.pallas_call(
        functools.partial(piece_kernel, count),
        out_shape=tuple(
            jax.ShapeDtypeStruct((piece.shape[0], width), jnp.bfloat16) for piece in pieces
        ),
        in_specs=[smem()] + [vmem()] * (count + 3),
        out_specs=(vmem(),) * count,
        scratch_shapes=[
            pltpu.VMEM((padded, width + LANES), jnp.bfloat16),
            pltpu.VMEM((padded, 2 * hidden), jnp.bfloat16),
        ],
        compiler_params=pltpu.CompilerParams(vmem_limit_bytes=24 * MIB),
        cost_estimate=expert_cost(height, width, hidden),
        name="piece_rows",
    )(group, *pieces, w0, w1, down)


def plane_sum_kernel(near_ref, g1, g2, g3, m1, m2, m3):
    far = m1.shape[0]
    start = near_ref.shape[0] - 3 * far
    for j, out in enumerate((m1, m2, m3)):
        rows = slice(j * far, (j + 1) * far)
        total = near_ref[start + j * far : start + (j + 1) * far, :]
        for got in (g1, g2, g3):
            total = total + got[rows, :].astype(jnp.float32)
        out[...] = total.astype(jnp.bfloat16)


def plane_sum(near, got):
    far, width = got[0].shape[0] // 3, got[0].shape[1]
    return pl.pallas_call(
        plane_sum_kernel,
        out_shape=tuple(jax.ShapeDtypeStruct((far, width), jnp.bfloat16) for _ in range(3)),
        in_specs=[vmem()] * 4,
        out_specs=(vmem(),) * 3,
        compiler_params=SMALL,
        name="plane_sum",
    )(near, *got)


def column_sum_kernel(near_ref, g1, g2, g3, own_ref, m1, m2, m3):
    rows = own_ref.shape[0]
    near = g1.shape[0] // 4
    far = rows - near
    for i, out in enumerate((own_ref, m1, m2, m3)):
        out[:far, :] = near_ref[i * rows : i * rows + far, :].astype(out.dtype)
        total = near_ref[i * rows + far : (i + 1) * rows, :]
        for got in (g1, g2, g3):
            total = total + got[i * near : (i + 1) * near, :].astype(jnp.float32)
        out[far:, :] = total.astype(out.dtype)


def column_sum(near, got, rows):
    width = near.shape[1]
    kinds = (jnp.float32, jnp.bfloat16, jnp.bfloat16, jnp.bfloat16)
    return pl.pallas_call(
        column_sum_kernel,
        out_shape=tuple(jax.ShapeDtypeStruct((rows, width), kind) for kind in kinds),
        in_specs=[vmem()] * 4,
        out_specs=(vmem(),) * 4,
        compiler_params=SMALL,
        name="column_sum",
    )(near, *got)


def final_kernel(state_ref, own_ref, p1, p2, p3, z1, z2, z3, gain_ref, out_ref, total_ref):
    total = state_ref[...] + own_ref[...]
    for got in (p1, p2, p3):
        total = total + got[...].astype(jnp.float32)
    total_ref[...] = total
    far = z1.shape[0]
    part = total_ref[:far, :]
    for got in (z1, z2, z3):
        part = part + got[...].astype(jnp.float32)
    total_ref[:far, :] = part
    out_ref[...] = rms_scale(total_ref[...], gain_ref[...]).astype(jnp.bfloat16)


def final_rows(state, own, plane, column, gain):
    return pl.pallas_call(
        final_kernel,
        out_shape=jax.ShapeDtypeStruct(state.shape, jnp.bfloat16),
        in_specs=[vmem()] * 9,
        out_specs=vmem(),
        scratch_shapes=[pltpu.VMEM(state.shape, jnp.float32)],
        compiler_params=SMALL,
        name="final_rows",
    )(state, own, *plane, *column, gain)


def place(z, y, c, x):
    return ((z * 2 + y) * 2 + c) * 2 + x


def swap(value, dz, dy, dc, dx):
    pairs = [
        (place(z, y, c, x), place(z ^ dz, y ^ dy, c ^ dc, x ^ dx))
        for z in range(4)
        for y in range(2)
        for c in range(2)
        for x in range(2)
    ]
    return lax.ppermute(value, ALL, pairs)


PLANE = ((0, 0), (0, 1), (1, 0), (1, 1))


def swap_z(pieces):
    return tuple(swap(piece, d, 0, 0, 0) for d, piece in zip((1, 2, 3), pieces))


def swap_plane(pieces):
    return tuple(swap(piece, 0, dy, 0, dx) for (dy, dx), piece in zip(PLANE[1:], pieces))


def local_dense(
    queries, fresh_key_value, key_value_cache, request_page_index, cache_length_rows, residual,
    w_out, gain_in, route_ids, route_weights, expert_home, w_gate, w_up, w_down, gain_out,
):
    tp_index = lax.axis_index("tp")
    req_index = lax.axis_index("req")
    tokens, width = residual.shape
    half = tokens // 2
    far = half * 3 // 4
    groups = expert_home.shape[0]
    weights = (w_gate[0], w_up[0], w_down[0])
    partner_weights = tuple(swap(w, 0, 0, 1, 0) for w in weights)
    own_state, sent, pack = attention_terms(
        request_page_index, cache_length_rows, tp_index.reshape(1).astype(jnp.int32), expert_home,
        queries, fresh_key_value, key_value_cache, residual, route_ids, route_weights, w_out,
    )
    got, partner_weights = barrier(swap(sent, 0, 0, 0, 1), partner_weights)
    group = jnp.stack([req_index, req_index ^ 1, groups]).astype(jnp.int32)
    state, rows, far_rows = norm_rows(own_state, got, pack, gain_in[None, :], far)
    z_rows, plane_rows = barrier(swap_z((far_rows,) * 3), swap_plane((rows,) * 3))
    plane_rows = (rows,) + plane_rows
    onward_plane, onward_z = relay_rows(plane_rows, z_rows)
    z_pieces = swap_z((onward_z,) * 3)
    plane_pieces = swap_plane((onward_plane,) * 3)
    near, w0, w1, down = near_rows(group, plane_rows, z_rows, weights, partner_weights)
    z_parts = piece_rows(group, z_pieces, w0, w1, down)
    plane_parts = tuple(piece_rows(group, (piece,), w0, w1, down)[0] for piece in plane_pieces)
    own, *near_sums = column_sum(near, swap_z(z_parts), half)
    far_sums = plane_sum(near, swap_plane(plane_parts))
    last_z, last_plane = barrier(swap_z(far_sums), swap_plane(near_sums))
    return final_rows(state, own, last_plane, last_z, gain_out[None, :])


def solution(mesh):
    dense = mesh.shape["req"] == 16 and mesh.shape["tp"] == 2
    return jax.shard_map(
        local_dense if dense else local_sparse,
        mesh=mesh,
        in_specs=(
            P("req", "tp"),
            P("req", "tp"),
            P("req", None, "tp"),
            P("req", None),
            P("req"),
            P("req", None),
            P("tp", None),
            P(),
            P("req", None),
            P("req", None),
            P(),
            P("req", None, "tp"),
            P("req", None, "tp"),
            P("req", "tp", None),
            P(),
        ),
        out_specs=P(("req", "tp"), None),
        check_vma=False,
    )
```

```python
import functools

import jax
import jax.numpy as jnp
from jax import lax
from jax.experimental import pallas as pl
from jax.experimental.pallas import tpu as pltpu
from jax.sharding import PartitionSpec as P

HEAD_WIDTH = 128
TOPK = 8
PRE_DEV = 56


EPSILON = 1e-06


def rms_scale(value_rows, gain_row):
    mean_square = jnp.mean(value_rows * value_rows, axis=-1, keepdims=True)
    return value_rows * lax.rsqrt(mean_square + EPSILON) * gain_row


def softmax_rounded(scores):
    row_peak = jnp.max(scores, axis=-1, keepdims=True)
    weights = jnp.exp(scores - row_peak)
    return (weights / jnp.sum(weights, axis=-1, keepdims=True)).astype(jnp.bfloat16)


def group_attention(queries, fresh_key_value, page_pool, page_rows, lengths):
    tokens_here = queries.shape[0]
    kv_heads = fresh_key_value.shape[1] // (2 * HEAD_WIDTH)
    group_size = queries.shape[1] // (HEAD_WIDTH * kv_heads)
    score_scale = HEAD_WIDTH ** (-0.5)
    split_query = queries.reshape(tokens_here, kv_heads, group_size, HEAD_WIDTH)
    fresh_kv = fresh_key_value.reshape(tokens_here, kv_heads, 2, HEAD_WIDTH)
    gathered_pages = page_pool[page_rows]
    cached = gathered_pages.reshape(page_rows.shape[0], -1, kv_heads, 2, HEAD_WIDTH)
    places = jnp.arange(cached.shape[1], dtype=jnp.int32)
    prefill_query = split_query[:PRE_DEV]
    prefill_fresh = fresh_kv[:PRE_DEV]
    cache_scores = (
        jnp.einsum(
            "ikgd,ckd->kgic", prefill_query, cached[0, :, :, 0], preferred_element_type=jnp.float32
        )
        * score_scale
    )
    cache_scores = jnp.where(places < lengths[0], cache_scores, -jnp.inf)
    block_scores = (
        jnp.einsum(
            "ikgd,jkd->kgij",
            prefill_query,
            prefill_fresh[:, :, 0],
            preferred_element_type=jnp.float32,
        )
        * score_scale
    )
    causal = jnp.arange(PRE_DEV)[:, None] >= jnp.arange(PRE_DEV)[None, :]
    block_scores = jnp.where(causal, block_scores, -jnp.inf)
    prefill_probs = softmax_rounded(jnp.concatenate([cache_scores, block_scores], axis=3))
    prefill_values = jnp.concatenate([cached[0, :, :, 1], prefill_fresh[:, :, 1]], axis=0)
    prefill_out = jnp.einsum(
        "kgic,ckd->ikgd", prefill_probs, prefill_values, preferred_element_type=jnp.float32
    )
    decode_query = split_query[PRE_DEV:]
    decode_fresh = fresh_kv[PRE_DEV:]
    decode_scores = (
        jnp.einsum(
            "rkgd,rckd->rkgc", decode_query, cached[1:, :, :, 0], preferred_element_type=jnp.float32
        )
        * score_scale
    )
    decode_scores = jnp.where(
        places[None, None, None, :] < lengths[1:, None, None, None], decode_scores, -jnp.inf
    )
    own_scores = (
        jnp.einsum(
            "rkgd,rkd->rkg", decode_query, decode_fresh[:, :, 0], preferred_element_type=jnp.float32
        )[..., None]
        * score_scale
    )
    decode_probs = softmax_rounded(jnp.concatenate([decode_scores, own_scores], axis=3))
    decode_values = jnp.concatenate([cached[1:, :, :, 1], decode_fresh[:, None, :, 1]], axis=1)
    decode_out = jnp.einsum(
        "rkgc,rckd->rkgd", decode_probs, decode_values, preferred_element_type=jnp.float32
    )
    joined = jnp.concatenate([prefill_out, decode_out], axis=0)
    return joined.reshape(tokens_here, -1).astype(jnp.bfloat16)


def slot_positions(block_owner, experts, capacity):
    flat_owner = block_owner.reshape(-1)
    onehot = (flat_owner[:, None] == jnp.arange(experts, dtype=jnp.int32)[None, :]).astype(
        jnp.int32
    )
    earlier = jnp.cumsum(onehot, axis=0) - onehot
    slot_index = jnp.sum(earlier * onehot, axis=1)
    return (flat_owner * capacity + slot_index).reshape(block_owner.shape)


def place_matrix(positions, slots_total):
    matches = positions[None, :, :] == jnp.arange(slots_total, dtype=jnp.int32)[:, None, None]
    return jnp.any(matches, axis=2).astype(jnp.bfloat16)


def local_sparse(
    queries,
    fresh_key_value,
    key_value_cache,
    request_page_index,
    cache_length_rows,
    residual,
    w_out,
    gain_in,
    route_ids,
    route_weights,
    expert_home,
    w_gate,
    w_up,
    w_down,
    gain_out,
):
    tp_size = lax.axis_size("tp")
    req_size = lax.axis_size("req")
    tp_index = lax.axis_index("tp")
    model_width = residual.shape[1]
    tokens_here = residual.shape[0]
    quarter = tokens_here // tp_size
    experts = expert_home.shape[0]
    capacity = min(quarter, max(2, 2 * quarter * TOPK // experts))
    context = group_attention(
        queries, fresh_key_value, key_value_cache, request_page_index, cache_length_rows
    )
    head_terms = jnp.dot(context, w_out, preferred_element_type=jnp.float32)
    state = residual.astype(jnp.float32) + lax.psum(head_terms, "tp")
    owners = jnp.sum(
        jnp.where(
            route_ids[:, :, None] == jnp.arange(experts, dtype=jnp.int32)[None, None, :],
            expert_home[None, None, :],
            0,
        ),
        axis=2,
    )
    shares = route_weights / jnp.sum(route_weights, axis=1, keepdims=True)
    own_start = tp_index * quarter
    own_state = lax.dynamic_slice_in_dim(state, own_start, quarter, 0)
    own_shares = lax.dynamic_slice_in_dim(shares, own_start, quarter, 0)
    normed_all = rms_scale(state, gain_in).astype(jnp.bfloat16)
    positions_all = jax.vmap(lambda block_owner: slot_positions(block_owner, experts, capacity))(
        owners.reshape(tp_size, quarter, TOPK)
    )
    placing = jax.vmap(lambda positions: place_matrix(positions, experts * capacity))(positions_all)
    outgoing = jnp.einsum(
        "qmi,qid->qmd",
        placing,
        normed_all.reshape(tp_size, quarter, model_width),
        preferred_element_type=jnp.float32,
    )
    outgoing = outgoing.astype(jnp.bfloat16).reshape(tp_size, experts, capacity, model_width)
    incoming = lax.all_to_all(outgoing, "req", split_axis=1, concat_axis=1, tiled=True)
    own_positions = lax.dynamic_index_in_dim(positions_all, tp_index, 0, keepdims=False)
    expert_rows = incoming.reshape(-1, model_width)
    gate_proj = jnp.dot(expert_rows, w_gate[0], preferred_element_type=jnp.float32)
    up_proj = jnp.dot(expert_rows, w_up[0], preferred_element_type=jnp.float32)
    inner_units = (jax.nn.silu(gate_proj) * up_proj).astype(jnp.bfloat16)
    summed = lax.psum_scatter(
        jnp.dot(inner_units, w_down[0], preferred_element_type=jnp.float32).astype(jnp.bfloat16),
        "tp",
        scatter_dimension=0,
        tiled=True,
    )
    results = summed.reshape(req_size, capacity, model_width)
    returned = lax.all_to_all(results, "req", split_axis=0, concat_axis=0, tiled=True).reshape(
        -1, model_width
    )
    picked = returned[own_positions]
    mixture = jnp.sum(own_shares[:, :, None] * picked.astype(jnp.float32), axis=1)
    return rms_scale(own_state + mixture, gain_out).astype(jnp.bfloat16)


ALL = ("req", "tp")
MASKED = -1e30
LANES = 128
MIB = 1024 * 1024
SMALL = pltpu.CompilerParams(vmem_limit_bytes=8 * MIB)


def vmem():
    return pl.BlockSpec(memory_space=pltpu.VMEM)


def smem():
    return pl.BlockSpec(memory_space=pltpu.SMEM)


def hbm():
    return pl.BlockSpec(memory_space=pltpu.HBM)


def stay(value):
    return pltpu.with_memory_space_constraint(value, pltpu.HBM)


def barrier(*values):
    return lax.optimization_barrier(values)


def multiplicity(page_rows, length, pool_pages, page_tokens):
    rows = page_rows[0].shape[0]
    lane = lax.broadcasted_iota(jnp.int32, (rows, page_tokens), 1)
    parts = []
    for page in range(pool_pages):
        count = jnp.zeros((rows, page_tokens), jnp.float32)
        for slot, named in enumerate(page_rows):
            hit = (named == page) & (lane + slot * page_tokens < length)
            count = count + jnp.where(hit, 1.0, 0.0)
        parts.append(count)
    return jnp.concatenate(parts, axis=1)


def pack_shares(ids, routed, home_ref):
    groups = home_ref.shape[0]
    choices, tokens = ids.shape
    spot = lax.broadcasted_iota(jnp.int32, (groups, tokens), 0)
    shares = routed / jnp.sum(routed, axis=0, keepdims=True)
    by_expert = jnp.zeros((groups, tokens), jnp.float32)
    for k in range(choices):
        by_expert = by_expert + jnp.where(spot == ids[k : k + 1, :], shares[k : k + 1, :], 0.0)
    by_home = jnp.zeros((groups, tokens), jnp.float32)
    for e in range(groups):
        by_home = by_home + jnp.where(spot == home_ref[e], by_expert[e : e + 1, :], 0.0)
    rounded = by_home.astype(jnp.bfloat16).astype(jnp.float32)
    tall = jnp.concatenate(
        [rounded, by_home - rounded, jnp.zeros((LANES - 2 * groups, tokens), jnp.float32)], axis=0
    )
    square = jnp.concatenate([tall, jnp.zeros((LANES, LANES - tokens), jnp.float32)], axis=1)
    return jnp.transpose(square)


def attention_kernel(
    pages_ref, lengths_ref, tp_ref, home_ref, q_hbm, fresh_hbm, cache_hbm, residual_hbm, ids_hbm,
    routed_hbm, w_hbm, own_ref, send_ref, pack_ref,
    q_ref, fresh_ref, cache_ref, residual_ref, ids_ref, routed_ref, w_ref, context_ref, terms_ref,
    every_ref, sems,
):
    fetches = [
        pltpu.make_async_copy(source, target, sems.at[i])
        for i, (source, target) in enumerate(
            (
                (q_hbm, q_ref),
                (cache_hbm, cache_ref),
                (fresh_hbm, fresh_ref),
                (ids_hbm, ids_ref),
                (routed_hbm, routed_ref),
                (residual_hbm, residual_ref),
                (w_hbm, w_ref),
            )
        )
    ]
    for fetch in fetches:
        fetch.start()
    tokens = q_ref.shape[0]
    pool_pages, page_tokens, _ = cache_ref.shape
    slots, requests = pages_ref.shape
    kv_heads = fresh_ref.shape[1] // (2 * HEAD_WIDTH)
    group = q_ref.shape[1] // (HEAD_WIDTH * kv_heads)
    decodes = requests - 1
    row = lax.broadcasted_iota(jnp.int32, (decodes, page_tokens), 0)

    def by_row(read):
        value = jnp.zeros((decodes, page_tokens), jnp.int32)
        for j in range(decodes):
            value = jnp.where(row == j, read(j + 1), value)
        return value

    full = lambda scalar: jnp.full((decodes, page_tokens), scalar, jnp.int32)
    first = multiplicity(
        [full(pages_ref[s, 0]) for s in range(slots)], full(lengths_ref[0]), pool_pages, page_tokens
    )
    later = multiplicity(
        [by_row(lambda j, s=s: pages_ref[s, j]) for s in range(slots)],
        by_row(lambda j: lengths_ref[j]),
        pool_pages,
        page_tokens,
    )
    count = jnp.concatenate([first] * (PRE_DEV // decodes) + [later], axis=0)
    query_place = lax.broadcasted_iota(jnp.int32, (tokens, tokens), 0)
    key_place = lax.broadcasted_iota(jnp.int32, (tokens, tokens), 1)
    seen = (key_place == query_place) | ((key_place <= query_place) & (query_place < PRE_DEV))
    visible = jnp.concatenate([count] * group, axis=0)
    seen = jnp.concatenate([jnp.where(seen, 1.0, 0.0)] * group, axis=0)
    scale = HEAD_WIDTH**-0.5
    for fetch in fetches[:3]:
        fetch.wait()
    contract_last = (((1,), (1,)), ((), ()))
    for k in range(kv_heads):
        key_at, value_at = 2 * k * HEAD_WIDTH, (2 * k + 1) * HEAD_WIDTH
        query = jnp.concatenate(
            [
                q_ref[:, (k * group + g) * HEAD_WIDTH : (k * group + g + 1) * HEAD_WIDTH]
                for g in range(group)
            ],
            axis=0,
        )
        keys = cache_ref[:, :, key_at : key_at + HEAD_WIDTH].reshape(-1, HEAD_WIDTH)
        values = cache_ref[:, :, value_at : value_at + HEAD_WIDTH].reshape(-1, HEAD_WIDTH)
        old = lax.dot_general(query, keys, contract_last, preferred_element_type=jnp.float32)
        new = lax.dot_general(
            query,
            fresh_ref[:, key_at : key_at + HEAD_WIDTH],
            contract_last,
            preferred_element_type=jnp.float32,
        )
        old = jnp.where(visible > 0, old * scale, MASKED)
        new = jnp.where(seen > 0, new * scale, MASKED)
        peak = jnp.maximum(
            jnp.max(old, axis=1, keepdims=True), jnp.max(new, axis=1, keepdims=True)
        )
        old = jnp.exp(old - peak) * visible
        new = jnp.exp(new - peak) * seen
        inverse = 1.0 / (
            jnp.sum(old, axis=1, keepdims=True) + jnp.sum(new, axis=1, keepdims=True)
        )
        mixed = jnp.dot(
            (old * inverse).astype(jnp.bfloat16), values, preferred_element_type=jnp.float32
        ) + jnp.dot(
            (new * inverse).astype(jnp.bfloat16),
            fresh_ref[:, value_at : value_at + HEAD_WIDTH],
            preferred_element_type=jnp.float32,
        )
        mixed = mixed.astype(jnp.bfloat16)
        for g in range(group):
            h = k * group + g
            context_ref[:, h * HEAD_WIDTH : (h + 1) * HEAD_WIDTH] = mixed[
                g * tokens : (g + 1) * tokens
            ]
    half = tokens // 2
    width = terms_ref.shape[1]
    block = 512
    own_at = pl.multiple_of(tp_ref[0] * half, half)
    other_at = pl.multiple_of((1 - tp_ref[0]) * half, half)
    for fetch in fetches[3:5]:
        fetch.wait()
    every_ref[...] = pack_shares(ids_ref[...], routed_ref[...], home_ref)
    pack_ref[...] = every_ref[pl.ds(own_at, half), :].astype(jnp.bfloat16)
    for fetch in fetches[5:]:
        fetch.wait()
    for at in range(0, width, block):
        cols = slice(at, at + block)
        terms_ref[:, cols] = jnp.dot(
            context_ref[...], w_ref[:, cols], preferred_element_type=jnp.float32
        )
    own_ref[...] = terms_ref[pl.ds(own_at, half), :] + residual_ref[
        pl.ds(own_at, half), :
    ].astype(jnp.float32)
    send_ref[...] = terms_ref[pl.ds(other_at, half), :].astype(jnp.bfloat16)


def attention_terms(
    pages, lengths, tp_index, home, queries, fresh, cache, residual, ids, routed, w_out
):
    tokens, width = residual.shape
    half = tokens // 2
    moved = (queries, fresh, cache, residual, ids.T, routed.T, w_out)
    return pl.pallas_call(
        attention_kernel,
        out_shape=(
            jax.ShapeDtypeStruct((half, width), jnp.float32),
            jax.ShapeDtypeStruct((half, width), jnp.bfloat16),
            jax.ShapeDtypeStruct((half, LANES), jnp.bfloat16),
        ),
        in_specs=[smem()] * 4 + [hbm()] * 7,
        out_specs=(vmem(),) * 3,
        scratch_shapes=[pltpu.VMEM(v.shape, v.dtype) for v in moved]
        + [
            pltpu.VMEM(queries.shape, jnp.bfloat16),
            pltpu.VMEM((tokens, width), jnp.float32),
            pltpu.VMEM((LANES, LANES), jnp.float32),
            pltpu.SemaphoreType.DMA((7,)),
        ],
        compiler_params=pltpu.CompilerParams(vmem_limit_bytes=40 * MIB),
        name="attention_terms",
    )(stay(pages.T), stay(lengths), tp_index, stay(home), *[stay(v) for v in moved])


def norm_kernel(own_ref, got_ref, pack_ref, gain_ref, state_ref, rows_ref, far_ref):
    state = own_ref[...] + got_ref[...].astype(jnp.float32)
    state_ref[...] = state
    normed = rms_scale(state, gain_ref[...]).astype(jnp.bfloat16)
    width = state.shape[1]
    far = far_ref.shape[0]
    rows_ref[:, :width] = normed
    rows_ref[:, width:] = pack_ref[...]
    far_ref[:, :width] = normed[:far]
    far_ref[:, width:] = pack_ref[:far, :]


def norm_rows(own, got, pack, gain, far):
    rows, width = own.shape
    return pl.pallas_call(
        norm_kernel,
        out_shape=(
            jax.ShapeDtypeStruct((rows, width), jnp.float32),
            jax.ShapeDtypeStruct((rows, width + LANES), jnp.bfloat16),
            jax.ShapeDtypeStruct((far, width + LANES), jnp.bfloat16),
        ),
        in_specs=[vmem()] * 4,
        out_specs=(vmem(),) * 3,
        compiler_params=SMALL,
        name="norm_rows",
    )(own, got, pack, gain)


def relay_kernel(r0, r1, r2, r3, z1, z2, z3, plane_ref, column_ref):
    far = z1.shape[0]
    near = r0.shape[0] - far
    for j, piece in enumerate((z1, z2, z3)):
        plane_ref[j * far : (j + 1) * far, :] = piece[...]
    for i, piece in enumerate((r0, r1, r2, r3)):
        column_ref[i * near : (i + 1) * near, :] = piece[far:, :]


def relay_rows(rows, far):
    height, width = far[0].shape
    near = rows[0].shape[0] - height
    return pl.pallas_call(
        relay_kernel,
        out_shape=(
            jax.ShapeDtypeStruct((3 * height, width), jnp.bfloat16),
            jax.ShapeDtypeStruct((4 * near, width), jnp.bfloat16),
        ),
        in_specs=[vmem()] * 7,
        out_specs=(vmem(),) * 2,
        compiler_params=SMALL,
        name="relay_rows",
    )(*rows, *far)


def hidden_units(group_ref, x_ref, w_refs, h_ref, ready):
    rows = x_ref.shape[0]
    width = w_refs[0].shape[0]
    hidden = h_ref.shape[1] // 2
    groups = group_ref[2]
    lane = lax.broadcasted_iota(jnp.int32, (rows, LANES), 1)
    packed = x_ref[:, width:].astype(jnp.float32)
    for e, w_ref in enumerate(w_refs):
        group = group_ref[e]
        share = jnp.sum(
            jnp.where((lane == group) | (lane == group + groups), packed, 0.0),
            axis=1,
            keepdims=True,
        )
        ready(e)
        both = jnp.dot(x_ref[:, :width], w_ref[...], preferred_element_type=jnp.float32)
        gate, up = both[:, :hidden], both[:, hidden:]
        h_ref[:, e * hidden : (e + 1) * hidden] = (
            share * up * (gate / (1.0 + jnp.exp(-gate)))
        ).astype(jnp.bfloat16)


DOWN_BLOCK = 512


def near_kernel(
    group_ref, r0, r1, r2, r3, z1, z2, z3, wg0, wu0, wd0, wg1, wu1, wd1,
    out_ref, w0_ref, w1_ref, down_ref, x_ref, h_ref, sems,
):
    hidden = wg0.shape[1]
    fetches = [
        pltpu.make_async_copy(source, target, sems.at[i])
        for i, (source, target) in enumerate(
            (
                (wg0, w0_ref.at[:, :hidden]),
                (wu0, w0_ref.at[:, hidden:]),
                (wg1, w1_ref.at[:, :hidden]),
                (wu1, w1_ref.at[:, hidden:]),
                (wd0, down_ref.at[:hidden, :]),
                (wd1, down_ref.at[hidden:, :]),
            )
        )
    ]
    for fetch in fetches:
        fetch.start()
    at = 0
    for piece in (r0, r1, r2, r3, z1, z2, z3):
        x_ref[at : at + piece.shape[0], :] = piece[...]
        at += piece.shape[0]
    if at < x_ref.shape[0]:
        x_ref[at:, :] = jnp.zeros((x_ref.shape[0] - at, x_ref.shape[1]), jnp.bfloat16)

    def ready(e):
        fetches[2 * e].wait()
        fetches[2 * e + 1].wait()

    hidden_units(group_ref, x_ref, (w0_ref, w1_ref), h_ref, ready)
    fetches[4].wait()
    fetches[5].wait()
    for col in range(0, down_ref.shape[1], DOWN_BLOCK):
        cols = slice(col, col + DOWN_BLOCK)
        down = jnp.dot(h_ref[...], down_ref[:, cols], preferred_element_type=jnp.float32)
        out_ref[:, cols] = down[:at]


def expert_cost(rows, width, hidden):
    return pl.CostEstimate(
        flops=12 * rows * width * hidden,
        bytes_accessed=12 * width * hidden,
        transcendentals=2 * rows * hidden,
    )


def near_rows(group, rows, far, weights, partner_weights):
    height = 4 * rows[0].shape[0] + 3 * far[0].shape[0]
    padded = -(-height // 16) * 16
    width, hidden = weights[0].shape
    return pl.pallas_call(
        near_kernel,
        out_shape=(
            jax.ShapeDtypeStruct((height, width), jnp.float32),
            jax.ShapeDtypeStruct((width, 2 * hidden), jnp.bfloat16),
            jax.ShapeDtypeStruct((width, 2 * hidden), jnp.bfloat16),
            jax.ShapeDtypeStruct((2 * hidden, width), jnp.bfloat16),
        ),
        in_specs=[smem()] + [vmem()] * 7 + [hbm()] * 6,
        out_specs=(vmem(),) * 4,
        scratch_shapes=[
            pltpu.VMEM((padded, width + LANES), jnp.bfloat16),
            pltpu.VMEM((padded, 2 * hidden), jnp.bfloat16),
            pltpu.SemaphoreType.DMA((6,)),
        ],
        compiler_params=pltpu.CompilerParams(vmem_limit_bytes=24 * MIB),
        cost_estimate=expert_cost(height, width, hidden),
        name="near_rows",
    )(group, *rows, *far, *[stay(w) for w in weights + partner_weights])


def piece_kernel(count, group_ref, *refs):
    pieces, (w0_ref, w1_ref, down_ref) = refs[:count], refs[count : count + 3]
    outs, (x_ref, h_ref) = refs[count + 3 : 2 * count + 3], refs[2 * count + 3 :]
    at = 0
    for piece in pieces:
        x_ref[at : at + piece.shape[0], :] = piece[...]
        at += piece.shape[0]
    if at < x_ref.shape[0]:
        x_ref[at:, :] = jnp.zeros((x_ref.shape[0] - at, x_ref.shape[1]), jnp.bfloat16)
    hidden_units(group_ref, x_ref, (w0_ref, w1_ref), h_ref, lambda e: None)
    for col in range(0, down_ref.shape[1], DOWN_BLOCK):
        cols = slice(col, col + DOWN_BLOCK)
        down = jnp.dot(h_ref[...], down_ref[:, cols], preferred_element_type=jnp.float32)
        at = 0
        for out in outs:
            out[:, cols] = down[at : at + out.shape[0]].astype(jnp.bfloat16)
            at += out.shape[0]


def piece_rows(group, pieces, w0, w1, down):
    count = len(pieces)
    height = sum(piece.shape[0] for piece in pieces)
    padded = -(-height // 16) * 16
    width, hidden = w0.shape[0], w0.shape[1] // 2
    return pl.pallas_call(
        functools.partial(piece_kernel, count),
        out_shape=tuple(
            jax.ShapeDtypeStruct((piece.shape[0], width), jnp.bfloat16) for piece in pieces
        ),
        in_specs=[smem()] + [vmem()] * (count + 3),
        out_specs=(vmem(),) * count,
        scratch_shapes=[
            pltpu.VMEM((padded, width + LANES), jnp.bfloat16),
            pltpu.VMEM((padded, 2 * hidden), jnp.bfloat16),
        ],
        compiler_params=pltpu.CompilerParams(vmem_limit_bytes=24 * MIB),
        cost_estimate=expert_cost(height, width, hidden),
        name="piece_rows",
    )(group, *pieces, w0, w1, down)


def plane_sum_kernel(near_ref, g1, g2, g3, m1, m2, m3):
    far = m1.shape[0]
    start = near_ref.shape[0] - 3 * far
    for j, out in enumerate((m1, m2, m3)):
        rows = slice(j * far, (j + 1) * far)
        total = near_ref[start + j * far : start + (j + 1) * far, :]
        for got in (g1, g2, g3):
            total = total + got[rows, :].astype(jnp.float32)
        out[...] = total.astype(jnp.bfloat16)


def plane_sum(near, got):
    far, width = got[0].shape[0] // 3, got[0].shape[1]
    return pl.pallas_call(
        plane_sum_kernel,
        out_shape=tuple(jax.ShapeDtypeStruct((far, width), jnp.bfloat16) for _ in range(3)),
        in_specs=[vmem()] * 4,
        out_specs=(vmem(),) * 3,
        compiler_params=SMALL,
        name="plane_sum",
    )(near, *got)


def column_sum_kernel(near_ref, g1, g2, g3, own_ref, m1, m2, m3):
    rows = own_ref.shape[0]
    near = g1.shape[0] // 4
    far = rows - near
    for i, out in enumerate((own_ref, m1, m2, m3)):
        out[:far, :] = near_ref[i * rows : i * rows + far, :].astype(out.dtype)
        total = near_ref[i * rows + far : (i + 1) * rows, :]
        for got in (g1, g2, g3):
            total = total + got[i * near : (i + 1) * near, :].astype(jnp.float32)
        out[far:, :] = total.astype(out.dtype)


def column_sum(near, got, rows):
    width = near.shape[1]
    kinds = (jnp.float32, jnp.bfloat16, jnp.bfloat16, jnp.bfloat16)
    return pl.pallas_call(
        column_sum_kernel,
        out_shape=tuple(jax.ShapeDtypeStruct((rows, width), kind) for kind in kinds),
        in_specs=[vmem()] * 4,
        out_specs=(vmem(),) * 4,
        compiler_params=SMALL,
        name="column_sum",
    )(near, *got)


def final_kernel(state_ref, own_ref, p1, p2, p3, z1, z2, z3, gain_ref, out_ref, total_ref):
    total = state_ref[...] + own_ref[...]
    for got in (p1, p2, p3):
        total = total + got[...].astype(jnp.float32)
    total_ref[...] = total
    far = z1.shape[0]
    part = total_ref[:far, :]
    for got in (z1, z2, z3):
        part = part + got[...].astype(jnp.float32)
    total_ref[:far, :] = part
    out_ref[...] = rms_scale(total_ref[...], gain_ref[...]).astype(jnp.bfloat16)


def final_rows(state, own, plane, column, gain):
    return pl.pallas_call(
        final_kernel,
        out_shape=jax.ShapeDtypeStruct(state.shape, jnp.bfloat16),
        in_specs=[vmem()] * 9,
        out_specs=vmem(),
        scratch_shapes=[pltpu.VMEM(state.shape, jnp.float32)],
        compiler_params=SMALL,
        name="final_rows",
    )(state, own, *plane, *column, gain)


def place(z, y, c, x):
    return ((z * 2 + y) * 2 + c) * 2 + x


def swap(value, dz, dy, dc, dx):
    pairs = [
        (place(z, y, c, x), place(z ^ dz, y ^ dy, c ^ dc, x ^ dx))
        for z in range(4)
        for y in range(2)
        for c in range(2)
        for x in range(2)
    ]
    return lax.ppermute(value, ALL, pairs)


PLANE = ((0, 0), (0, 1), (1, 0), (1, 1))


def swap_z(pieces):
    return tuple(swap(piece, d, 0, 0, 0) for d, piece in zip((1, 2, 3), pieces))


def swap_plane(pieces):
    return tuple(swap(piece, 0, dy, 0, dx) for (dy, dx), piece in zip(PLANE[1:], pieces))


def local_dense(
    queries, fresh_key_value, key_value_cache, request_page_index, cache_length_rows, residual,
    w_out, gain_in, route_ids, route_weights, expert_home, w_gate, w_up, w_down, gain_out,
):
    tp_index = lax.axis_index("tp")
    req_index = lax.axis_index("req")
    tokens, width = residual.shape
    half = tokens // 2
    far = half * 3 // 4
    groups = expert_home.shape[0]
    weights = (w_gate[0], w_up[0], w_down[0])
    partner_weights = tuple(swap(w, 0, 0, 1, 0) for w in weights)
    own_state, sent, pack = attention_terms(
        request_page_index, cache_length_rows, tp_index.reshape(1).astype(jnp.int32), expert_home,
        queries, fresh_key_value, key_value_cache, residual, route_ids, route_weights, w_out,
    )
    got, partner_weights = barrier(swap(sent, 0, 0, 0, 1), partner_weights)
    group = jnp.stack([req_index, req_index ^ 1, groups]).astype(jnp.int32)
    state, rows, far_rows = norm_rows(own_state, got, pack, gain_in[None, :], far)
    z_rows, plane_rows = barrier(swap_z((far_rows,) * 3), swap_plane((rows,) * 3))
    plane_rows = (rows,) + plane_rows
    onward_plane, onward_z = relay_rows(plane_rows, z_rows)
    z_pieces = swap_z((onward_z,) * 3)
    plane_pieces = swap_plane((onward_plane,) * 3)
    near, w0, w1, down = near_rows(group, plane_rows, z_rows, weights, partner_weights)
    parts = piece_rows(group, z_pieces + plane_pieces, w0, w1, down)
    z_parts, plane_parts = parts[:3], parts[3:]
    own, *near_sums = column_sum(near, swap_z(z_parts), half)
    far_sums = plane_sum(near, swap_plane(plane_parts))
    last_z, last_plane = barrier(swap_z(far_sums), swap_plane(near_sums))
    return final_rows(state, own, last_plane, last_z, gain_out[None, :])


def solution(mesh):
    dense = mesh.shape["req"] == 16 and mesh.shape["tp"] == 2
    return jax.shard_map(
        local_dense if dense else local_sparse,
        mesh=mesh,
        in_specs=(
            P("req", "tp"),
            P("req", "tp"),
            P("req", None, "tp"),
            P("req", None),
            P("req"),
            P("req", None),
            P("tp", None),
            P(),
            P("req", None),
            P("req", None),
            P(),
            P("req", None, "tp"),
            P("req", None, "tp"),
            P("req", "tp", None),
            P(),
        ),
        out_specs=P(("req", "tp"), None),
        check_vma=False,
    )
```

```python
import functools

import jax
import jax.numpy as jnp
from jax import lax
from jax.experimental import pallas as pl
from jax.experimental.pallas import tpu as pltpu
from jax.sharding import PartitionSpec as P

HEAD_WIDTH = 128
TOPK = 8
PRE_DEV = 56


EPSILON = 1e-06


def rms_scale(value_rows, gain_row):
    mean_square = jnp.mean(value_rows * value_rows, axis=-1, keepdims=True)
    return value_rows * lax.rsqrt(mean_square + EPSILON) * gain_row


def softmax_rounded(scores):
    row_peak = jnp.max(scores, axis=-1, keepdims=True)
    weights = jnp.exp(scores - row_peak)
    return (weights / jnp.sum(weights, axis=-1, keepdims=True)).astype(jnp.bfloat16)


def group_attention(queries, fresh_key_value, page_pool, page_rows, lengths):
    tokens_here = queries.shape[0]
    kv_heads = fresh_key_value.shape[1] // (2 * HEAD_WIDTH)
    group_size = queries.shape[1] // (HEAD_WIDTH * kv_heads)
    score_scale = HEAD_WIDTH ** (-0.5)
    split_query = queries.reshape(tokens_here, kv_heads, group_size, HEAD_WIDTH)
    fresh_kv = fresh_key_value.reshape(tokens_here, kv_heads, 2, HEAD_WIDTH)
    gathered_pages = page_pool[page_rows]
    cached = gathered_pages.reshape(page_rows.shape[0], -1, kv_heads, 2, HEAD_WIDTH)
    places = jnp.arange(cached.shape[1], dtype=jnp.int32)
    prefill_query = split_query[:PRE_DEV]
    prefill_fresh = fresh_kv[:PRE_DEV]
    cache_scores = (
        jnp.einsum(
            "ikgd,ckd->kgic", prefill_query, cached[0, :, :, 0], preferred_element_type=jnp.float32
        )
        * score_scale
    )
    cache_scores = jnp.where(places < lengths[0], cache_scores, -jnp.inf)
    block_scores = (
        jnp.einsum(
            "ikgd,jkd->kgij",
            prefill_query,
            prefill_fresh[:, :, 0],
            preferred_element_type=jnp.float32,
        )
        * score_scale
    )
    causal = jnp.arange(PRE_DEV)[:, None] >= jnp.arange(PRE_DEV)[None, :]
    block_scores = jnp.where(causal, block_scores, -jnp.inf)
    prefill_probs = softmax_rounded(jnp.concatenate([cache_scores, block_scores], axis=3))
    prefill_values = jnp.concatenate([cached[0, :, :, 1], prefill_fresh[:, :, 1]], axis=0)
    prefill_out = jnp.einsum(
        "kgic,ckd->ikgd", prefill_probs, prefill_values, preferred_element_type=jnp.float32
    )
    decode_query = split_query[PRE_DEV:]
    decode_fresh = fresh_kv[PRE_DEV:]
    decode_scores = (
        jnp.einsum(
            "rkgd,rckd->rkgc", decode_query, cached[1:, :, :, 0], preferred_element_type=jnp.float32
        )
        * score_scale
    )
    decode_scores = jnp.where(
        places[None, None, None, :] < lengths[1:, None, None, None], decode_scores, -jnp.inf
    )
    own_scores = (
        jnp.einsum(
            "rkgd,rkd->rkg", decode_query, decode_fresh[:, :, 0], preferred_element_type=jnp.float32
        )[..., None]
        * score_scale
    )
    decode_probs = softmax_rounded(jnp.concatenate([decode_scores, own_scores], axis=3))
    decode_values = jnp.concatenate([cached[1:, :, :, 1], decode_fresh[:, None, :, 1]], axis=1)
    decode_out = jnp.einsum(
        "rkgc,rckd->rkgd", decode_probs, decode_values, preferred_element_type=jnp.float32
    )
    joined = jnp.concatenate([prefill_out, decode_out], axis=0)
    return joined.reshape(tokens_here, -1).astype(jnp.bfloat16)


def slot_positions(block_owner, experts, capacity):
    flat_owner = block_owner.reshape(-1)
    onehot = (flat_owner[:, None] == jnp.arange(experts, dtype=jnp.int32)[None, :]).astype(
        jnp.int32
    )
    earlier = jnp.cumsum(onehot, axis=0) - onehot
    slot_index = jnp.sum(earlier * onehot, axis=1)
    return (flat_owner * capacity + slot_index).reshape(block_owner.shape)


def place_matrix(positions, slots_total):
    matches = positions[None, :, :] == jnp.arange(slots_total, dtype=jnp.int32)[:, None, None]
    return jnp.any(matches, axis=2).astype(jnp.bfloat16)


def local_sparse(
    queries,
    fresh_key_value,
    key_value_cache,
    request_page_index,
    cache_length_rows,
    residual,
    w_out,
    gain_in,
    route_ids,
    route_weights,
    expert_home,
    w_gate,
    w_up,
    w_down,
    gain_out,
):
    tp_size = lax.axis_size("tp")
    req_size = lax.axis_size("req")
    tp_index = lax.axis_index("tp")
    model_width = residual.shape[1]
    tokens_here = residual.shape[0]
    quarter = tokens_here // tp_size
    experts = expert_home.shape[0]
    capacity = min(quarter, max(2, 2 * quarter * TOPK // experts))
    context = group_attention(
        queries, fresh_key_value, key_value_cache, request_page_index, cache_length_rows
    )
    head_terms = jnp.dot(context, w_out, preferred_element_type=jnp.float32)
    state = residual.astype(jnp.float32) + lax.psum(head_terms, "tp")
    owners = jnp.sum(
        jnp.where(
            route_ids[:, :, None] == jnp.arange(experts, dtype=jnp.int32)[None, None, :],
            expert_home[None, None, :],
            0,
        ),
        axis=2,
    )
    shares = route_weights / jnp.sum(route_weights, axis=1, keepdims=True)
    own_start = tp_index * quarter
    own_state = lax.dynamic_slice_in_dim(state, own_start, quarter, 0)
    own_shares = lax.dynamic_slice_in_dim(shares, own_start, quarter, 0)
    normed_all = rms_scale(state, gain_in).astype(jnp.bfloat16)
    positions_all = jax.vmap(lambda block_owner: slot_positions(block_owner, experts, capacity))(
        owners.reshape(tp_size, quarter, TOPK)
    )
    placing = jax.vmap(lambda positions: place_matrix(positions, experts * capacity))(positions_all)
    outgoing = jnp.einsum(
        "qmi,qid->qmd",
        placing,
        normed_all.reshape(tp_size, quarter, model_width),
        preferred_element_type=jnp.float32,
    )
    outgoing = outgoing.astype(jnp.bfloat16).reshape(tp_size, experts, capacity, model_width)
    incoming = lax.all_to_all(outgoing, "req", split_axis=1, concat_axis=1, tiled=True)
    own_positions = lax.dynamic_index_in_dim(positions_all, tp_index, 0, keepdims=False)
    expert_rows = incoming.reshape(-1, model_width)
    gate_proj = jnp.dot(expert_rows, w_gate[0], preferred_element_type=jnp.float32)
    up_proj = jnp.dot(expert_rows, w_up[0], preferred_element_type=jnp.float32)
    inner_units = (jax.nn.silu(gate_proj) * up_proj).astype(jnp.bfloat16)
    summed = lax.psum_scatter(
        jnp.dot(inner_units, w_down[0], preferred_element_type=jnp.float32).astype(jnp.bfloat16),
        "tp",
        scatter_dimension=0,
        tiled=True,
    )
    results = summed.reshape(req_size, capacity, model_width)
    returned = lax.all_to_all(results, "req", split_axis=0, concat_axis=0, tiled=True).reshape(
        -1, model_width
    )
    picked = returned[own_positions]
    mixture = jnp.sum(own_shares[:, :, None] * picked.astype(jnp.float32), axis=1)
    return rms_scale(own_state + mixture, gain_out).astype(jnp.bfloat16)


ALL = ("req", "tp")
MASKED = -1e30
LANES = 128
MIB = 1024 * 1024
SMALL = pltpu.CompilerParams(vmem_limit_bytes=8 * MIB)


def vmem():
    return pl.BlockSpec(memory_space=pltpu.VMEM)


def smem():
    return pl.BlockSpec(memory_space=pltpu.SMEM)


def hbm():
    return pl.BlockSpec(memory_space=pltpu.HBM)


def stay(value):
    return pltpu.with_memory_space_constraint(value, pltpu.HBM)


def barrier(*values):
    return lax.optimization_barrier(values)


def multiplicity(page_rows, length, pool_pages, page_tokens):
    rows = page_rows[0].shape[0]
    lane = lax.broadcasted_iota(jnp.int32, (rows, page_tokens), 1)
    parts = []
    for page in range(pool_pages):
        count = jnp.zeros((rows, page_tokens), jnp.float32)
        for slot, named in enumerate(page_rows):
            hit = (named == page) & (lane + slot * page_tokens < length)
            count = count + jnp.where(hit, 1.0, 0.0)
        parts.append(count)
    return jnp.concatenate(parts, axis=1)


def pack_shares(ids, routed, home_ref):
    groups = home_ref.shape[0]
    choices, tokens = ids.shape
    spot = lax.broadcasted_iota(jnp.int32, (groups, tokens), 0)
    shares = routed / jnp.sum(routed, axis=0, keepdims=True)
    by_expert = jnp.zeros((groups, tokens), jnp.float32)
    for k in range(choices):
        by_expert = by_expert + jnp.where(spot == ids[k : k + 1, :], shares[k : k + 1, :], 0.0)
    by_home = jnp.zeros((groups, tokens), jnp.float32)
    for e in range(groups):
        by_home = by_home + jnp.where(spot == home_ref[e], by_expert[e : e + 1, :], 0.0)
    rounded = by_home.astype(jnp.bfloat16).astype(jnp.float32)
    tall = jnp.concatenate(
        [rounded, by_home - rounded, jnp.zeros((LANES - 2 * groups, tokens), jnp.float32)], axis=0
    )
    square = jnp.concatenate([tall, jnp.zeros((LANES, LANES - tokens), jnp.float32)], axis=1)
    return jnp.transpose(square)


def attention_kernel(
    pages_ref, lengths_ref, tp_ref, group_ref, home_ref, q_hbm, fresh_hbm, cache_hbm, residual_hbm, ids_hbm,
    routed_hbm, w_hbm, own_ref, send_ref, pack_ref,
    q_ref, fresh_ref, cache_ref, residual_ref, ids_ref, routed_ref, w_ref, context_ref, terms_ref,
    every_ref, sems,
):
    fetches = [
        pltpu.make_async_copy(source, target, sems.at[i])
        for i, (source, target) in enumerate(
            (
                (q_hbm, q_ref),
                (cache_hbm, cache_ref),
                (fresh_hbm, fresh_ref),
                (ids_hbm, ids_ref),
                (routed_hbm, routed_ref),
                (residual_hbm, residual_ref),
                (w_hbm, w_ref),
            )
        )
    ]
    for fetch in fetches:
        fetch.start()
    tokens = q_ref.shape[0]
    pool_pages, page_tokens, _ = cache_ref.shape
    slots, requests = pages_ref.shape
    kv_heads = fresh_ref.shape[1] // (2 * HEAD_WIDTH)
    group = q_ref.shape[1] // (HEAD_WIDTH * kv_heads)
    decodes = requests - 1
    row = lax.broadcasted_iota(jnp.int32, (decodes, page_tokens), 0)

    def by_row(read):
        value = jnp.zeros((decodes, page_tokens), jnp.int32)
        for j in range(decodes):
            value = jnp.where(row == j, read(j + 1), value)
        return value

    full = lambda scalar: jnp.full((decodes, page_tokens), scalar, jnp.int32)
    first = multiplicity(
        [full(pages_ref[s, 0]) for s in range(slots)], full(lengths_ref[0]), pool_pages, page_tokens
    )
    later = multiplicity(
        [by_row(lambda j, s=s: pages_ref[s, j]) for s in range(slots)],
        by_row(lambda j: lengths_ref[j]),
        pool_pages,
        page_tokens,
    )
    count = jnp.concatenate([first] * (PRE_DEV // decodes) + [later], axis=0)
    query_place = lax.broadcasted_iota(jnp.int32, (tokens, tokens), 0)
    key_place = lax.broadcasted_iota(jnp.int32, (tokens, tokens), 1)
    seen = (key_place == query_place) | ((key_place <= query_place) & (query_place < PRE_DEV))
    visible = jnp.concatenate([count] * group, axis=0)
    seen = jnp.concatenate([jnp.where(seen, 1.0, 0.0)] * group, axis=0)
    scale = HEAD_WIDTH**-0.5
    for fetch in fetches[:3]:
        fetch.wait()
    contract_last = (((1,), (1,)), ((), ()))
    for k in range(kv_heads):
        key_at, value_at = 2 * k * HEAD_WIDTH, (2 * k + 1) * HEAD_WIDTH
        query = jnp.concatenate(
            [
                q_ref[:, (k * group + g) * HEAD_WIDTH : (k * group + g + 1) * HEAD_WIDTH]
                for g in range(group)
            ],
            axis=0,
        )
        keys = cache_ref[:, :, key_at : key_at + HEAD_WIDTH].reshape(-1, HEAD_WIDTH)
        values = cache_ref[:, :, value_at : value_at + HEAD_WIDTH].reshape(-1, HEAD_WIDTH)
        old = lax.dot_general(query, keys, contract_last, preferred_element_type=jnp.float32)
        new = lax.dot_general(
            query,
            fresh_ref[:, key_at : key_at + HEAD_WIDTH],
            contract_last,
            preferred_element_type=jnp.float32,
        )
        old = jnp.where(visible > 0, old * scale, MASKED)
        new = jnp.where(seen > 0, new * scale, MASKED)
        peak = jnp.maximum(
            jnp.max(old, axis=1, keepdims=True), jnp.max(new, axis=1, keepdims=True)
        )
        old = jnp.exp(old - peak) * visible
        new = jnp.exp(new - peak) * seen
        inverse = 1.0 / (
            jnp.sum(old, axis=1, keepdims=True) + jnp.sum(new, axis=1, keepdims=True)
        )
        mixed = jnp.dot(
            (old * inverse).astype(jnp.bfloat16), values, preferred_element_type=jnp.float32
        ) + jnp.dot(
            (new * inverse).astype(jnp.bfloat16),
            fresh_ref[:, value_at : value_at + HEAD_WIDTH],
            preferred_element_type=jnp.float32,
        )
        mixed = mixed.astype(jnp.bfloat16)
        for g in range(group):
            h = k * group + g
            context_ref[:, h * HEAD_WIDTH : (h + 1) * HEAD_WIDTH] = mixed[
                g * tokens : (g + 1) * tokens
            ]
    half = tokens // 2
    width = terms_ref.shape[1]
    block = 512
    own_at = pl.multiple_of(tp_ref[0] * half, half)
    other_at = pl.multiple_of((1 - tp_ref[0]) * half, half)
    for fetch in fetches[3:5]:
        fetch.wait()
    every_ref[...] = pack_shares(ids_ref[...], routed_ref[...], home_ref)
    pack_ref[...] = every_ref[pl.ds(own_at, half), :].astype(jnp.bfloat16)
    for fetch in fetches[5:]:
        fetch.wait()
    for at in range(0, width, block):
        cols = slice(at, at + block)
        terms_ref[:, cols] = jnp.dot(
            context_ref[...], w_ref[:, cols], preferred_element_type=jnp.float32
        )
    own_ref[...] = terms_ref[pl.ds(own_at, half), :] + residual_ref[
        pl.ds(own_at, half), :
    ].astype(jnp.float32)
    send_ref[...] = terms_ref[pl.ds(other_at, half), :].astype(jnp.bfloat16)


def attention_terms(
    pages, lengths, tp_index, group, home, queries, fresh, cache, residual, ids, routed, w_out
):
    tokens, width = residual.shape
    half = tokens // 2
    moved = (queries, fresh, cache, residual, ids.T, routed.T, w_out)
    return pl.pallas_call(
        attention_kernel,
        out_shape=(
            jax.ShapeDtypeStruct((half, width), jnp.float32),
            jax.ShapeDtypeStruct((half, width), jnp.bfloat16),
            jax.ShapeDtypeStruct((half, LANES), jnp.bfloat16),
        ),
        in_specs=[smem()] * 5 + [hbm()] * 7,
        out_specs=(vmem(),) * 3,
        scratch_shapes=[pltpu.VMEM(v.shape, v.dtype) for v in moved]
        + [
            pltpu.VMEM(queries.shape, jnp.bfloat16),
            pltpu.VMEM((tokens, width), jnp.float32),
            pltpu.VMEM((LANES, LANES), jnp.float32),
            pltpu.SemaphoreType.DMA((7,)),
        ],
        compiler_params=pltpu.CompilerParams(vmem_limit_bytes=40 * MIB),
        name="attention_terms",
    )(stay(pages.T), stay(lengths), tp_index, group, stay(home), *[stay(v) for v in moved])


LATE = pl.CostEstimate(flops=3 * 10**10, bytes_accessed=1 << 20, transcendentals=0)


def norm_kernel(own_ref, got_ref, pack_ref, gain_ref, state_ref, far_ref, near_ref):
    state = own_ref[...] + got_ref[...].astype(jnp.float32)
    state_ref[...] = state
    normed = rms_scale(state, gain_ref[...]).astype(jnp.bfloat16)
    width = state.shape[1]
    far = far_ref.shape[0]
    far_ref[:, :width] = normed[:far]
    far_ref[:, width:] = pack_ref[:far, :]
    near_ref[:, :width] = normed[far:]
    near_ref[:, width:] = pack_ref[far:, :]


def norm_rows(own, got, pack, gain, far):
    rows, width = own.shape
    return pl.pallas_call(
        norm_kernel,
        out_shape=(
            jax.ShapeDtypeStruct((rows, width), jnp.float32),
            jax.ShapeDtypeStruct((far, width + LANES), jnp.bfloat16),
            jax.ShapeDtypeStruct((rows - far, width + LANES), jnp.bfloat16),
        ),
        in_specs=[vmem()] * 4,
        out_specs=(vmem(),) * 3,
        compiler_params=SMALL,
        name="norm_rows",
    )(own, got, pack, gain)


def join_kernel(starts, *refs):
    out_ref = refs[-1]
    at = 0
    for start, piece in zip(starts, refs[:-1]):
        height = piece.shape[0] - start
        out_ref[at : at + height, :] = piece[start:, :]
        at += height


def join_rows(pieces, starts, cost, name):
    height = sum(piece.shape[0] - start for piece, start in zip(pieces, starts))
    return pl.pallas_call(
        functools.partial(join_kernel, starts),
        out_shape=jax.ShapeDtypeStruct((height, pieces[0].shape[1]), jnp.bfloat16),
        in_specs=[vmem()] * len(pieces),
        out_specs=vmem(),
        compiler_params=SMALL,
        cost_estimate=cost,
        name=name,
    )(*pieces)


def hidden_units(groups, group_ref, x_ref, w0_ref, wg1_ref, wu1_ref, h_ref, ready):
    rows = x_ref.shape[0]
    width, hidden = wg1_ref.shape
    lane = lax.broadcasted_iota(jnp.int32, (rows, LANES), 1)
    packed = x_ref[:, width:].astype(jnp.float32)

    def product(w_ref):
        return jnp.dot(x_ref[:, :width], w_ref[...], preferred_element_type=jnp.float32)

    def store(e, gate, up):
        group = group_ref[0] ^ e
        share = jnp.sum(
            jnp.where((lane == group) | (lane == group + groups), packed, 0.0),
            axis=1,
            keepdims=True,
        )
        h_ref[:, e * hidden : (e + 1) * hidden] = (
            share * up * (gate / (1.0 + jnp.exp(-gate)))
        ).astype(jnp.bfloat16)

    store(1, product(wg1_ref), product(wu1_ref))
    ready()
    both = product(w0_ref)
    store(0, both[:, :hidden], both[:, hidden:])


DOWN_BLOCK = 512


def gather_pieces(pieces, x_ref):
    at = 0
    for piece in pieces:
        x_ref[at : at + piece.shape[0], :] = piece[...]
        at += piece.shape[0]
    if at < x_ref.shape[0]:
        x_ref[at:, :] = jnp.zeros((x_ref.shape[0] - at, x_ref.shape[1]), jnp.bfloat16)


def near_kernel(
    groups, group_ref, r0, r1, r2, r3, far_ref, wg1_ref, wu1_ref, wg0, wu0, wd0, wd1,
    out_ref, w0_ref, down_ref, x_ref, h_ref, sems,
):
    hidden = wg0.shape[1]
    fetches = [
        pltpu.make_async_copy(source, target, sems.at[i])
        for i, (source, target) in enumerate(
            (
                (wg0, w0_ref.at[:, :hidden]),
                (wu0, w0_ref.at[:, hidden:]),
                (wd0, down_ref.at[:hidden, :]),
                (wd1, down_ref.at[hidden:, :]),
            )
        )
    ]
    for fetch in fetches:
        fetch.start()
    gather_pieces((r0, r1, r2, r3, far_ref), x_ref)

    def ready():
        fetches[0].wait()
        fetches[1].wait()

    hidden_units(groups, group_ref, x_ref, w0_ref, wg1_ref, wu1_ref, h_ref, ready)
    fetches[2].wait()
    fetches[3].wait()
    height = out_ref.shape[0]
    for col in range(0, down_ref.shape[1], DOWN_BLOCK):
        cols = slice(col, col + DOWN_BLOCK)
        down = jnp.dot(h_ref[...], down_ref[:, cols], preferred_element_type=jnp.float32)
        out_ref[:, cols] = down[:height]


def expert_cost(rows, width, hidden):
    return pl.CostEstimate(
        flops=12 * rows * width * hidden,
        bytes_accessed=12 * width * hidden,
        transcendentals=2 * rows * hidden,
    )


def near_rows(groups, group, rows, far, weights, partner_weights):
    height = 4 * rows[0].shape[0] + far.shape[0]
    padded = -(-height // 16) * 16
    width, hidden = weights[0].shape
    wg0, wu0, wd0 = weights
    wg1, wu1, wd1 = partner_weights
    return pl.pallas_call(
        functools.partial(near_kernel, groups),
        out_shape=(
            jax.ShapeDtypeStruct((height, width), jnp.float32),
            jax.ShapeDtypeStruct((width, 2 * hidden), jnp.bfloat16),
            jax.ShapeDtypeStruct((2 * hidden, width), jnp.bfloat16),
        ),
        in_specs=[smem()] + [vmem()] * 7 + [hbm()] * 4,
        out_specs=(vmem(),) * 3,
        scratch_shapes=[
            pltpu.VMEM((padded, width + LANES), jnp.bfloat16),
            pltpu.VMEM((padded, 2 * hidden), jnp.bfloat16),
            pltpu.SemaphoreType.DMA((4,)),
        ],
        compiler_params=pltpu.CompilerParams(vmem_limit_bytes=24 * MIB),
        cost_estimate=expert_cost(height, width, hidden),
        name="near_rows",
    )(group, *rows, far, wg1, wu1, *[stay(w) for w in (wg0, wu0, wd0, wd1)])


def piece_kernel(groups, count, group_ref, *refs):
    pieces, (w0_ref, wg1_ref, wu1_ref, down_ref) = refs[:count], refs[count : count + 4]
    outs, (x_ref, h_ref) = refs[count + 4 : 2 * count + 4], refs[2 * count + 4 :]
    gather_pieces(pieces, x_ref)
    hidden_units(groups, group_ref, x_ref, w0_ref, wg1_ref, wu1_ref, h_ref, lambda: None)
    for col in range(0, down_ref.shape[1], DOWN_BLOCK):
        cols = slice(col, col + DOWN_BLOCK)
        down = jnp.dot(h_ref[...], down_ref[:, cols], preferred_element_type=jnp.float32)
        at = 0
        for out in outs:
            out[:, cols] = down[at : at + out.shape[0]].astype(jnp.bfloat16)
            at += out.shape[0]


def piece_rows(groups, group, pieces, w0, wg1, wu1, down):
    count = len(pieces)
    height = sum(piece.shape[0] for piece in pieces)
    padded = -(-height // 16) * 16
    width, hidden = wg1.shape
    return pl.pallas_call(
        functools.partial(piece_kernel, groups, count),
        out_shape=tuple(
            jax.ShapeDtypeStruct((piece.shape[0], width), jnp.bfloat16) for piece in pieces
        ),
        in_specs=[smem()] + [vmem()] * (count + 4),
        out_specs=(vmem(),) * count,
        scratch_shapes=[
            pltpu.VMEM((padded, width + LANES), jnp.bfloat16),
            pltpu.VMEM((padded, 2 * hidden), jnp.bfloat16),
        ],
        compiler_params=pltpu.CompilerParams(vmem_limit_bytes=24 * MIB),
        cost_estimate=expert_cost(height, width, hidden),
        name="piece_rows",
    )(group, *pieces, w0, wg1, wu1, down)


def plane_sum_kernel(near_ref, g1, g2, g3, m1, m2, m3):
    far = m1.shape[0]
    start = near_ref.shape[0] - 3 * far
    for j, out in enumerate((m1, m2, m3)):
        rows = slice(j * far, (j + 1) * far)
        total = near_ref[start + j * far : start + (j + 1) * far, :]
        for got in (g1, g2, g3):
            total = total + got[rows, :].astype(jnp.float32)
        out[...] = total.astype(jnp.bfloat16)


def plane_sum(near, got):
    far, width = got[0].shape[0] // 3, got[0].shape[1]
    return pl.pallas_call(
        plane_sum_kernel,
        out_shape=tuple(jax.ShapeDtypeStruct((far, width), jnp.bfloat16) for _ in range(3)),
        in_specs=[vmem()] * 4,
        out_specs=(vmem(),) * 3,
        compiler_params=SMALL,
        name="plane_sum",
    )(near, *got)


def first_sum_kernel(rows, near_ref, g1, out_ref):
    near = g1.shape[0] // 4
    for i in range(4):
        there = slice(i * near, (i + 1) * near)
        out_ref[there, :] = near_ref[(i + 1) * rows - near : (i + 1) * rows, :] + g1[
            there, :
        ].astype(jnp.float32)


def first_sum(near, got, rows):
    return pl.pallas_call(
        functools.partial(first_sum_kernel, rows),
        out_shape=jax.ShapeDtypeStruct(got.shape, jnp.float32),
        in_specs=[vmem()] * 2,
        out_specs=vmem(),
        compiler_params=SMALL,
        cost_estimate=LATE,
        name="first_sum",
    )(near, got)


def column_sum_kernel(near_ref, first_ref, g2, g3, own_ref, m1, m2, m3):
    rows = own_ref.shape[0]
    near = first_ref.shape[0] // 4
    far = rows - near
    for i, out in enumerate((own_ref, m1, m2, m3)):
        out[:far, :] = near_ref[i * rows : i * rows + far, :].astype(out.dtype)
        total = first_ref[i * near : (i + 1) * near, :]
        for got in (g2, g3):
            total = total + got[i * near : (i + 1) * near, :].astype(jnp.float32)
        out[far:, :] = total.astype(out.dtype)


def column_sum(near, first, got, rows):
    width = near.shape[1]
    kinds = (jnp.float32, jnp.bfloat16, jnp.bfloat16, jnp.bfloat16)
    return pl.pallas_call(
        column_sum_kernel,
        out_shape=tuple(jax.ShapeDtypeStruct((rows, width), kind) for kind in kinds),
        in_specs=[vmem()] * 4,
        out_specs=(vmem(),) * 4,
        compiler_params=SMALL,
        cost_estimate=LATE,
        name="column_sum",
    )(near, first, *got)


def total_kernel(state_ref, own_ref, z1, z2, z3, total_ref):
    total_ref[...] = state_ref[...] + own_ref[...]
    far = z1.shape[0]
    part = total_ref[:far, :]
    for got in (z1, z2, z3):
        part = part + got[...].astype(jnp.float32)
    total_ref[:far, :] = part


def total_rows(state, own, column):
    return pl.pallas_call(
        total_kernel,
        out_shape=jax.ShapeDtypeStruct(state.shape, jnp.float32),
        in_specs=[vmem()] * 5,
        out_specs=vmem(),
        compiler_params=SMALL,
        cost_estimate=LATE,
        name="total_rows",
    )(state, own, *column)


def final_kernel(total_ref, p1, p2, p3, gain_ref, out_ref):
    total = total_ref[...]
    for got in (p1, p2, p3):
        total = total + got[...].astype(jnp.float32)
    out_ref[...] = rms_scale(total, gain_ref[...]).astype(jnp.bfloat16)


def final_rows(total, plane, gain):
    return pl.pallas_call(
        final_kernel,
        out_shape=jax.ShapeDtypeStruct(total.shape, jnp.bfloat16),
        in_specs=[vmem()] * 5,
        out_specs=vmem(),
        compiler_params=SMALL,
        name="final_rows",
    )(total, *plane, gain)


def place(z, y, c, x):
    return ((z * 2 + y) * 2 + c) * 2 + x


def swap(value, dz, dy, dc, dx):
    pairs = [
        (place(z, y, c, x), place(z ^ dz, y ^ dy, c ^ dc, x ^ dx))
        for z in range(4)
        for y in range(2)
        for c in range(2)
        for x in range(2)
    ]
    return lax.ppermute(value, ALL, pairs)


PLANE = ((0, 0), (0, 1), (1, 0), (1, 1))


def swap_z(pieces):
    return tuple(swap(piece, d, 0, 0, 0) for d, piece in zip((1, 2, 3), pieces))


def swap_plane(pieces):
    return tuple(swap(piece, 0, dy, 0, dx) for (dy, dx), piece in zip(PLANE[1:], pieces))


def local_dense(
    queries, fresh_key_value, key_value_cache, request_page_index, cache_length_rows, residual,
    w_out, gain_in, route_ids, route_weights, expert_home, w_gate, w_up, w_down, gain_out,
):
    tp_index = lax.axis_index("tp")
    req_index = lax.axis_index("req")
    tokens, width = residual.shape
    half = tokens // 2
    far = half * 3 // 4
    groups = expert_home.shape[0]
    weights = (w_gate[0], w_up[0], w_down[0])
    partner_weights = tuple(swap(w, 0, 0, 1, 0) for w in weights)
    group = req_index.reshape(1)
    own_state, sent, pack = attention_terms(
        request_page_index, cache_length_rows, tp_index.reshape(1), group, expert_home,
        queries, fresh_key_value, key_value_cache, residual, route_ids, route_weights, w_out,
    )
    got, partner_weights = barrier(swap(sent, 0, 0, 0, 1), partner_weights)
    state, far_rows, last_rows = norm_rows(own_state, got, pack, gain_in[None, :], far)
    rows = join_rows((far_rows, last_rows), (0, 0), LATE, "own_rows")
    z_rows = swap_z((far_rows,) * 3)
    onward_plane = join_rows(z_rows, (0, 0, 0), LATE, "onward_plane")
    plane_rows, far_pieces = barrier(swap_plane((rows,) * 3), onward_plane)
    plane_rows = (rows,) + plane_rows
    onward_z = join_rows(plane_rows, (far,) * 4, None, "onward_z")
    z_pieces = swap_z((onward_z,) * 3)
    plane_pieces = swap_plane((onward_plane,) * 3)
    near, w0, down = near_rows(groups, group, plane_rows, far_pieces, weights, partner_weights)
    parts = piece_rows(groups, group, z_pieces + plane_pieces, w0, *partner_weights[:2], down)
    z_parts, plane_parts = swap_z(parts[:3]), swap_plane(parts[3:])
    first = first_sum(near, z_parts[0], half)
    plane_parts, first = barrier(plane_parts, first)
    far_sums = plane_sum(near, plane_parts)
    last_parts, far_sums = barrier(z_parts[1:], far_sums)
    own, *near_sums = column_sum(near, first, last_parts, half)
    total = total_rows(state, own, swap_z(far_sums))
    last_plane, total = barrier(swap_plane(near_sums), total)
    return final_rows(total, last_plane, gain_out[None, :])


def solution(mesh):
    dense = mesh.shape["req"] == 16 and mesh.shape["tp"] == 2
    return jax.shard_map(
        local_dense if dense else local_sparse,
        mesh=mesh,
        in_specs=(
            P("req", "tp"),
            P("req", "tp"),
            P("req", None, "tp"),
            P("req", None),
            P("req"),
            P("req", None),
            P("tp", None),
            P(),
            P("req", None),
            P("req", None),
            P(),
            P("req", None, "tp"),
            P("req", None, "tp"),
            P("req", "tp", None),
            P(),
        ),
        out_specs=P(("req", "tp"), None),
        check_vma=False,
    )
```

```python
import functools

import jax
import jax.numpy as jnp
from jax import lax
from jax.experimental import pallas as pl
from jax.experimental.pallas import tpu as pltpu
from jax.sharding import PartitionSpec as P

HEAD_WIDTH = 128
TOPK = 8
PRE_DEV = 56


EPSILON = 1e-06


def rms_scale(value_rows, gain_row):
    mean_square = jnp.mean(value_rows * value_rows, axis=-1, keepdims=True)
    return value_rows * lax.rsqrt(mean_square + EPSILON) * gain_row


def softmax_rounded(scores):
    row_peak = jnp.max(scores, axis=-1, keepdims=True)
    weights = jnp.exp(scores - row_peak)
    return (weights / jnp.sum(weights, axis=-1, keepdims=True)).astype(jnp.bfloat16)


def group_attention(queries, fresh_key_value, page_pool, page_rows, lengths):
    tokens_here = queries.shape[0]
    kv_heads = fresh_key_value.shape[1] // (2 * HEAD_WIDTH)
    group_size = queries.shape[1] // (HEAD_WIDTH * kv_heads)
    score_scale = HEAD_WIDTH ** (-0.5)
    split_query = queries.reshape(tokens_here, kv_heads, group_size, HEAD_WIDTH)
    fresh_kv = fresh_key_value.reshape(tokens_here, kv_heads, 2, HEAD_WIDTH)
    gathered_pages = page_pool[page_rows]
    cached = gathered_pages.reshape(page_rows.shape[0], -1, kv_heads, 2, HEAD_WIDTH)
    places = jnp.arange(cached.shape[1], dtype=jnp.int32)
    prefill_query = split_query[:PRE_DEV]
    prefill_fresh = fresh_kv[:PRE_DEV]
    cache_scores = (
        jnp.einsum(
            "ikgd,ckd->kgic", prefill_query, cached[0, :, :, 0], preferred_element_type=jnp.float32
        )
        * score_scale
    )
    cache_scores = jnp.where(places < lengths[0], cache_scores, -jnp.inf)
    block_scores = (
        jnp.einsum(
            "ikgd,jkd->kgij",
            prefill_query,
            prefill_fresh[:, :, 0],
            preferred_element_type=jnp.float32,
        )
        * score_scale
    )
    causal = jnp.arange(PRE_DEV)[:, None] >= jnp.arange(PRE_DEV)[None, :]
    block_scores = jnp.where(causal, block_scores, -jnp.inf)
    prefill_probs = softmax_rounded(jnp.concatenate([cache_scores, block_scores], axis=3))
    prefill_values = jnp.concatenate([cached[0, :, :, 1], prefill_fresh[:, :, 1]], axis=0)
    prefill_out = jnp.einsum(
        "kgic,ckd->ikgd", prefill_probs, prefill_values, preferred_element_type=jnp.float32
    )
    decode_query = split_query[PRE_DEV:]
    decode_fresh = fresh_kv[PRE_DEV:]
    decode_scores = (
        jnp.einsum(
            "rkgd,rckd->rkgc", decode_query, cached[1:, :, :, 0], preferred_element_type=jnp.float32
        )
        * score_scale
    )
    decode_scores = jnp.where(
        places[None, None, None, :] < lengths[1:, None, None, None], decode_scores, -jnp.inf
    )
    own_scores = (
        jnp.einsum(
            "rkgd,rkd->rkg", decode_query, decode_fresh[:, :, 0], preferred_element_type=jnp.float32
        )[..., None]
        * score_scale
    )
    decode_probs = softmax_rounded(jnp.concatenate([decode_scores, own_scores], axis=3))
    decode_values = jnp.concatenate([cached[1:, :, :, 1], decode_fresh[:, None, :, 1]], axis=1)
    decode_out = jnp.einsum(
        "rkgc,rckd->rkgd", decode_probs, decode_values, preferred_element_type=jnp.float32
    )
    joined = jnp.concatenate([prefill_out, decode_out], axis=0)
    return joined.reshape(tokens_here, -1).astype(jnp.bfloat16)


def slot_positions(block_owner, experts, capacity):
    flat_owner = block_owner.reshape(-1)
    onehot = (flat_owner[:, None] == jnp.arange(experts, dtype=jnp.int32)[None, :]).astype(
        jnp.int32
    )
    earlier = jnp.cumsum(onehot, axis=0) - onehot
    slot_index = jnp.sum(earlier * onehot, axis=1)
    return (flat_owner * capacity + slot_index).reshape(block_owner.shape)


def place_matrix(positions, slots_total):
    matches = positions[None, :, :] == jnp.arange(slots_total, dtype=jnp.int32)[:, None, None]
    return jnp.any(matches, axis=2).astype(jnp.bfloat16)


def local_sparse(
    queries,
    fresh_key_value,
    key_value_cache,
    request_page_index,
    cache_length_rows,
    residual,
    w_out,
    gain_in,
    route_ids,
    route_weights,
    expert_home,
    w_gate,
    w_up,
    w_down,
    gain_out,
):
    tp_size = lax.axis_size("tp")
    req_size = lax.axis_size("req")
    tp_index = lax.axis_index("tp")
    model_width = residual.shape[1]
    tokens_here = residual.shape[0]
    quarter = tokens_here // tp_size
    experts = expert_home.shape[0]
    capacity = min(quarter, max(2, 2 * quarter * TOPK // experts))
    context = group_attention(
        queries, fresh_key_value, key_value_cache, request_page_index, cache_length_rows
    )
    head_terms = jnp.dot(context, w_out, preferred_element_type=jnp.float32)
    state = residual.astype(jnp.float32) + lax.psum(head_terms, "tp")
    owners = jnp.sum(
        jnp.where(
            route_ids[:, :, None] == jnp.arange(experts, dtype=jnp.int32)[None, None, :],
            expert_home[None, None, :],
            0,
        ),
        axis=2,
    )
    shares = route_weights / jnp.sum(route_weights, axis=1, keepdims=True)
    own_start = tp_index * quarter
    own_state = lax.dynamic_slice_in_dim(state, own_start, quarter, 0)
    own_shares = lax.dynamic_slice_in_dim(shares, own_start, quarter, 0)
    normed_all = rms_scale(state, gain_in).astype(jnp.bfloat16)
    positions_all = jax.vmap(lambda block_owner: slot_positions(block_owner, experts, capacity))(
        owners.reshape(tp_size, quarter, TOPK)
    )
    placing = jax.vmap(lambda positions: place_matrix(positions, experts * capacity))(positions_all)
    outgoing = jnp.einsum(
        "qmi,qid->qmd",
        placing,
        normed_all.reshape(tp_size, quarter, model_width),
        preferred_element_type=jnp.float32,
    )
    outgoing = outgoing.astype(jnp.bfloat16).reshape(tp_size, experts, capacity, model_width)
    incoming = lax.all_to_all(outgoing, "req", split_axis=1, concat_axis=1, tiled=True)
    own_positions = lax.dynamic_index_in_dim(positions_all, tp_index, 0, keepdims=False)
    expert_rows = incoming.reshape(-1, model_width)
    gate_proj = jnp.dot(expert_rows, w_gate[0], preferred_element_type=jnp.float32)
    up_proj = jnp.dot(expert_rows, w_up[0], preferred_element_type=jnp.float32)
    inner_units = (jax.nn.silu(gate_proj) * up_proj).astype(jnp.bfloat16)
    summed = lax.psum_scatter(
        jnp.dot(inner_units, w_down[0], preferred_element_type=jnp.float32).astype(jnp.bfloat16),
        "tp",
        scatter_dimension=0,
        tiled=True,
    )
    results = summed.reshape(req_size, capacity, model_width)
    returned = lax.all_to_all(results, "req", split_axis=0, concat_axis=0, tiled=True).reshape(
        -1, model_width
    )
    picked = returned[own_positions]
    mixture = jnp.sum(own_shares[:, :, None] * picked.astype(jnp.float32), axis=1)
    return rms_scale(own_state + mixture, gain_out).astype(jnp.bfloat16)


ALL = ("req", "tp")
MASKED = -1e30
LANES = 128
MIB = 1024 * 1024
SMALL = pltpu.CompilerParams(vmem_limit_bytes=8 * MIB)


def vmem():
    return pl.BlockSpec(memory_space=pltpu.VMEM)


def smem():
    return pl.BlockSpec(memory_space=pltpu.SMEM)


def hbm():
    return pl.BlockSpec(memory_space=pltpu.HBM)


def stay(value):
    return pltpu.with_memory_space_constraint(value, pltpu.HBM)


def barrier(*values):
    return lax.optimization_barrier(values)


def multiplicity(page_rows, length, pool_pages, page_tokens):
    rows = page_rows[0].shape[0]
    lane = lax.broadcasted_iota(jnp.int32, (rows, page_tokens), 1)
    parts = []
    for page in range(pool_pages):
        count = jnp.zeros((rows, page_tokens), jnp.float32)
        for slot, named in enumerate(page_rows):
            hit = (named == page) & (lane + slot * page_tokens < length)
            count = count + jnp.where(hit, 1.0, 0.0)
        parts.append(count)
    return jnp.concatenate(parts, axis=1)


def pack_shares(ids, routed, home_ref):
    groups = home_ref.shape[0]
    choices, tokens = ids.shape
    spot = lax.broadcasted_iota(jnp.int32, (groups, tokens), 0)
    shares = routed / jnp.sum(routed, axis=0, keepdims=True)
    by_expert = jnp.zeros((groups, tokens), jnp.float32)
    for k in range(choices):
        by_expert = by_expert + jnp.where(spot == ids[k : k + 1, :], shares[k : k + 1, :], 0.0)
    by_home = jnp.zeros((groups, tokens), jnp.float32)
    for e in range(groups):
        by_home = by_home + jnp.where(spot == home_ref[e], by_expert[e : e + 1, :], 0.0)
    rounded = by_home.astype(jnp.bfloat16).astype(jnp.float32)
    tall = jnp.concatenate(
        [rounded, by_home - rounded, jnp.zeros((LANES - 2 * groups, tokens), jnp.float32)], axis=0
    )
    square = jnp.concatenate([tall, jnp.zeros((LANES, LANES - tokens), jnp.float32)], axis=1)
    return jnp.transpose(square)


def count_positions(pages_ref, lengths_ref, pool_pages, page_tokens, count_ref):
    slots, requests = pages_ref.shape
    decodes = requests - 1
    row = lax.broadcasted_iota(jnp.int32, (decodes, page_tokens), 0)

    def by_row(read):
        value = jnp.zeros((decodes, page_tokens), jnp.int32)
        for j in range(decodes):
            value = jnp.where(row == j, read(j + 1), value)
        return value

    full = lambda scalar: jnp.full((decodes, page_tokens), scalar, jnp.int32)
    first = multiplicity(
        [full(pages_ref[s, 0]) for s in range(slots)], full(lengths_ref[0]), pool_pages, page_tokens
    )
    later = multiplicity(
        [by_row(lambda j, s=s: pages_ref[s, j]) for s in range(slots)],
        by_row(lambda j: lengths_ref[j]),
        pool_pages,
        page_tokens,
    )
    count_ref[...] = jnp.concatenate([first] * (PRE_DEV // decodes) + [later], axis=0)


def attend(start, q_ref, fresh_ref, cache_ref, count_ref, context_ref):
    rows = context_ref.shape[0]
    tokens = q_ref.shape[0]
    kv_heads = fresh_ref.shape[1] // (2 * HEAD_WIDTH)
    group = q_ref.shape[1] // (HEAD_WIDTH * kv_heads)
    query_place = start + lax.broadcasted_iota(jnp.int32, (rows, tokens), 0)
    key_place = lax.broadcasted_iota(jnp.int32, (rows, tokens), 1)
    seen = (key_place == query_place) | ((key_place <= query_place) & (query_place < PRE_DEV))
    seen = jnp.concatenate([jnp.where(seen, 1.0, 0.0)] * group, axis=0)
    visible = jnp.concatenate([count_ref[pl.ds(start, rows), :]] * group, axis=0)
    scale = HEAD_WIDTH**-0.5
    contract_last = (((1,), (1,)), ((), ()))
    for k in range(kv_heads):
        key_at, value_at = 2 * k * HEAD_WIDTH, (2 * k + 1) * HEAD_WIDTH
        heads = [k * group + g for g in range(group)]
        query = jnp.concatenate(
            [q_ref[pl.ds(start, rows), h * HEAD_WIDTH : (h + 1) * HEAD_WIDTH] for h in heads],
            axis=0,
        )
        keys = cache_ref[:, :, key_at : key_at + HEAD_WIDTH].reshape(-1, HEAD_WIDTH)
        values = cache_ref[:, :, value_at : value_at + HEAD_WIDTH].reshape(-1, HEAD_WIDTH)
        old = lax.dot_general(query, keys, contract_last, preferred_element_type=jnp.float32)
        new = lax.dot_general(
            query,
            fresh_ref[:, key_at : key_at + HEAD_WIDTH],
            contract_last,
            preferred_element_type=jnp.float32,
        )
        old = jnp.where(visible > 0, old * scale, MASKED)
        new = jnp.where(seen > 0, new * scale, MASKED)
        peak = jnp.maximum(
            jnp.max(old, axis=1, keepdims=True), jnp.max(new, axis=1, keepdims=True)
        )
        old = jnp.exp(old - peak) * visible
        new = jnp.exp(new - peak) * seen
        inverse = 1.0 / (
            jnp.sum(old, axis=1, keepdims=True) + jnp.sum(new, axis=1, keepdims=True)
        )
        mixed = jnp.dot(
            (old * inverse).astype(jnp.bfloat16), values, preferred_element_type=jnp.float32
        ) + jnp.dot(
            (new * inverse).astype(jnp.bfloat16),
            fresh_ref[:, value_at : value_at + HEAD_WIDTH],
            preferred_element_type=jnp.float32,
        )
        mixed = mixed.astype(jnp.bfloat16)
        for g, h in enumerate(heads):
            context_ref[:, h * HEAD_WIDTH : (h + 1) * HEAD_WIDTH] = mixed[g * rows : (g + 1) * rows]


OUT_BLOCK = 512
W_PIECES = 4


def other_kernel(
    pages_ref, lengths_ref, tp_ref, group_ref, q_hbm, fresh_hbm, cache_hbm, w_hbm,
    send_ref, q_ref, fresh_ref, cache_ref, w_ref, count_ref, context_ref, terms_ref, sems,
):
    moves = [(q_hbm, q_ref), (fresh_hbm, fresh_ref), (cache_hbm, cache_ref)]
    depth = w_ref.shape[0] // W_PIECES
    parts = [slice(i * depth, (i + 1) * depth) for i in range(W_PIECES)]
    moves += [(w_hbm.at[part, :], w_ref.at[part, :]) for part in parts]
    fetches = [
        pltpu.make_async_copy(source, target, sems.at[i])
        for i, (source, target) in enumerate(moves)
    ]
    for fetch in fetches:
        fetch.start()
    half = context_ref.shape[0]
    start = pl.multiple_of((1 - tp_ref[0]) * half, half)
    count_positions(pages_ref, lengths_ref, cache_ref.shape[0], cache_ref.shape[1], count_ref)
    for fetch in fetches[:3]:
        fetch.wait()
    attend(start, q_ref, fresh_ref, cache_ref, count_ref, context_ref)
    for i, part in enumerate(parts):
        fetches[3 + i].wait()
        for at in range(0, w_ref.shape[1], OUT_BLOCK):
            cols = slice(at, at + OUT_BLOCK)
            terms = jnp.dot(
                context_ref[:, part], w_ref[part, cols], preferred_element_type=jnp.float32
            )
            terms_ref[:, cols] = terms if i == 0 else terms_ref[:, cols] + terms
    send_ref[...] = terms_ref[...].astype(jnp.bfloat16)


def other_terms(pages, lengths, tp_index, group, queries, fresh, cache, w_out):
    half = queries.shape[0] // 2
    moved = (queries, fresh, cache, w_out)
    return pl.pallas_call(
        other_kernel,
        out_shape=(jax.ShapeDtypeStruct((half, w_out.shape[1]), jnp.bfloat16),)
        + tuple(jax.ShapeDtypeStruct(v.shape, v.dtype) for v in moved),
        in_specs=[smem()] * 4 + [hbm()] * 4,
        out_specs=(vmem(),) * 5,
        scratch_shapes=[
            pltpu.VMEM((queries.shape[0], cache.shape[0] * cache.shape[1]), jnp.float32),
            pltpu.VMEM((half, queries.shape[1]), jnp.bfloat16),
            pltpu.VMEM((half, w_out.shape[1]), jnp.float32),
            pltpu.SemaphoreType.DMA((3 + W_PIECES,)),
        ],
        compiler_params=pltpu.CompilerParams(vmem_limit_bytes=16 * MIB),
        name="other_terms",
    )(stay(pages), stay(lengths), tp_index, group, *[stay(v) for v in moved])


def own_kernel(
    pages_ref, lengths_ref, tp_ref, home_ref, q_ref, fresh_ref, cache_ref, w_ref,
    residual_hbm, ids_hbm, routed_hbm,
    own_ref, pack_ref, residual_ref, ids_ref, routed_ref, count_ref, context_ref, every_ref, sems,
):
    moves = ((ids_hbm, ids_ref), (routed_hbm, routed_ref), (residual_hbm, residual_ref))
    fetches = [
        pltpu.make_async_copy(source, target, sems.at[i])
        for i, (source, target) in enumerate(moves)
    ]
    for fetch in fetches:
        fetch.start()
    half = context_ref.shape[0]
    start = pl.multiple_of(tp_ref[0] * half, half)
    count_positions(pages_ref, lengths_ref, cache_ref.shape[0], cache_ref.shape[1], count_ref)
    attend(start, q_ref, fresh_ref, cache_ref, count_ref, context_ref)
    for fetch in fetches:
        fetch.wait()
    every_ref[...] = pack_shares(ids_ref[...], routed_ref[...], home_ref)
    pack_ref[...] = every_ref[pl.ds(start, half), :].astype(jnp.bfloat16)
    for at in range(0, w_ref.shape[1], OUT_BLOCK):
        cols = slice(at, at + OUT_BLOCK)
        own_ref[:, cols] = residual_ref[pl.ds(start, half), cols].astype(jnp.float32) + jnp.dot(
            context_ref[...], w_ref[:, cols], preferred_element_type=jnp.float32
        )


def own_terms(pages, lengths, tp_index, home, kept, residual, ids, routed):
    tokens, width = residual.shape
    half = tokens // 2
    queries, _, cache, _ = kept
    moved = (residual, ids, routed)
    return pl.pallas_call(
        own_kernel,
        out_shape=(
            jax.ShapeDtypeStruct((half, width), jnp.float32),
            jax.ShapeDtypeStruct((half, LANES), jnp.bfloat16),
        ),
        in_specs=[smem()] * 4 + [vmem()] * 4 + [hbm()] * 3,
        out_specs=(vmem(),) * 2,
        scratch_shapes=[pltpu.VMEM(v.shape, v.dtype) for v in moved]
        + [
            pltpu.VMEM((tokens, cache.shape[0] * cache.shape[1]), jnp.float32),
            pltpu.VMEM((half, queries.shape[1]), jnp.bfloat16),
            pltpu.VMEM((LANES, LANES), jnp.float32),
            pltpu.SemaphoreType.DMA((3,)),
        ],
        compiler_params=pltpu.CompilerParams(vmem_limit_bytes=16 * MIB),
        name="own_terms",
    )(stay(pages), stay(lengths), tp_index, stay(home), *kept, *[stay(v) for v in moved])


LATE = pl.CostEstimate(flops=3 * 10**10, bytes_accessed=1 << 20, transcendentals=0)


def norm_kernel(own_ref, got_ref, pack_ref, gain_ref, state_ref, far_ref, near_ref):
    state = own_ref[...] + got_ref[...].astype(jnp.float32)
    state_ref[...] = state
    normed = rms_scale(state, gain_ref[...]).astype(jnp.bfloat16)
    width = state.shape[1]
    far = far_ref.shape[0]
    far_ref[:, :width] = normed[:far]
    far_ref[:, width:] = pack_ref[:far, :]
    near_ref[:, :width] = normed[far:]
    near_ref[:, width:] = pack_ref[far:, :]


def norm_rows(own, got, pack, gain, far):
    rows, width = own.shape
    return pl.pallas_call(
        norm_kernel,
        out_shape=(
            jax.ShapeDtypeStruct((rows, width), jnp.float32),
            jax.ShapeDtypeStruct((far, width + LANES), jnp.bfloat16),
            jax.ShapeDtypeStruct((rows - far, width + LANES), jnp.bfloat16),
        ),
        in_specs=[vmem()] * 4,
        out_specs=(vmem(),) * 3,
        compiler_params=SMALL,
        name="norm_rows",
    )(own, got, pack, gain)


def join_kernel(starts, *refs):
    out_ref = refs[-1]
    at = 0
    for start, piece in zip(starts, refs[:-1]):
        height = piece.shape[0] - start
        out_ref[at : at + height, :] = piece[start:, :]
        at += height


def join_rows(pieces, starts, cost, name):
    height = sum(piece.shape[0] - start for piece, start in zip(pieces, starts))
    return pl.pallas_call(
        functools.partial(join_kernel, starts),
        out_shape=jax.ShapeDtypeStruct((height, pieces[0].shape[1]), jnp.bfloat16),
        in_specs=[vmem()] * len(pieces),
        out_specs=vmem(),
        compiler_params=SMALL,
        cost_estimate=cost,
        name=name,
    )(*pieces)


def hidden_units(groups, group_ref, x_ref, w_refs, h_ref, ready):
    rows = x_ref.shape[0]
    width = w_refs[0].shape[0]
    hidden = h_ref.shape[1] // 2
    lane = lax.broadcasted_iota(jnp.int32, (rows, LANES), 1)
    packed = x_ref[:, width:].astype(jnp.float32)
    for e in (1, 0):
        group = group_ref[0] ^ e
        share = jnp.sum(
            jnp.where((lane == group) | (lane == group + groups), packed, 0.0),
            axis=1,
            keepdims=True,
        )
        ready(e)
        both = jnp.dot(x_ref[:, :width], w_refs[e][...], preferred_element_type=jnp.float32)
        gate, up = both[:, :hidden], both[:, hidden:]
        h_ref[:, e * hidden : (e + 1) * hidden] = (
            share * up * (gate / (1.0 + jnp.exp(-gate)))
        ).astype(jnp.bfloat16)


DOWN_BLOCK = 512


def gather_pieces(pieces, x_ref):
    at = 0
    for piece in pieces:
        x_ref[at : at + piece.shape[0], :] = piece[...]
        at += piece.shape[0]
    if at < x_ref.shape[0]:
        x_ref[at:, :] = jnp.zeros((x_ref.shape[0] - at, x_ref.shape[1]), jnp.bfloat16)


def near_kernel(
    groups, group_ref, r0, r1, r2, r3, far_ref, wg1, wu1, wg0, wu0, wd0, wd1,
    out_ref, w0_ref, w1_ref, down_ref, x_ref, h_ref, sems,
):
    hidden = wg0.shape[1]
    fetches = [
        pltpu.make_async_copy(source, target, sems.at[i])
        for i, (source, target) in enumerate(
            (
                (wg0, w0_ref.at[:, :hidden]),
                (wu0, w0_ref.at[:, hidden:]),
                (wd0, down_ref.at[:hidden, :]),
                (wd1, down_ref.at[hidden:, :]),
                (wg1, w1_ref.at[:, :hidden]),
                (wu1, w1_ref.at[:, hidden:]),
            )
        )
    ]
    for fetch in fetches:
        fetch.start()
    gather_pieces((r0, r1, r2, r3, far_ref), x_ref)

    def ready(e):
        for fetch in fetches[4:] if e else fetches[:2]:
            fetch.wait()

    hidden_units(groups, group_ref, x_ref, (w0_ref, w1_ref), h_ref, ready)
    fetches[2].wait()
    fetches[3].wait()
    height = out_ref.shape[0]
    for col in range(0, down_ref.shape[1], DOWN_BLOCK):
        cols = slice(col, col + DOWN_BLOCK)
        down = jnp.dot(h_ref[...], down_ref[:, cols], preferred_element_type=jnp.float32)
        out_ref[:, cols] = down[:height]


def expert_cost(rows, width, hidden):
    return pl.CostEstimate(
        flops=12 * rows * width * hidden,
        bytes_accessed=12 * width * hidden,
        transcendentals=2 * rows * hidden,
    )


def near_rows(groups, group, rows, far, weights, partner_weights):
    height = 4 * rows[0].shape[0] + far.shape[0]
    padded = -(-height // 16) * 16
    width, hidden = weights[0].shape
    wg0, wu0, wd0 = weights
    wg1, wu1, wd1 = partner_weights
    return pl.pallas_call(
        functools.partial(near_kernel, groups),
        out_shape=(
            jax.ShapeDtypeStruct((height, width), jnp.float32),
            jax.ShapeDtypeStruct((width, 2 * hidden), jnp.bfloat16),
            jax.ShapeDtypeStruct((width, 2 * hidden), jnp.bfloat16),
            jax.ShapeDtypeStruct((2 * hidden, width), jnp.bfloat16),
        ),
        in_specs=[smem()] + [vmem()] * 7 + [hbm()] * 4,
        out_specs=(vmem(),) * 4,
        scratch_shapes=[
            pltpu.VMEM((padded, width + LANES), jnp.bfloat16),
            pltpu.VMEM((padded, 2 * hidden), jnp.bfloat16),
            pltpu.SemaphoreType.DMA((6,)),
        ],
        compiler_params=pltpu.CompilerParams(vmem_limit_bytes=24 * MIB),
        cost_estimate=expert_cost(height, width, hidden),
        name="near_rows",
    )(group, *rows, far, wg1, wu1, *[stay(w) for w in (wg0, wu0, wd0, wd1)])


def piece_kernel(groups, count, group_ref, *refs):
    pieces, (w0_ref, w1_ref, down_ref) = refs[:count], refs[count : count + 3]
    outs, (x_ref, h_ref) = refs[count + 3 : 2 * count + 3], refs[2 * count + 3 :]
    gather_pieces(pieces, x_ref)
    hidden_units(groups, group_ref, x_ref, (w0_ref, w1_ref), h_ref, lambda e: None)
    for col in range(0, down_ref.shape[1], DOWN_BLOCK):
        cols = slice(col, col + DOWN_BLOCK)
        down = jnp.dot(h_ref[...], down_ref[:, cols], preferred_element_type=jnp.float32)
        at = 0
        for out in outs:
            out[:, cols] = down[at : at + out.shape[0]].astype(jnp.bfloat16)
            at += out.shape[0]


def piece_rows(groups, group, pieces, w0, w1, down):
    count = len(pieces)
    height = sum(piece.shape[0] for piece in pieces)
    padded = -(-height // 16) * 16
    width, hidden = w1.shape[0], w1.shape[1] // 2
    return pl.pallas_call(
        functools.partial(piece_kernel, groups, count),
        out_shape=tuple(
            jax.ShapeDtypeStruct((piece.shape[0], width), jnp.bfloat16) for piece in pieces
        ),
        in_specs=[smem()] + [vmem()] * (count + 3),
        out_specs=(vmem(),) * count,
        scratch_shapes=[
            pltpu.VMEM((padded, width + LANES), jnp.bfloat16),
            pltpu.VMEM((padded, 2 * hidden), jnp.bfloat16),
        ],
        compiler_params=pltpu.CompilerParams(vmem_limit_bytes=24 * MIB),
        cost_estimate=expert_cost(height, width, hidden),
        name="piece_rows",
    )(group, *pieces, w0, w1, down)


def plane_sum_kernel(near_ref, g1, g2, g3, m1, m2, m3):
    far = m1.shape[0]
    start = near_ref.shape[0] - 3 * far
    for j, out in enumerate((m1, m2, m3)):
        rows = slice(j * far, (j + 1) * far)
        total = near_ref[start + j * far : start + (j + 1) * far, :]
        for got in (g1, g2, g3):
            total = total + got[rows, :].astype(jnp.float32)
        out[...] = total.astype(jnp.bfloat16)


def plane_sum(near, got):
    far, width = got[0].shape[0] // 3, got[0].shape[1]
    return pl.pallas_call(
        plane_sum_kernel,
        out_shape=tuple(jax.ShapeDtypeStruct((far, width), jnp.bfloat16) for _ in range(3)),
        in_specs=[vmem()] * 4,
        out_specs=(vmem(),) * 3,
        compiler_params=SMALL,
        name="plane_sum",
    )(near, *got)


def first_sum_kernel(rows, near_ref, g1, out_ref):
    near = g1.shape[0] // 4
    for i in range(4):
        there = slice(i * near, (i + 1) * near)
        out_ref[there, :] = near_ref[(i + 1) * rows - near : (i + 1) * rows, :] + g1[
            there, :
        ].astype(jnp.float32)


def first_sum(near, got, rows):
    return pl.pallas_call(
        functools.partial(first_sum_kernel, rows),
        out_shape=jax.ShapeDtypeStruct(got.shape, jnp.float32),
        in_specs=[vmem()] * 2,
        out_specs=vmem(),
        compiler_params=SMALL,
        cost_estimate=LATE,
        name="first_sum",
    )(near, got)


def column_sum_kernel(near_ref, first_ref, g2, g3, own_ref, m1, m2, m3):
    rows = own_ref.shape[0]
    near = first_ref.shape[0] // 4
    far = rows - near
    for i, out in enumerate((own_ref, m1, m2, m3)):
        out[:far, :] = near_ref[i * rows : i * rows + far, :].astype(out.dtype)
        total = first_ref[i * near : (i + 1) * near, :]
        for got in (g2, g3):
            total = total + got[i * near : (i + 1) * near, :].astype(jnp.float32)
        out[far:, :] = total.astype(out.dtype)


def column_sum(near, first, got, rows):
    width = near.shape[1]
    kinds = (jnp.float32, jnp.bfloat16, jnp.bfloat16, jnp.bfloat16)
    return pl.pallas_call(
        column_sum_kernel,
        out_shape=tuple(jax.ShapeDtypeStruct((rows, width), kind) for kind in kinds),
        in_specs=[vmem()] * 4,
        out_specs=(vmem(),) * 4,
        compiler_params=SMALL,
        cost_estimate=LATE,
        name="column_sum",
    )(near, first, *got)


def total_kernel(state_ref, own_ref, z1, z2, z3, total_ref):
    total_ref[...] = state_ref[...] + own_ref[...]
    far = z1.shape[0]
    part = total_ref[:far, :]
    for got in (z1, z2, z3):
        part = part + got[...].astype(jnp.float32)
    total_ref[:far, :] = part


def total_rows(state, own, column):
    return pl.pallas_call(
        total_kernel,
        out_shape=jax.ShapeDtypeStruct(state.shape, jnp.float32),
        in_specs=[vmem()] * 5,
        out_specs=vmem(),
        compiler_params=SMALL,
        cost_estimate=LATE,
        name="total_rows",
    )(state, own, *column)


def final_kernel(total_ref, p1, p2, p3, gain_ref, out_ref):
    total = total_ref[...]
    for got in (p1, p2, p3):
        total = total + got[...].astype(jnp.float32)
    out_ref[...] = rms_scale(total, gain_ref[...]).astype(jnp.bfloat16)


def final_rows(total, plane, gain):
    return pl.pallas_call(
        final_kernel,
        out_shape=jax.ShapeDtypeStruct(total.shape, jnp.bfloat16),
        in_specs=[vmem()] * 5,
        out_specs=vmem(),
        compiler_params=SMALL,
        name="final_rows",
    )(total, *plane, gain)


def place(z, y, c, x):
    return ((z * 2 + y) * 2 + c) * 2 + x


def swap(value, dz, dy, dc, dx):
    pairs = [
        (place(z, y, c, x), place(z ^ dz, y ^ dy, c ^ dc, x ^ dx))
        for z in range(4)
        for y in range(2)
        for c in range(2)
        for x in range(2)
    ]
    return lax.ppermute(value, ALL, pairs)


PLANE = ((0, 0), (1, 1), (0, 1), (1, 0))


def swap_z(pieces):
    return tuple(swap(piece, d, 0, 0, 0) for d, piece in zip((1, 2, 3), pieces))


def swap_plane(pieces):
    return tuple(swap(piece, 0, dy, 0, dx) for (dy, dx), piece in zip(PLANE[1:], pieces))


def local_dense(
    queries, fresh_key_value, key_value_cache, request_page_index, cache_length_rows, residual,
    w_out, gain_in, route_ids, route_weights, expert_home, w_gate, w_up, w_down, gain_out,
):
    tp_index = lax.axis_index("tp")
    req_index = lax.axis_index("req")
    tokens, width = residual.shape
    half = tokens // 2
    far = half * 3 // 4
    groups = expert_home.shape[0]
    weights = (w_gate[0], w_up[0], w_down[0])
    partner_weights = tuple(swap(stay(w), 0, 0, 1, 0) for w in weights)
    group = req_index.reshape(1)
    tp_index, pages = tp_index.reshape(1), request_page_index.T
    sent, *kept = other_terms(
        pages, cache_length_rows, tp_index, group, queries, fresh_key_value, key_value_cache, w_out
    )
    own_state, pack = own_terms(
        pages, cache_length_rows, tp_index, expert_home, kept, residual, route_ids.T,
        route_weights.T,
    )
    got, partner_weights = barrier(swap(sent, 0, 0, 0, 1), partner_weights)
    state, far_rows, last_rows = norm_rows(own_state, got, pack, gain_in[None, :], far)
    rows = join_rows((far_rows, last_rows), (0, 0), LATE, "own_rows")
    z_rows = swap_z((far_rows,) * 3)
    onward_plane = join_rows(z_rows, (0, 0, 0), LATE, "onward_plane")
    plane_rows, far_pieces = barrier(swap_plane((rows,) * 3), onward_plane)
    plane_rows = (rows,) + plane_rows
    onward_z = join_rows(plane_rows, (far,) * 4, None, "onward_z")
    z_pieces = swap_z((onward_z,) * 3)
    plane_pieces = swap_plane((onward_plane,) * 3)
    near, *kept = near_rows(groups, group, plane_rows, far_pieces, weights, partner_weights)
    parts = piece_rows(groups, group, z_pieces + plane_pieces, *kept)
    z_parts, plane_parts = swap_z(parts[:3]), swap_plane(parts[3:])
    first = first_sum(near, z_parts[0], half)
    plane_parts, first = barrier(plane_parts, first)
    far_sums = plane_sum(near, plane_parts)
    last_parts, far_sums = barrier(z_parts[1:], far_sums)
    own, *near_sums = column_sum(near, first, last_parts, half)
    total = total_rows(state, own, swap_z(far_sums))
    last_plane, total = barrier(swap_plane(near_sums), total)
    return final_rows(total, last_plane, gain_out[None, :])


def solution(mesh):
    dense = mesh.shape["req"] == 16 and mesh.shape["tp"] == 2
    return jax.shard_map(
        local_dense if dense else local_sparse,
        mesh=mesh,
        in_specs=(
            P("req", "tp"),
            P("req", "tp"),
            P("req", None, "tp"),
            P("req", None),
            P("req"),
            P("req", None),
            P("tp", None),
            P(),
            P("req", None),
            P("req", None),
            P(),
            P("req", None, "tp"),
            P("req", None, "tp"),
            P("req", "tp", None),
            P(),
        ),
        out_specs=P(("req", "tp"), None),
        check_vma=False,
    )
```

```python
import functools

import jax
import jax.numpy as jnp
from jax import lax
from jax.experimental import pallas as pl
from jax.experimental.pallas import tpu as pltpu
from jax.sharding import PartitionSpec as P

HEAD_WIDTH = 128
TOPK = 8
PRE_DEV = 56


EPSILON = 1e-06


def rms_scale(value_rows, gain_row):
    mean_square = jnp.mean(value_rows * value_rows, axis=-1, keepdims=True)
    return value_rows * lax.rsqrt(mean_square + EPSILON) * gain_row


def softmax_rounded(scores):
    row_peak = jnp.max(scores, axis=-1, keepdims=True)
    weights = jnp.exp(scores - row_peak)
    return (weights / jnp.sum(weights, axis=-1, keepdims=True)).astype(jnp.bfloat16)


def group_attention(queries, fresh_key_value, page_pool, page_rows, lengths):
    tokens_here = queries.shape[0]
    kv_heads = fresh_key_value.shape[1] // (2 * HEAD_WIDTH)
    group_size = queries.shape[1] // (HEAD_WIDTH * kv_heads)
    score_scale = HEAD_WIDTH ** (-0.5)
    split_query = queries.reshape(tokens_here, kv_heads, group_size, HEAD_WIDTH)
    fresh_kv = fresh_key_value.reshape(tokens_here, kv_heads, 2, HEAD_WIDTH)
    gathered_pages = page_pool[page_rows]
    cached = gathered_pages.reshape(page_rows.shape[0], -1, kv_heads, 2, HEAD_WIDTH)
    places = jnp.arange(cached.shape[1], dtype=jnp.int32)
    prefill_query = split_query[:PRE_DEV]
    prefill_fresh = fresh_kv[:PRE_DEV]
    cache_scores = (
        jnp.einsum(
            "ikgd,ckd->kgic", prefill_query, cached[0, :, :, 0], preferred_element_type=jnp.float32
        )
        * score_scale
    )
    cache_scores = jnp.where(places < lengths[0], cache_scores, -jnp.inf)
    block_scores = (
        jnp.einsum(
            "ikgd,jkd->kgij",
            prefill_query,
            prefill_fresh[:, :, 0],
            preferred_element_type=jnp.float32,
        )
        * score_scale
    )
    causal = jnp.arange(PRE_DEV)[:, None] >= jnp.arange(PRE_DEV)[None, :]
    block_scores = jnp.where(causal, block_scores, -jnp.inf)
    prefill_probs = softmax_rounded(jnp.concatenate([cache_scores, block_scores], axis=3))
    prefill_values = jnp.concatenate([cached[0, :, :, 1], prefill_fresh[:, :, 1]], axis=0)
    prefill_out = jnp.einsum(
        "kgic,ckd->ikgd", prefill_probs, prefill_values, preferred_element_type=jnp.float32
    )
    decode_query = split_query[PRE_DEV:]
    decode_fresh = fresh_kv[PRE_DEV:]
    decode_scores = (
        jnp.einsum(
            "rkgd,rckd->rkgc", decode_query, cached[1:, :, :, 0], preferred_element_type=jnp.float32
        )
        * score_scale
    )
    decode_scores = jnp.where(
        places[None, None, None, :] < lengths[1:, None, None, None], decode_scores, -jnp.inf
    )
    own_scores = (
        jnp.einsum(
            "rkgd,rkd->rkg", decode_query, decode_fresh[:, :, 0], preferred_element_type=jnp.float32
        )[..., None]
        * score_scale
    )
    decode_probs = softmax_rounded(jnp.concatenate([decode_scores, own_scores], axis=3))
    decode_values = jnp.concatenate([cached[1:, :, :, 1], decode_fresh[:, None, :, 1]], axis=1)
    decode_out = jnp.einsum(
        "rkgc,rckd->rkgd", decode_probs, decode_values, preferred_element_type=jnp.float32
    )
    joined = jnp.concatenate([prefill_out, decode_out], axis=0)
    return joined.reshape(tokens_here, -1).astype(jnp.bfloat16)


def slot_positions(block_owner, experts, capacity):
    flat_owner = block_owner.reshape(-1)
    onehot = (flat_owner[:, None] == jnp.arange(experts, dtype=jnp.int32)[None, :]).astype(
        jnp.int32
    )
    earlier = jnp.cumsum(onehot, axis=0) - onehot
    slot_index = jnp.sum(earlier * onehot, axis=1)
    return (flat_owner * capacity + slot_index).reshape(block_owner.shape)


def place_matrix(positions, slots_total):
    matches = positions[None, :, :] == jnp.arange(slots_total, dtype=jnp.int32)[:, None, None]
    return jnp.any(matches, axis=2).astype(jnp.bfloat16)


def local_sparse(
    queries,
    fresh_key_value,
    key_value_cache,
    request_page_index,
    cache_length_rows,
    residual,
    w_out,
    gain_in,
    route_ids,
    route_weights,
    expert_home,
    w_gate,
    w_up,
    w_down,
    gain_out,
):
    tp_size = lax.axis_size("tp")
    req_size = lax.axis_size("req")
    tp_index = lax.axis_index("tp")
    model_width = residual.shape[1]
    tokens_here = residual.shape[0]
    quarter = tokens_here // tp_size
    experts = expert_home.shape[0]
    capacity = min(quarter, max(2, 2 * quarter * TOPK // experts))
    context = group_attention(
        queries, fresh_key_value, key_value_cache, request_page_index, cache_length_rows
    )
    head_terms = jnp.dot(context, w_out, preferred_element_type=jnp.float32)
    state = residual.astype(jnp.float32) + lax.psum(head_terms, "tp")
    owners = jnp.sum(
        jnp.where(
            route_ids[:, :, None] == jnp.arange(experts, dtype=jnp.int32)[None, None, :],
            expert_home[None, None, :],
            0,
        ),
        axis=2,
    )
    shares = route_weights / jnp.sum(route_weights, axis=1, keepdims=True)
    own_start = tp_index * quarter
    own_state = lax.dynamic_slice_in_dim(state, own_start, quarter, 0)
    own_shares = lax.dynamic_slice_in_dim(shares, own_start, quarter, 0)
    normed_all = rms_scale(state, gain_in).astype(jnp.bfloat16)
    positions_all = jax.vmap(lambda block_owner: slot_positions(block_owner, experts, capacity))(
        owners.reshape(tp_size, quarter, TOPK)
    )
    placing = jax.vmap(lambda positions: place_matrix(positions, experts * capacity))(positions_all)
    outgoing = jnp.einsum(
        "qmi,qid->qmd",
        placing,
        normed_all.reshape(tp_size, quarter, model_width),
        preferred_element_type=jnp.float32,
    )
    outgoing = outgoing.astype(jnp.bfloat16).reshape(tp_size, experts, capacity, model_width)
    incoming = lax.all_to_all(outgoing, "req", split_axis=1, concat_axis=1, tiled=True)
    own_positions = lax.dynamic_index_in_dim(positions_all, tp_index, 0, keepdims=False)
    expert_rows = incoming.reshape(-1, model_width)
    gate_proj = jnp.dot(expert_rows, w_gate[0], preferred_element_type=jnp.float32)
    up_proj = jnp.dot(expert_rows, w_up[0], preferred_element_type=jnp.float32)
    inner_units = (jax.nn.silu(gate_proj) * up_proj).astype(jnp.bfloat16)
    summed = lax.psum_scatter(
        jnp.dot(inner_units, w_down[0], preferred_element_type=jnp.float32).astype(jnp.bfloat16),
        "tp",
        scatter_dimension=0,
        tiled=True,
    )
    results = summed.reshape(req_size, capacity, model_width)
    returned = lax.all_to_all(results, "req", split_axis=0, concat_axis=0, tiled=True).reshape(
        -1, model_width
    )
    picked = returned[own_positions]
    mixture = jnp.sum(own_shares[:, :, None] * picked.astype(jnp.float32), axis=1)
    return rms_scale(own_state + mixture, gain_out).astype(jnp.bfloat16)


ALL = ("req", "tp")
MASKED = -1e30
LANES = 128
MIB = 1024 * 1024
SMALL = pltpu.CompilerParams(vmem_limit_bytes=8 * MIB)


def vmem():
    return pl.BlockSpec(memory_space=pltpu.VMEM)


def smem():
    return pl.BlockSpec(memory_space=pltpu.SMEM)


def hbm():
    return pl.BlockSpec(memory_space=pltpu.HBM)


def stay(value):
    return pltpu.with_memory_space_constraint(value, pltpu.HBM)


def barrier(*values):
    return lax.optimization_barrier(values)


def multiplicity(page_rows, length, pool_pages, page_tokens):
    rows = page_rows[0].shape[0]
    lane = lax.broadcasted_iota(jnp.int32, (rows, page_tokens), 1)
    parts = []
    for page in range(pool_pages):
        count = jnp.zeros((rows, page_tokens), jnp.float32)
        for slot, named in enumerate(page_rows):
            hit = (named == page) & (lane + slot * page_tokens < length)
            count = count + jnp.where(hit, 1.0, 0.0)
        parts.append(count)
    return jnp.concatenate(parts, axis=1)


def pack_shares(ids, routed, home_ref):
    groups = home_ref.shape[0]
    choices, tokens = ids.shape
    spot = lax.broadcasted_iota(jnp.int32, (groups, tokens), 0)
    shares = routed / jnp.sum(routed, axis=0, keepdims=True)
    by_expert = jnp.zeros((groups, tokens), jnp.float32)
    for k in range(choices):
        by_expert = by_expert + jnp.where(spot == ids[k : k + 1, :], shares[k : k + 1, :], 0.0)
    by_home = jnp.zeros((groups, tokens), jnp.float32)
    for e in range(groups):
        by_home = by_home + jnp.where(spot == home_ref[e], by_expert[e : e + 1, :], 0.0)
    rounded = by_home.astype(jnp.bfloat16).astype(jnp.float32)
    tall = jnp.concatenate(
        [rounded, by_home - rounded, jnp.zeros((LANES - 2 * groups, tokens), jnp.float32)], axis=0
    )
    square = jnp.concatenate([tall, jnp.zeros((LANES, LANES - tokens), jnp.float32)], axis=1)
    return jnp.transpose(square)


def count_positions(pages_ref, lengths_ref, pool_pages, page_tokens, count_ref):
    slots, requests = pages_ref.shape
    decodes = requests - 1
    row = lax.broadcasted_iota(jnp.int32, (decodes, page_tokens), 0)

    def by_row(read):
        value = jnp.zeros((decodes, page_tokens), jnp.int32)
        for j in range(decodes):
            value = jnp.where(row == j, read(j + 1), value)
        return value

    full = lambda scalar: jnp.full((decodes, page_tokens), scalar, jnp.int32)
    first = multiplicity(
        [full(pages_ref[s, 0]) for s in range(slots)], full(lengths_ref[0]), pool_pages, page_tokens
    )
    later = multiplicity(
        [by_row(lambda j, s=s: pages_ref[s, j]) for s in range(slots)],
        by_row(lambda j: lengths_ref[j]),
        pool_pages,
        page_tokens,
    )
    count_ref[...] = jnp.concatenate([first] * (PRE_DEV // decodes) + [later], axis=0)


def attend(start, q_ref, fresh_ref, cache_ref, count_ref, context_ref):
    rows = context_ref.shape[0]
    tokens = q_ref.shape[0]
    kv_heads = fresh_ref.shape[1] // (2 * HEAD_WIDTH)
    group = q_ref.shape[1] // (HEAD_WIDTH * kv_heads)
    query_place = start + lax.broadcasted_iota(jnp.int32, (rows, tokens), 0)
    key_place = lax.broadcasted_iota(jnp.int32, (rows, tokens), 1)
    seen = (key_place == query_place) | ((key_place <= query_place) & (query_place < PRE_DEV))
    seen = jnp.concatenate([jnp.where(seen, 1.0, 0.0)] * group, axis=0)
    visible = jnp.concatenate([count_ref[pl.ds(start, rows), :]] * group, axis=0)
    scale = HEAD_WIDTH**-0.5
    contract_last = (((1,), (1,)), ((), ()))
    for k in range(kv_heads):
        key_at, value_at = 2 * k * HEAD_WIDTH, (2 * k + 1) * HEAD_WIDTH
        heads = [k * group + g for g in range(group)]
        query = jnp.concatenate(
            [q_ref[pl.ds(start, rows), h * HEAD_WIDTH : (h + 1) * HEAD_WIDTH] for h in heads],
            axis=0,
        )
        keys = cache_ref[:, :, key_at : key_at + HEAD_WIDTH].reshape(-1, HEAD_WIDTH)
        values = cache_ref[:, :, value_at : value_at + HEAD_WIDTH].reshape(-1, HEAD_WIDTH)
        old = lax.dot_general(query, keys, contract_last, preferred_element_type=jnp.float32)
        new = lax.dot_general(
            query,
            fresh_ref[:, key_at : key_at + HEAD_WIDTH],
            contract_last,
            preferred_element_type=jnp.float32,
        )
        old = jnp.where(visible > 0, old * scale, MASKED)
        new = jnp.where(seen > 0, new * scale, MASKED)
        peak = jnp.maximum(
            jnp.max(old, axis=1, keepdims=True), jnp.max(new, axis=1, keepdims=True)
        )
        old = jnp.exp(old - peak) * visible
        new = jnp.exp(new - peak) * seen
        inverse = 1.0 / (
            jnp.sum(old, axis=1, keepdims=True) + jnp.sum(new, axis=1, keepdims=True)
        )
        mixed = jnp.dot(
            (old * inverse).astype(jnp.bfloat16), values, preferred_element_type=jnp.float32
        ) + jnp.dot(
            (new * inverse).astype(jnp.bfloat16),
            fresh_ref[:, value_at : value_at + HEAD_WIDTH],
            preferred_element_type=jnp.float32,
        )
        mixed = mixed.astype(jnp.bfloat16)
        for g, h in enumerate(heads):
            context_ref[:, h * HEAD_WIDTH : (h + 1) * HEAD_WIDTH] = mixed[g * rows : (g + 1) * rows]


OUT_BLOCK = 512
W_PIECES = 4


def other_kernel(
    pages_ref, lengths_ref, tp_ref, group_ref, q_hbm, fresh_hbm, cache_hbm, w_hbm,
    send_ref, q_ref, fresh_ref, cache_ref, w_ref, count_ref, context_ref, terms_ref, sems,
):
    moves = [(q_hbm, q_ref), (fresh_hbm, fresh_ref), (cache_hbm, cache_ref)]
    depth = w_ref.shape[0] // W_PIECES
    parts = [slice(i * depth, (i + 1) * depth) for i in range(W_PIECES)]
    moves += [(w_hbm.at[part, :], w_ref.at[part, :]) for part in parts]
    fetches = [
        pltpu.make_async_copy(source, target, sems.at[i])
        for i, (source, target) in enumerate(moves)
    ]
    for fetch in fetches:
        fetch.start()
    half = context_ref.shape[0]
    start = pl.multiple_of((1 - tp_ref[0]) * half, half)
    count_positions(pages_ref, lengths_ref, cache_ref.shape[0], cache_ref.shape[1], count_ref)
    for fetch in fetches[:3]:
        fetch.wait()
    attend(start, q_ref, fresh_ref, cache_ref, count_ref, context_ref)
    for i, part in enumerate(parts):
        fetches[3 + i].wait()
        for at in range(0, w_ref.shape[1], OUT_BLOCK):
            cols = slice(at, at + OUT_BLOCK)
            terms = jnp.dot(
                context_ref[:, part], w_ref[part, cols], preferred_element_type=jnp.float32
            )
            terms_ref[:, cols] = terms if i == 0 else terms_ref[:, cols] + terms
    send_ref[...] = terms_ref[...].astype(jnp.bfloat16)


def other_terms(pages, lengths, tp_index, group, queries, fresh, cache, w_out):
    half = queries.shape[0] // 2
    moved = (queries, fresh, cache, w_out)
    return pl.pallas_call(
        other_kernel,
        out_shape=(jax.ShapeDtypeStruct((half, w_out.shape[1]), jnp.bfloat16),)
        + tuple(jax.ShapeDtypeStruct(v.shape, v.dtype) for v in moved),
        in_specs=[smem()] * 4 + [hbm()] * 4,
        out_specs=(vmem(),) * 5,
        scratch_shapes=[
            pltpu.VMEM((queries.shape[0], cache.shape[0] * cache.shape[1]), jnp.float32),
            pltpu.VMEM((half, queries.shape[1]), jnp.bfloat16),
            pltpu.VMEM((half, w_out.shape[1]), jnp.float32),
            pltpu.SemaphoreType.DMA((3 + W_PIECES,)),
        ],
        compiler_params=pltpu.CompilerParams(vmem_limit_bytes=16 * MIB),
        name="other_terms",
    )(stay(pages), stay(lengths), tp_index, group, *[stay(v) for v in moved])


def own_kernel(
    pages_ref, lengths_ref, tp_ref, home_ref, q_ref, fresh_ref, cache_ref, w_ref,
    residual_hbm, ids_hbm, routed_hbm,
    own_ref, pack_ref, residual_ref, ids_ref, routed_ref, count_ref, context_ref, every_ref, sems,
):
    moves = ((ids_hbm, ids_ref), (routed_hbm, routed_ref), (residual_hbm, residual_ref))
    fetches = [
        pltpu.make_async_copy(source, target, sems.at[i])
        for i, (source, target) in enumerate(moves)
    ]
    for fetch in fetches:
        fetch.start()
    half = context_ref.shape[0]
    start = pl.multiple_of(tp_ref[0] * half, half)
    count_positions(pages_ref, lengths_ref, cache_ref.shape[0], cache_ref.shape[1], count_ref)
    attend(start, q_ref, fresh_ref, cache_ref, count_ref, context_ref)
    for fetch in fetches:
        fetch.wait()
    every_ref[...] = pack_shares(ids_ref[...], routed_ref[...], home_ref)
    pack_ref[...] = every_ref[pl.ds(start, half), :].astype(jnp.bfloat16)
    for at in range(0, w_ref.shape[1], OUT_BLOCK):
        cols = slice(at, at + OUT_BLOCK)
        own_ref[:, cols] = residual_ref[pl.ds(start, half), cols].astype(jnp.float32) + jnp.dot(
            context_ref[...], w_ref[:, cols], preferred_element_type=jnp.float32
        )


def own_terms(pages, lengths, tp_index, home, kept, residual, ids, routed):
    tokens, width = residual.shape
    half = tokens // 2
    queries, _, cache, _ = kept
    moved = (residual, ids, routed)
    return pl.pallas_call(
        own_kernel,
        out_shape=(
            jax.ShapeDtypeStruct((half, width), jnp.float32),
            jax.ShapeDtypeStruct((half, LANES), jnp.bfloat16),
        ),
        in_specs=[smem()] * 4 + [vmem()] * 4 + [hbm()] * 3,
        out_specs=(vmem(),) * 2,
        scratch_shapes=[pltpu.VMEM(v.shape, v.dtype) for v in moved]
        + [
            pltpu.VMEM((tokens, cache.shape[0] * cache.shape[1]), jnp.float32),
            pltpu.VMEM((half, queries.shape[1]), jnp.bfloat16),
            pltpu.VMEM((LANES, LANES), jnp.float32),
            pltpu.SemaphoreType.DMA((3,)),
        ],
        compiler_params=pltpu.CompilerParams(vmem_limit_bytes=16 * MIB),
        name="own_terms",
    )(stay(pages), stay(lengths), tp_index, stay(home), *kept, *[stay(v) for v in moved])


LATE = pl.CostEstimate(flops=3 * 10**10, bytes_accessed=1 << 20, transcendentals=0)


def norm_kernel(own_ref, got_ref, pack_ref, gain_ref, state_ref, far_ref, near_ref):
    state = own_ref[...] + got_ref[...].astype(jnp.float32)
    state_ref[...] = state
    normed = rms_scale(state, gain_ref[...]).astype(jnp.bfloat16)
    width = state.shape[1]
    far = far_ref.shape[0]
    far_ref[:, :width] = normed[:far]
    far_ref[:, width:] = pack_ref[:far, :]
    near_ref[:, :width] = normed[far:]
    near_ref[:, width:] = pack_ref[far:, :]


def norm_rows(own, got, pack, gain, far):
    rows, width = own.shape
    return pl.pallas_call(
        norm_kernel,
        out_shape=(
            jax.ShapeDtypeStruct((rows, width), jnp.float32),
            jax.ShapeDtypeStruct((far, width + LANES), jnp.bfloat16),
            jax.ShapeDtypeStruct((rows - far, width + LANES), jnp.bfloat16),
        ),
        in_specs=[vmem()] * 4,
        out_specs=(vmem(),) * 3,
        compiler_params=SMALL,
        name="norm_rows",
    )(own, got, pack, gain)


def join_kernel(starts, *refs):
    out_ref = refs[-1]
    at = 0
    for start, piece in zip(starts, refs[:-1]):
        height = piece.shape[0] - start
        out_ref[at : at + height, :] = piece[start:, :]
        at += height


def join_rows(pieces, starts, cost, name):
    height = sum(piece.shape[0] - start for piece, start in zip(pieces, starts))
    return pl.pallas_call(
        functools.partial(join_kernel, starts),
        out_shape=jax.ShapeDtypeStruct((height, pieces[0].shape[1]), jnp.bfloat16),
        in_specs=[vmem()] * len(pieces),
        out_specs=vmem(),
        compiler_params=SMALL,
        cost_estimate=cost,
        name=name,
    )(*pieces)


def hidden_units(groups, group_ref, x_ref, w_refs, h_ref, ready):
    rows = x_ref.shape[0]
    width = w_refs[0].shape[0]
    hidden = h_ref.shape[1] // 2
    lane = lax.broadcasted_iota(jnp.int32, (rows, LANES), 1)
    packed = x_ref[:, width:].astype(jnp.float32)
    for e in (1, 0):
        group = group_ref[0] ^ e
        share = jnp.sum(
            jnp.where((lane == group) | (lane == group + groups), packed, 0.0),
            axis=1,
            keepdims=True,
        )
        ready(e)
        both = jnp.dot(x_ref[:, :width], w_refs[e][...], preferred_element_type=jnp.float32)
        gate, up = both[:, :hidden], both[:, hidden:]
        h_ref[:, e * hidden : (e + 1) * hidden] = (
            share * up * (gate / (1.0 + jnp.exp(-gate)))
        ).astype(jnp.bfloat16)


DOWN_BLOCK = 512


def gather_pieces(pieces, x_ref):
    at = 0
    for piece in pieces:
        x_ref[at : at + piece.shape[0], :] = piece[...]
        at += piece.shape[0]
    if at < x_ref.shape[0]:
        x_ref[at:, :] = jnp.zeros((x_ref.shape[0] - at, x_ref.shape[1]), jnp.bfloat16)


def near_kernel(
    groups, group_ref, r0, r1, r2, r3, far_ref, z1_ref, wg1, wu1, wg0, wu0, wd0, wd1,
    out_ref, z1_out_ref, w0_ref, w1_ref, down_ref, x_ref, h_ref, sems,
):
    hidden = wg0.shape[1]
    fetches = [
        pltpu.make_async_copy(source, target, sems.at[i])
        for i, (source, target) in enumerate(
            (
                (wg0, w0_ref.at[:, :hidden]),
                (wu0, w0_ref.at[:, hidden:]),
                (wd0, down_ref.at[:hidden, :]),
                (wd1, down_ref.at[hidden:, :]),
                (wg1, w1_ref.at[:, :hidden]),
                (wu1, w1_ref.at[:, hidden:]),
            )
        )
    ]
    for fetch in fetches:
        fetch.start()
    gather_pieces((r0, r1, r2, r3, far_ref, z1_ref), x_ref)

    def ready(e):
        for fetch in fetches[4:] if e else fetches[:2]:
            fetch.wait()

    hidden_units(groups, group_ref, x_ref, (w0_ref, w1_ref), h_ref, ready)
    fetches[2].wait()
    fetches[3].wait()
    height = out_ref.shape[0]
    for col in range(0, down_ref.shape[1], DOWN_BLOCK):
        cols = slice(col, col + DOWN_BLOCK)
        down = jnp.dot(h_ref[...], down_ref[:, cols], preferred_element_type=jnp.float32)
        out_ref[:, cols] = down[:height]
        z1_out_ref[:, cols] = down[height : height + z1_ref.shape[0]].astype(jnp.bfloat16)


def expert_cost(rows, width, hidden):
    return pl.CostEstimate(
        flops=12 * rows * width * hidden,
        bytes_accessed=12 * width * hidden,
        transcendentals=2 * rows * hidden,
    )


def near_rows(groups, group, rows, far, near_z, weights, partner_weights):
    height = 4 * rows[0].shape[0] + far.shape[0]
    padded = -(-(height + near_z.shape[0]) // 16) * 16
    width, hidden = weights[0].shape
    wg0, wu0, wd0 = weights
    wg1, wu1, wd1 = partner_weights
    return pl.pallas_call(
        functools.partial(near_kernel, groups),
        out_shape=(
            jax.ShapeDtypeStruct((height, width), jnp.float32),
            jax.ShapeDtypeStruct((near_z.shape[0], width), jnp.bfloat16),
            jax.ShapeDtypeStruct((width, 2 * hidden), jnp.bfloat16),
            jax.ShapeDtypeStruct((width, 2 * hidden), jnp.bfloat16),
            jax.ShapeDtypeStruct((2 * hidden, width), jnp.bfloat16),
        ),
        in_specs=[smem()] + [vmem()] * 8 + [hbm()] * 4,
        out_specs=(vmem(),) * 5,
        scratch_shapes=[
            pltpu.VMEM((padded, width + LANES), jnp.bfloat16),
            pltpu.VMEM((padded, 2 * hidden), jnp.bfloat16),
            pltpu.SemaphoreType.DMA((6,)),
        ],
        compiler_params=pltpu.CompilerParams(vmem_limit_bytes=24 * MIB),
        cost_estimate=expert_cost(height, width, hidden),
        name="near_rows",
    )(group, *rows, far, near_z, wg1, wu1, *[stay(w) for w in (wg0, wu0, wd0, wd1)])


def piece_kernel(groups, count, group_ref, *refs):
    pieces, (w0_ref, w1_ref, down_ref) = refs[:count], refs[count : count + 3]
    outs, (x_ref, h_ref) = refs[count + 3 : 2 * count + 3], refs[2 * count + 3 :]
    gather_pieces(pieces, x_ref)
    hidden_units(groups, group_ref, x_ref, (w0_ref, w1_ref), h_ref, lambda e: None)
    for col in range(0, down_ref.shape[1], DOWN_BLOCK):
        cols = slice(col, col + DOWN_BLOCK)
        down = jnp.dot(h_ref[...], down_ref[:, cols], preferred_element_type=jnp.float32)
        at = 0
        for out in outs:
            out[:, cols] = down[at : at + out.shape[0]].astype(jnp.bfloat16)
            at += out.shape[0]


def piece_rows(groups, group, pieces, w0, w1, down):
    count = len(pieces)
    height = sum(piece.shape[0] for piece in pieces)
    padded = -(-height // 16) * 16
    width, hidden = w1.shape[0], w1.shape[1] // 2
    return pl.pallas_call(
        functools.partial(piece_kernel, groups, count),
        out_shape=tuple(
            jax.ShapeDtypeStruct((piece.shape[0], width), jnp.bfloat16) for piece in pieces
        ),
        in_specs=[smem()] + [vmem()] * (count + 3),
        out_specs=(vmem(),) * count,
        scratch_shapes=[
            pltpu.VMEM((padded, width + LANES), jnp.bfloat16),
            pltpu.VMEM((padded, 2 * hidden), jnp.bfloat16),
        ],
        compiler_params=pltpu.CompilerParams(vmem_limit_bytes=24 * MIB),
        cost_estimate=expert_cost(height, width, hidden),
        name="piece_rows",
    )(group, *pieces, w0, w1, down)


def plane_sum_kernel(near_ref, g1, g2, g3, m1, m2, m3):
    far = m1.shape[0]
    start = near_ref.shape[0] - 3 * far
    for j, out in enumerate((m1, m2, m3)):
        rows = slice(j * far, (j + 1) * far)
        total = near_ref[start + j * far : start + (j + 1) * far, :]
        for got in (g1, g2, g3):
            total = total + got[rows, :].astype(jnp.float32)
        out[...] = total.astype(jnp.bfloat16)


def plane_sum(near, got):
    far, width = got[0].shape[0] // 3, got[0].shape[1]
    return pl.pallas_call(
        plane_sum_kernel,
        out_shape=tuple(jax.ShapeDtypeStruct((far, width), jnp.bfloat16) for _ in range(3)),
        in_specs=[vmem()] * 4,
        out_specs=(vmem(),) * 3,
        compiler_params=SMALL,
        name="plane_sum",
    )(near, *got)


def first_sum_kernel(rows, near_ref, g1, out_ref):
    near = g1.shape[0] // 4
    for i in range(4):
        there = slice(i * near, (i + 1) * near)
        out_ref[there, :] = near_ref[(i + 1) * rows - near : (i + 1) * rows, :] + g1[
            there, :
        ].astype(jnp.float32)


def first_sum(near, got, rows):
    return pl.pallas_call(
        functools.partial(first_sum_kernel, rows),
        out_shape=jax.ShapeDtypeStruct(got.shape, jnp.float32),
        in_specs=[vmem()] * 2,
        out_specs=vmem(),
        compiler_params=SMALL,
        cost_estimate=LATE,
        name="first_sum",
    )(near, got)


def column_sum_kernel(near_ref, first_ref, g2, g3, own_ref, m1, m2, m3):
    rows = own_ref.shape[0]
    near = first_ref.shape[0] // 4
    far = rows - near
    for i, out in enumerate((own_ref, m1, m2, m3)):
        out[:far, :] = near_ref[i * rows : i * rows + far, :].astype(out.dtype)
        total = first_ref[i * near : (i + 1) * near, :]
        for got in (g2, g3):
            total = total + got[i * near : (i + 1) * near, :].astype(jnp.float32)
        out[far:, :] = total.astype(out.dtype)


def column_sum(near, first, got, rows):
    width = near.shape[1]
    kinds = (jnp.float32, jnp.bfloat16, jnp.bfloat16, jnp.bfloat16)
    return pl.pallas_call(
        column_sum_kernel,
        out_shape=tuple(jax.ShapeDtypeStruct((rows, width), kind) for kind in kinds),
        in_specs=[vmem()] * 4,
        out_specs=(vmem(),) * 4,
        compiler_params=SMALL,
        cost_estimate=LATE,
        name="column_sum",
    )(near, first, *got)


def total_kernel(state_ref, own_ref, z1, z2, z3, total_ref):
    total_ref[...] = state_ref[...] + own_ref[...]
    far = z1.shape[0]
    part = total_ref[:far, :]
    for got in (z1, z2, z3):
        part = part + got[...].astype(jnp.float32)
    total_ref[:far, :] = part


def total_rows(state, own, column):
    return pl.pallas_call(
        total_kernel,
        out_shape=jax.ShapeDtypeStruct(state.shape, jnp.float32),
        in_specs=[vmem()] * 5,
        out_specs=vmem(),
        compiler_params=SMALL,
        cost_estimate=LATE,
        name="total_rows",
    )(state, own, *column)


def final_kernel(total_ref, p1, p2, p3, gain_ref, out_ref):
    total = total_ref[...]
    for got in (p1, p2, p3):
        total = total + got[...].astype(jnp.float32)
    out_ref[...] = rms_scale(total, gain_ref[...]).astype(jnp.bfloat16)


def final_rows(total, plane, gain):
    return pl.pallas_call(
        final_kernel,
        out_shape=jax.ShapeDtypeStruct(total.shape, jnp.bfloat16),
        in_specs=[vmem()] * 5,
        out_specs=vmem(),
        compiler_params=SMALL,
        name="final_rows",
    )(total, *plane, gain)


def place(z, y, c, x):
    return ((z * 2 + y) * 2 + c) * 2 + x


def swap(value, dz, dy, dc, dx):
    pairs = [
        (place(z, y, c, x), place(z ^ dz, y ^ dy, c ^ dc, x ^ dx))
        for z in range(4)
        for y in range(2)
        for c in range(2)
        for x in range(2)
    ]
    return lax.ppermute(value, ALL, pairs)


PLANE = ((0, 0), (1, 1), (0, 1), (1, 0))


def swap_z(pieces):
    return tuple(swap(piece, d, 0, 0, 0) for d, piece in zip((1, 2, 3), pieces))


def swap_plane(pieces):
    return tuple(swap(piece, 0, dy, 0, dx) for (dy, dx), piece in zip(PLANE[1:], pieces))


def local_dense(
    queries, fresh_key_value, key_value_cache, request_page_index, cache_length_rows, residual,
    w_out, gain_in, route_ids, route_weights, expert_home, w_gate, w_up, w_down, gain_out,
):
    tp_index = lax.axis_index("tp")
    req_index = lax.axis_index("req")
    tokens, width = residual.shape
    half = tokens // 2
    far = half * 3 // 4
    groups = expert_home.shape[0]
    weights = (w_gate[0], w_up[0], w_down[0])
    partner_weights = tuple(swap(stay(w), 0, 0, 1, 0) for w in weights)
    group = req_index.reshape(1)
    tp_index, pages = tp_index.reshape(1), request_page_index.T
    sent, *kept = other_terms(
        pages, cache_length_rows, tp_index, group, queries, fresh_key_value, key_value_cache, w_out
    )
    own_state, pack = own_terms(
        pages, cache_length_rows, tp_index, expert_home, kept, residual, route_ids.T,
        route_weights.T,
    )
    got, partner_weights = barrier(swap(sent, 0, 0, 0, 1), partner_weights)
    state, far_rows, last_rows = norm_rows(own_state, got, pack, gain_in[None, :], far)
    rows = join_rows((far_rows, last_rows), (0, 0), LATE, "own_rows")
    z_rows = swap_z((far_rows,) * 3)
    onward_plane = join_rows(z_rows, (0, 0, 0), LATE, "onward_plane")
    plane_rows, far_pieces = barrier(swap_plane((rows,) * 3), onward_plane)
    plane_rows = (rows,) + plane_rows
    onward_z = join_rows(plane_rows, (far,) * 4, None, "onward_z")
    z_pieces = swap_z((onward_z,) * 3)
    plane_pieces = swap_plane((onward_plane,) * 3)
    near, near_part, *kept = near_rows(
        groups, group, plane_rows, far_pieces, z_pieces[0], weights, partner_weights
    )
    parts = piece_rows(groups, group, z_pieces[1:] + plane_pieces, *kept)
    z_parts, plane_parts = swap_z((near_part,) + parts[:2]), swap_plane(parts[2:])
    first = first_sum(near, z_parts[0], half)
    plane_parts, first = barrier(plane_parts, first)
    far_sums = plane_sum(near, plane_parts)
    last_parts, far_sums = barrier(z_parts[1:], far_sums)
    own, *near_sums = column_sum(near, first, last_parts, half)
    total = total_rows(state, own, swap_z(far_sums))
    last_plane, total = barrier(swap_plane(near_sums), total)
    return final_rows(total, last_plane, gain_out[None, :])


def solution(mesh):
    dense = mesh.shape["req"] == 16 and mesh.shape["tp"] == 2
    return jax.shard_map(
        local_dense if dense else local_sparse,
        mesh=mesh,
        in_specs=(
            P("req", "tp"),
            P("req", "tp"),
            P("req", None, "tp"),
            P("req", None),
            P("req"),
            P("req", None),
            P("tp", None),
            P(),
            P("req", None),
            P("req", None),
            P(),
            P("req", None, "tp"),
            P("req", None, "tp"),
            P("req", "tp", None),
            P(),
        ),
        out_specs=P(("req", "tp"), None),
        check_vma=False,
    )
```

```python
import functools

import jax
import jax.numpy as jnp
from jax import lax
from jax.experimental import pallas as pl
from jax.experimental.pallas import tpu as pltpu
from jax.sharding import PartitionSpec as P

HEAD_WIDTH = 128
TOPK = 8
PRE_DEV = 56


EPSILON = 1e-06


def rms_scale(value_rows, gain_row):
    mean_square = jnp.mean(value_rows * value_rows, axis=-1, keepdims=True)
    return value_rows * lax.rsqrt(mean_square + EPSILON) * gain_row


def softmax_rounded(scores):
    row_peak = jnp.max(scores, axis=-1, keepdims=True)
    weights = jnp.exp(scores - row_peak)
    return (weights / jnp.sum(weights, axis=-1, keepdims=True)).astype(jnp.bfloat16)


def group_attention(queries, fresh_key_value, page_pool, page_rows, lengths):
    tokens_here = queries.shape[0]
    kv_heads = fresh_key_value.shape[1] // (2 * HEAD_WIDTH)
    group_size = queries.shape[1] // (HEAD_WIDTH * kv_heads)
    score_scale = HEAD_WIDTH ** (-0.5)
    split_query = queries.reshape(tokens_here, kv_heads, group_size, HEAD_WIDTH)
    fresh_kv = fresh_key_value.reshape(tokens_here, kv_heads, 2, HEAD_WIDTH)
    gathered_pages = page_pool[page_rows]
    cached = gathered_pages.reshape(page_rows.shape[0], -1, kv_heads, 2, HEAD_WIDTH)
    places = jnp.arange(cached.shape[1], dtype=jnp.int32)
    prefill_query = split_query[:PRE_DEV]
    prefill_fresh = fresh_kv[:PRE_DEV]
    cache_scores = (
        jnp.einsum(
            "ikgd,ckd->kgic", prefill_query, cached[0, :, :, 0], preferred_element_type=jnp.float32
        )
        * score_scale
    )
    cache_scores = jnp.where(places < lengths[0], cache_scores, -jnp.inf)
    block_scores = (
        jnp.einsum(
            "ikgd,jkd->kgij",
            prefill_query,
            prefill_fresh[:, :, 0],
            preferred_element_type=jnp.float32,
        )
        * score_scale
    )
    causal = jnp.arange(PRE_DEV)[:, None] >= jnp.arange(PRE_DEV)[None, :]
    block_scores = jnp.where(causal, block_scores, -jnp.inf)
    prefill_probs = softmax_rounded(jnp.concatenate([cache_scores, block_scores], axis=3))
    prefill_values = jnp.concatenate([cached[0, :, :, 1], prefill_fresh[:, :, 1]], axis=0)
    prefill_out = jnp.einsum(
        "kgic,ckd->ikgd", prefill_probs, prefill_values, preferred_element_type=jnp.float32
    )
    decode_query = split_query[PRE_DEV:]
    decode_fresh = fresh_kv[PRE_DEV:]
    decode_scores = (
        jnp.einsum(
            "rkgd,rckd->rkgc", decode_query, cached[1:, :, :, 0], preferred_element_type=jnp.float32
        )
        * score_scale
    )
    decode_scores = jnp.where(
        places[None, None, None, :] < lengths[1:, None, None, None], decode_scores, -jnp.inf
    )
    own_scores = (
        jnp.einsum(
            "rkgd,rkd->rkg", decode_query, decode_fresh[:, :, 0], preferred_element_type=jnp.float32
        )[..., None]
        * score_scale
    )
    decode_probs = softmax_rounded(jnp.concatenate([decode_scores, own_scores], axis=3))
    decode_values = jnp.concatenate([cached[1:, :, :, 1], decode_fresh[:, None, :, 1]], axis=1)
    decode_out = jnp.einsum(
        "rkgc,rckd->rkgd", decode_probs, decode_values, preferred_element_type=jnp.float32
    )
    joined = jnp.concatenate([prefill_out, decode_out], axis=0)
    return joined.reshape(tokens_here, -1).astype(jnp.bfloat16)


def slot_positions(block_owner, experts, capacity):
    flat_owner = block_owner.reshape(-1)
    onehot = (flat_owner[:, None] == jnp.arange(experts, dtype=jnp.int32)[None, :]).astype(
        jnp.int32
    )
    earlier = jnp.cumsum(onehot, axis=0) - onehot
    slot_index = jnp.sum(earlier * onehot, axis=1)
    return (flat_owner * capacity + slot_index).reshape(block_owner.shape)


def place_matrix(positions, slots_total):
    matches = positions[None, :, :] == jnp.arange(slots_total, dtype=jnp.int32)[:, None, None]
    return jnp.any(matches, axis=2).astype(jnp.bfloat16)


def local_sparse(
    queries,
    fresh_key_value,
    key_value_cache,
    request_page_index,
    cache_length_rows,
    residual,
    w_out,
    gain_in,
    route_ids,
    route_weights,
    expert_home,
    w_gate,
    w_up,
    w_down,
    gain_out,
):
    tp_size = lax.axis_size("tp")
    req_size = lax.axis_size("req")
    tp_index = lax.axis_index("tp")
    model_width = residual.shape[1]
    tokens_here = residual.shape[0]
    quarter = tokens_here // tp_size
    experts = expert_home.shape[0]
    capacity = min(quarter, max(2, 2 * quarter * TOPK // experts))
    context = group_attention(
        queries, fresh_key_value, key_value_cache, request_page_index, cache_length_rows
    )
    head_terms = jnp.dot(context, w_out, preferred_element_type=jnp.float32)
    state = residual.astype(jnp.float32) + lax.psum(head_terms, "tp")
    owners = jnp.sum(
        jnp.where(
            route_ids[:, :, None] == jnp.arange(experts, dtype=jnp.int32)[None, None, :],
            expert_home[None, None, :],
            0,
        ),
        axis=2,
    )
    shares = route_weights / jnp.sum(route_weights, axis=1, keepdims=True)
    own_start = tp_index * quarter
    own_state = lax.dynamic_slice_in_dim(state, own_start, quarter, 0)
    own_shares = lax.dynamic_slice_in_dim(shares, own_start, quarter, 0)
    normed_all = rms_scale(state, gain_in).astype(jnp.bfloat16)
    positions_all = jax.vmap(lambda block_owner: slot_positions(block_owner, experts, capacity))(
        owners.reshape(tp_size, quarter, TOPK)
    )
    placing = jax.vmap(lambda positions: place_matrix(positions, experts * capacity))(positions_all)
    outgoing = jnp.einsum(
        "qmi,qid->qmd",
        placing,
        normed_all.reshape(tp_size, quarter, model_width),
        preferred_element_type=jnp.float32,
    )
    outgoing = outgoing.astype(jnp.bfloat16).reshape(tp_size, experts, capacity, model_width)
    incoming = lax.all_to_all(outgoing, "req", split_axis=1, concat_axis=1, tiled=True)
    own_positions = lax.dynamic_index_in_dim(positions_all, tp_index, 0, keepdims=False)
    expert_rows = incoming.reshape(-1, model_width)
    gate_proj = jnp.dot(expert_rows, w_gate[0], preferred_element_type=jnp.float32)
    up_proj = jnp.dot(expert_rows, w_up[0], preferred_element_type=jnp.float32)
    inner_units = (jax.nn.silu(gate_proj) * up_proj).astype(jnp.bfloat16)
    summed = lax.psum_scatter(
        jnp.dot(inner_units, w_down[0], preferred_element_type=jnp.float32).astype(jnp.bfloat16),
        "tp",
        scatter_dimension=0,
        tiled=True,
    )
    results = summed.reshape(req_size, capacity, model_width)
    returned = lax.all_to_all(results, "req", split_axis=0, concat_axis=0, tiled=True).reshape(
        -1, model_width
    )
    picked = returned[own_positions]
    mixture = jnp.sum(own_shares[:, :, None] * picked.astype(jnp.float32), axis=1)
    return rms_scale(own_state + mixture, gain_out).astype(jnp.bfloat16)


ALL = ("req", "tp")
MASKED = -1e30
LANES = 128
MIB = 1024 * 1024
SMALL = pltpu.CompilerParams(vmem_limit_bytes=8 * MIB)


def vmem():
    return pl.BlockSpec(memory_space=pltpu.VMEM)


def smem():
    return pl.BlockSpec(memory_space=pltpu.SMEM)


def hbm():
    return pl.BlockSpec(memory_space=pltpu.HBM)


def stay(value):
    return pltpu.with_memory_space_constraint(value, pltpu.HBM)


def barrier(*values):
    return lax.optimization_barrier(values)


def multiplicity(page_rows, length, pool_pages, page_tokens):
    rows = page_rows[0].shape[0]
    lane = lax.broadcasted_iota(jnp.int32, (rows, page_tokens), 1)
    parts = []
    for page in range(pool_pages):
        count = jnp.zeros((rows, page_tokens), jnp.float32)
        for slot, named in enumerate(page_rows):
            hit = (named == page) & (lane + slot * page_tokens < length)
            count = count + jnp.where(hit, 1.0, 0.0)
        parts.append(count)
    return jnp.concatenate(parts, axis=1)


def pack_shares(ids, routed, home_ref):
    groups = home_ref.shape[0]
    choices, tokens = ids.shape
    spot = lax.broadcasted_iota(jnp.int32, (groups, tokens), 0)
    shares = routed / jnp.sum(routed, axis=0, keepdims=True)
    by_expert = jnp.zeros((groups, tokens), jnp.float32)
    for k in range(choices):
        by_expert = by_expert + jnp.where(spot == ids[k : k + 1, :], shares[k : k + 1, :], 0.0)
    by_home = jnp.zeros((groups, tokens), jnp.float32)
    for e in range(groups):
        by_home = by_home + jnp.where(spot == home_ref[e], by_expert[e : e + 1, :], 0.0)
    rounded = by_home.astype(jnp.bfloat16).astype(jnp.float32)
    tall = jnp.concatenate(
        [rounded, by_home - rounded, jnp.zeros((LANES - 2 * groups, tokens), jnp.float32)], axis=0
    )
    square = jnp.concatenate([tall, jnp.zeros((LANES, LANES - tokens), jnp.float32)], axis=1)
    return jnp.transpose(square)


def count_positions(pages_ref, lengths_ref, pool_pages, page_tokens, count_ref):
    slots, requests = pages_ref.shape
    decodes = requests - 1
    row = lax.broadcasted_iota(jnp.int32, (decodes, page_tokens), 0)

    def by_row(read):
        value = jnp.zeros((decodes, page_tokens), jnp.int32)
        for j in range(decodes):
            value = jnp.where(row == j, read(j + 1), value)
        return value

    full = lambda scalar: jnp.full((decodes, page_tokens), scalar, jnp.int32)
    first = multiplicity(
        [full(pages_ref[s, 0]) for s in range(slots)], full(lengths_ref[0]), pool_pages, page_tokens
    )
    later = multiplicity(
        [by_row(lambda j, s=s: pages_ref[s, j]) for s in range(slots)],
        by_row(lambda j: lengths_ref[j]),
        pool_pages,
        page_tokens,
    )
    count_ref[...] = jnp.concatenate([first] * (PRE_DEV // decodes) + [later], axis=0)


def attend(start, q_ref, fresh_ref, cache_ref, count_ref, context_ref):
    rows = context_ref.shape[0]
    tokens = q_ref.shape[0]
    kv_heads = fresh_ref.shape[1] // (2 * HEAD_WIDTH)
    group = q_ref.shape[1] // (HEAD_WIDTH * kv_heads)
    query_place = start + lax.broadcasted_iota(jnp.int32, (rows, tokens), 0)
    key_place = lax.broadcasted_iota(jnp.int32, (rows, tokens), 1)
    seen = (key_place == query_place) | ((key_place <= query_place) & (query_place < PRE_DEV))
    seen = jnp.concatenate([jnp.where(seen, 1.0, 0.0)] * group, axis=0)
    visible = jnp.concatenate([count_ref[pl.ds(start, rows), :]] * group, axis=0)
    scale = HEAD_WIDTH**-0.5
    contract_last = (((1,), (1,)), ((), ()))
    for k in range(kv_heads):
        key_at, value_at = 2 * k * HEAD_WIDTH, (2 * k + 1) * HEAD_WIDTH
        heads = [k * group + g for g in range(group)]
        query = jnp.concatenate(
            [q_ref[pl.ds(start, rows), h * HEAD_WIDTH : (h + 1) * HEAD_WIDTH] for h in heads],
            axis=0,
        )
        keys = cache_ref[:, :, key_at : key_at + HEAD_WIDTH].reshape(-1, HEAD_WIDTH)
        values = cache_ref[:, :, value_at : value_at + HEAD_WIDTH].reshape(-1, HEAD_WIDTH)
        old = lax.dot_general(query, keys, contract_last, preferred_element_type=jnp.float32)
        new = lax.dot_general(
            query,
            fresh_ref[:, key_at : key_at + HEAD_WIDTH],
            contract_last,
            preferred_element_type=jnp.float32,
        )
        old = jnp.where(visible > 0, old * scale, MASKED)
        new = jnp.where(seen > 0, new * scale, MASKED)
        peak = jnp.maximum(
            jnp.max(old, axis=1, keepdims=True), jnp.max(new, axis=1, keepdims=True)
        )
        old = jnp.exp(old - peak) * visible
        new = jnp.exp(new - peak) * seen
        inverse = 1.0 / (
            jnp.sum(old, axis=1, keepdims=True) + jnp.sum(new, axis=1, keepdims=True)
        )
        mixed = jnp.dot(
            (old * inverse).astype(jnp.bfloat16), values, preferred_element_type=jnp.float32
        ) + jnp.dot(
            (new * inverse).astype(jnp.bfloat16),
            fresh_ref[:, value_at : value_at + HEAD_WIDTH],
            preferred_element_type=jnp.float32,
        )
        mixed = mixed.astype(jnp.bfloat16)
        for g, h in enumerate(heads):
            context_ref[:, h * HEAD_WIDTH : (h + 1) * HEAD_WIDTH] = mixed[g * rows : (g + 1) * rows]


OUT_BLOCK = 512
W_PIECES = 4


def other_kernel(
    pages_ref, lengths_ref, tp_ref, group_ref, q_hbm, fresh_hbm, cache_hbm, w_hbm,
    send_ref, q_ref, fresh_ref, cache_ref, w_ref, count_ref, context_ref, terms_ref, sems,
):
    moves = [(q_hbm, q_ref), (fresh_hbm, fresh_ref), (cache_hbm, cache_ref)]
    depth = w_ref.shape[0] // W_PIECES
    parts = [slice(i * depth, (i + 1) * depth) for i in range(W_PIECES)]
    moves += [(w_hbm.at[part, :], w_ref.at[part, :]) for part in parts]
    fetches = [
        pltpu.make_async_copy(source, target, sems.at[i])
        for i, (source, target) in enumerate(moves)
    ]
    for fetch in fetches:
        fetch.start()
    half = context_ref.shape[0]
    start = pl.multiple_of((1 - tp_ref[0]) * half, half)
    count_positions(pages_ref, lengths_ref, cache_ref.shape[0], cache_ref.shape[1], count_ref)
    for fetch in fetches[:3]:
        fetch.wait()
    attend(start, q_ref, fresh_ref, cache_ref, count_ref, context_ref)
    for i, part in enumerate(parts):
        fetches[3 + i].wait()
        for at in range(0, w_ref.shape[1], OUT_BLOCK):
            cols = slice(at, at + OUT_BLOCK)
            terms = jnp.dot(
                context_ref[:, part], w_ref[part, cols], preferred_element_type=jnp.float32
            )
            terms_ref[:, cols] = terms if i == 0 else terms_ref[:, cols] + terms
    send_ref[...] = terms_ref[...].astype(jnp.bfloat16)


def other_terms(pages, lengths, tp_index, group, queries, fresh, cache, w_out):
    half = queries.shape[0] // 2
    moved = (queries, fresh, cache, w_out)
    return pl.pallas_call(
        other_kernel,
        out_shape=(jax.ShapeDtypeStruct((half, w_out.shape[1]), jnp.bfloat16),)
        + tuple(jax.ShapeDtypeStruct(v.shape, v.dtype) for v in moved),
        in_specs=[smem()] * 4 + [hbm()] * 4,
        out_specs=(vmem(),) * 5,
        scratch_shapes=[
            pltpu.VMEM((queries.shape[0], cache.shape[0] * cache.shape[1]), jnp.float32),
            pltpu.VMEM((half, queries.shape[1]), jnp.bfloat16),
            pltpu.VMEM((half, w_out.shape[1]), jnp.float32),
            pltpu.SemaphoreType.DMA((3 + W_PIECES,)),
        ],
        compiler_params=pltpu.CompilerParams(vmem_limit_bytes=16 * MIB),
        name="other_terms",
    )(stay(pages), stay(lengths), tp_index, group, *[stay(v) for v in moved])


def own_kernel(
    pages_ref, lengths_ref, tp_ref, home_ref, q_ref, fresh_ref, cache_ref, w_ref,
    residual_hbm, ids_hbm, routed_hbm, gain_hbm,
    own_ref, pack_ref, gain_ref, residual_ref, ids_ref, routed_ref, count_ref, context_ref, every_ref, sems,
):
    moves = (
        (ids_hbm, ids_ref), (routed_hbm, routed_ref), (residual_hbm, residual_ref),
        (gain_hbm, gain_ref),
    )
    fetches = [
        pltpu.make_async_copy(source, target, sems.at[i])
        for i, (source, target) in enumerate(moves)
    ]
    for fetch in fetches:
        fetch.start()
    half = context_ref.shape[0]
    start = pl.multiple_of(tp_ref[0] * half, half)
    count_positions(pages_ref, lengths_ref, cache_ref.shape[0], cache_ref.shape[1], count_ref)
    attend(start, q_ref, fresh_ref, cache_ref, count_ref, context_ref)
    for fetch in fetches:
        fetch.wait()
    every_ref[...] = pack_shares(ids_ref[...], routed_ref[...], home_ref)
    pack_ref[...] = every_ref[pl.ds(start, half), :].astype(jnp.bfloat16)
    for at in range(0, w_ref.shape[1], OUT_BLOCK):
        cols = slice(at, at + OUT_BLOCK)
        own_ref[:, cols] = residual_ref[pl.ds(start, half), cols].astype(jnp.float32) + jnp.dot(
            context_ref[...], w_ref[:, cols], preferred_element_type=jnp.float32
        )


def own_terms(pages, lengths, tp_index, home, kept, residual, ids, routed, gain):
    tokens, width = residual.shape
    half = tokens // 2
    queries, _, cache, _ = kept
    moved = (residual, ids, routed)
    return pl.pallas_call(
        own_kernel,
        out_shape=(
            jax.ShapeDtypeStruct((half, width), jnp.float32),
            jax.ShapeDtypeStruct((half, LANES), jnp.bfloat16),
            jax.ShapeDtypeStruct(gain.shape, gain.dtype),
        ),
        in_specs=[smem()] * 4 + [vmem()] * 4 + [hbm()] * 4,
        out_specs=(vmem(),) * 3,
        scratch_shapes=[pltpu.VMEM(v.shape, v.dtype) for v in moved]
        + [
            pltpu.VMEM((tokens, cache.shape[0] * cache.shape[1]), jnp.float32),
            pltpu.VMEM((half, queries.shape[1]), jnp.bfloat16),
            pltpu.VMEM((LANES, LANES), jnp.float32),
            pltpu.SemaphoreType.DMA((4,)),
        ],
        compiler_params=pltpu.CompilerParams(vmem_limit_bytes=16 * MIB),
        name="own_terms",
    )(stay(pages), stay(lengths), tp_index, stay(home), *kept, *[stay(v) for v in moved + (gain,)])


LATE = pl.CostEstimate(flops=3 * 10**10, bytes_accessed=1 << 20, transcendentals=0)


def norm_kernel(own_ref, got_ref, pack_ref, gain_ref, state_ref, far_ref, near_ref):
    state = own_ref[...] + got_ref[...].astype(jnp.float32)
    state_ref[...] = state
    normed = rms_scale(state, gain_ref[...]).astype(jnp.bfloat16)
    width = state.shape[1]
    far = far_ref.shape[0]
    far_ref[:, :width] = normed[:far]
    far_ref[:, width:] = pack_ref[:far, :]
    near_ref[:, :width] = normed[far:]
    near_ref[:, width:] = pack_ref[far:, :]


def norm_rows(own, got, pack, gain, far):
    rows, width = own.shape
    return pl.pallas_call(
        norm_kernel,
        out_shape=(
            jax.ShapeDtypeStruct((rows, width), jnp.float32),
            jax.ShapeDtypeStruct((far, width + LANES), jnp.bfloat16),
            jax.ShapeDtypeStruct((rows - far, width + LANES), jnp.bfloat16),
        ),
        in_specs=[vmem()] * 4,
        out_specs=(vmem(),) * 3,
        compiler_params=SMALL,
        name="norm_rows",
    )(own, got, pack, gain)


def join_kernel(starts, *refs):
    out_ref = refs[-1]
    at = 0
    for start, piece in zip(starts, refs[:-1]):
        height = piece.shape[0] - start
        out_ref[at : at + height, :] = piece[start:, :]
        at += height


def join_rows(pieces, starts, cost, name):
    height = sum(piece.shape[0] - start for piece, start in zip(pieces, starts))
    return pl.pallas_call(
        functools.partial(join_kernel, starts),
        out_shape=jax.ShapeDtypeStruct((height, pieces[0].shape[1]), jnp.bfloat16),
        in_specs=[vmem()] * len(pieces),
        out_specs=vmem(),
        compiler_params=SMALL,
        cost_estimate=cost,
        name=name,
    )(*pieces)


def hidden_units(groups, group_ref, x_ref, w_refs, h_ref, ready):
    rows = x_ref.shape[0]
    width = w_refs[0].shape[0]
    hidden = h_ref.shape[1] // 2
    lane = lax.broadcasted_iota(jnp.int32, (rows, LANES), 1)
    packed = x_ref[:, width:].astype(jnp.float32)
    for e in (1, 0):
        group = group_ref[0] ^ e
        share = jnp.sum(
            jnp.where((lane == group) | (lane == group + groups), packed, 0.0),
            axis=1,
            keepdims=True,
        )
        ready(e)
        both = jnp.dot(x_ref[:, :width], w_refs[e][...], preferred_element_type=jnp.float32)
        gate, up = both[:, :hidden], both[:, hidden:]
        h_ref[:, e * hidden : (e + 1) * hidden] = (
            share * up * (gate / (1.0 + jnp.exp(-gate)))
        ).astype(jnp.bfloat16)


DOWN_BLOCK = 512


def gather_pieces(pieces, x_ref):
    at = 0
    for piece in pieces:
        x_ref[at : at + piece.shape[0], :] = piece[...]
        at += piece.shape[0]
    if at < x_ref.shape[0]:
        x_ref[at:, :] = jnp.zeros((x_ref.shape[0] - at, x_ref.shape[1]), jnp.bfloat16)


def near_kernel(
    groups, group_ref, r0, r1, r2, r3, far_ref, z1_ref, wg1, wu1, wg0, wu0, wd0, wd1,
    out_ref, z1_out_ref, w0_ref, w1_ref, down_ref, x_ref, h_ref, sems,
):
    hidden = wg0.shape[1]
    fetches = [
        pltpu.make_async_copy(source, target, sems.at[i])
        for i, (source, target) in enumerate(
            (
                (wg0, w0_ref.at[:, :hidden]),
                (wu0, w0_ref.at[:, hidden:]),
                (wd0, down_ref.at[:hidden, :]),
                (wd1, down_ref.at[hidden:, :]),
                (wg1, w1_ref.at[:, :hidden]),
                (wu1, w1_ref.at[:, hidden:]),
            )
        )
    ]
    for fetch in fetches:
        fetch.start()
    gather_pieces((r0, r1, r2, r3, far_ref, z1_ref), x_ref)

    def ready(e):
        for fetch in fetches[4:] if e else fetches[:2]:
            fetch.wait()

    hidden_units(groups, group_ref, x_ref, (w0_ref, w1_ref), h_ref, ready)
    fetches[2].wait()
    fetches[3].wait()
    height = out_ref.shape[0]
    for col in range(0, down_ref.shape[1], DOWN_BLOCK):
        cols = slice(col, col + DOWN_BLOCK)
        down = jnp.dot(h_ref[...], down_ref[:, cols], preferred_element_type=jnp.float32)
        out_ref[:, cols] = down[:height]
        z1_out_ref[:, cols] = down[height : height + z1_ref.shape[0]].astype(jnp.bfloat16)


def expert_cost(rows, width, hidden):
    return pl.CostEstimate(
        flops=12 * rows * width * hidden,
        bytes_accessed=12 * width * hidden,
        transcendentals=2 * rows * hidden,
    )


def near_rows(groups, group, rows, far, near_z, weights, partner_weights):
    height = 4 * rows[0].shape[0] + far.shape[0]
    padded = -(-(height + near_z.shape[0]) // 16) * 16
    width, hidden = weights[0].shape
    wg0, wu0, wd0 = weights
    wg1, wu1, wd1 = partner_weights
    return pl.pallas_call(
        functools.partial(near_kernel, groups),
        out_shape=(
            jax.ShapeDtypeStruct((height, width), jnp.float32),
            jax.ShapeDtypeStruct((near_z.shape[0], width), jnp.bfloat16),
            jax.ShapeDtypeStruct((width, 2 * hidden), jnp.bfloat16),
            jax.ShapeDtypeStruct((width, 2 * hidden), jnp.bfloat16),
            jax.ShapeDtypeStruct((2 * hidden, width), jnp.bfloat16),
        ),
        in_specs=[smem()] + [vmem()] * 8 + [hbm()] * 4,
        out_specs=(vmem(),) * 5,
        scratch_shapes=[
            pltpu.VMEM((padded, width + LANES), jnp.bfloat16),
            pltpu.VMEM((padded, 2 * hidden), jnp.bfloat16),
            pltpu.SemaphoreType.DMA((6,)),
        ],
        compiler_params=pltpu.CompilerParams(vmem_limit_bytes=24 * MIB),
        cost_estimate=expert_cost(height, width, hidden),
        name="near_rows",
    )(group, *rows, far, near_z, wg1, wu1, *[stay(w) for w in (wg0, wu0, wd0, wd1)])


def piece_kernel(groups, count, group_ref, *refs):
    pieces, (w0_ref, w1_ref, down_ref) = refs[:count], refs[count : count + 3]
    outs, (x_ref, h_ref) = refs[count + 3 : 2 * count + 3], refs[2 * count + 3 :]
    gather_pieces(pieces, x_ref)
    hidden_units(groups, group_ref, x_ref, (w0_ref, w1_ref), h_ref, lambda e: None)
    for col in range(0, down_ref.shape[1], DOWN_BLOCK):
        cols = slice(col, col + DOWN_BLOCK)
        down = jnp.dot(h_ref[...], down_ref[:, cols], preferred_element_type=jnp.float32)
        at = 0
        for out in outs:
            out[:, cols] = down[at : at + out.shape[0]].astype(jnp.bfloat16)
            at += out.shape[0]


def piece_rows(groups, group, pieces, w0, w1, down):
    count = len(pieces)
    height = sum(piece.shape[0] for piece in pieces)
    padded = -(-height // 16) * 16
    width, hidden = w1.shape[0], w1.shape[1] // 2
    return pl.pallas_call(
        functools.partial(piece_kernel, groups, count),
        out_shape=tuple(
            jax.ShapeDtypeStruct((piece.shape[0], width), jnp.bfloat16) for piece in pieces
        ),
        in_specs=[smem()] + [vmem()] * (count + 3),
        out_specs=(vmem(),) * count,
        scratch_shapes=[
            pltpu.VMEM((padded, width + LANES), jnp.bfloat16),
            pltpu.VMEM((padded, 2 * hidden), jnp.bfloat16),
        ],
        compiler_params=pltpu.CompilerParams(vmem_limit_bytes=24 * MIB),
        cost_estimate=expert_cost(height, width, hidden),
        name="piece_rows",
    )(group, *pieces, w0, w1, down)


def plane_sum_kernel(near_ref, g1, g2, g3, m1, m2, m3):
    far = m1.shape[0]
    start = near_ref.shape[0] - 3 * far
    for j, out in enumerate((m1, m2, m3)):
        rows = slice(j * far, (j + 1) * far)
        total = near_ref[start + j * far : start + (j + 1) * far, :]
        for got in (g1, g2, g3):
            total = total + got[rows, :].astype(jnp.float32)
        out[...] = total.astype(jnp.bfloat16)


def plane_sum(near, got):
    far, width = got[0].shape[0] // 3, got[0].shape[1]
    return pl.pallas_call(
        plane_sum_kernel,
        out_shape=tuple(jax.ShapeDtypeStruct((far, width), jnp.bfloat16) for _ in range(3)),
        in_specs=[vmem()] * 4,
        out_specs=(vmem(),) * 3,
        compiler_params=SMALL,
        name="plane_sum",
    )(near, *got)


def first_sum_kernel(rows, near_ref, g1, out_ref):
    near = g1.shape[0] // 4
    for i in range(4):
        there = slice(i * near, (i + 1) * near)
        out_ref[there, :] = near_ref[(i + 1) * rows - near : (i + 1) * rows, :] + g1[
            there, :
        ].astype(jnp.float32)


def first_sum(near, got, rows):
    return pl.pallas_call(
        functools.partial(first_sum_kernel, rows),
        out_shape=jax.ShapeDtypeStruct(got.shape, jnp.float32),
        in_specs=[vmem()] * 2,
        out_specs=vmem(),
        compiler_params=SMALL,
        cost_estimate=LATE,
        name="first_sum",
    )(near, got)


def column_sum_kernel(near_ref, first_ref, g2, g3, own_ref, m1, m2, m3):
    rows = own_ref.shape[0]
    near = first_ref.shape[0] // 4
    far = rows - near
    for i, out in enumerate((own_ref, m1, m2, m3)):
        out[:far, :] = near_ref[i * rows : i * rows + far, :].astype(out.dtype)
        total = first_ref[i * near : (i + 1) * near, :]
        for got in (g2, g3):
            total = total + got[i * near : (i + 1) * near, :].astype(jnp.float32)
        out[far:, :] = total.astype(out.dtype)


def column_sum(near, first, got, rows):
    width = near.shape[1]
    kinds = (jnp.float32, jnp.bfloat16, jnp.bfloat16, jnp.bfloat16)
    return pl.pallas_call(
        column_sum_kernel,
        out_shape=tuple(jax.ShapeDtypeStruct((rows, width), kind) for kind in kinds),
        in_specs=[vmem()] * 4,
        out_specs=(vmem(),) * 4,
        compiler_params=SMALL,
        cost_estimate=LATE,
        name="column_sum",
    )(near, first, *got)


def total_kernel(state_ref, own_ref, z1, z2, z3, total_ref):
    total_ref[...] = state_ref[...] + own_ref[...]
    far = z1.shape[0]
    part = total_ref[:far, :]
    for got in (z1, z2, z3):
        part = part + got[...].astype(jnp.float32)
    total_ref[:far, :] = part


def total_rows(state, own, column):
    return pl.pallas_call(
        total_kernel,
        out_shape=jax.ShapeDtypeStruct(state.shape, jnp.float32),
        in_specs=[vmem()] * 5,
        out_specs=vmem(),
        compiler_params=SMALL,
        cost_estimate=LATE,
        name="total_rows",
    )(state, own, *column)


def final_kernel(total_ref, p1, p2, p3, gain_ref, out_ref):
    total = total_ref[...]
    for got in (p1, p2, p3):
        total = total + got[...].astype(jnp.float32)
    out_ref[...] = rms_scale(total, gain_ref[...]).astype(jnp.bfloat16)


def final_rows(total, plane, gain):
    return pl.pallas_call(
        final_kernel,
        out_shape=jax.ShapeDtypeStruct(total.shape, jnp.bfloat16),
        in_specs=[vmem()] * 5,
        out_specs=vmem(),
        compiler_params=SMALL,
        name="final_rows",
    )(total, *plane, gain)


def place(z, y, c, x):
    return ((z * 2 + y) * 2 + c) * 2 + x


def swap(value, dz, dy, dc, dx):
    pairs = [
        (place(z, y, c, x), place(z ^ dz, y ^ dy, c ^ dc, x ^ dx))
        for z in range(4)
        for y in range(2)
        for c in range(2)
        for x in range(2)
    ]
    return lax.ppermute(value, ALL, pairs)


PLANE = ((0, 0), (1, 1), (0, 1), (1, 0))


def swap_z(pieces):
    return tuple(swap(piece, d, 0, 0, 0) for d, piece in zip((1, 2, 3), pieces))


def swap_plane(pieces):
    return tuple(swap(piece, 0, dy, 0, dx) for (dy, dx), piece in zip(PLANE[1:], pieces))


def local_dense(
    queries, fresh_key_value, key_value_cache, request_page_index, cache_length_rows, residual,
    w_out, gain_in, route_ids, route_weights, expert_home, w_gate, w_up, w_down, gain_out,
):
    tp_index = lax.axis_index("tp")
    req_index = lax.axis_index("req")
    tokens, width = residual.shape
    half = tokens // 2
    far = half * 3 // 4
    groups = expert_home.shape[0]
    weights = (w_gate[0], w_up[0], w_down[0])
    partner_weights = tuple(swap(stay(w), 0, 0, 1, 0) for w in weights)
    group = req_index.reshape(1)
    tp_index, pages = tp_index.reshape(1), request_page_index.T
    sent, *kept = other_terms(
        pages, cache_length_rows, tp_index, group, queries, fresh_key_value, key_value_cache, w_out
    )
    own_state, pack, last_gain = own_terms(
        pages, cache_length_rows, tp_index, expert_home, kept, residual, route_ids.T,
        route_weights.T, gain_out[None, :],
    )
    got, partner_weights = barrier(swap(sent, 0, 0, 0, 1), partner_weights)
    state, far_rows, last_rows = norm_rows(own_state, got, pack, gain_in[None, :], far)
    rows = join_rows((far_rows, last_rows), (0, 0), LATE, "own_rows")
    z_rows = swap_z((far_rows,) * 3)
    onward_plane = join_rows(z_rows, (0, 0, 0), LATE, "onward_plane")
    plane_rows, far_pieces = barrier(swap_plane((rows,) * 3), onward_plane)
    plane_rows = (rows,) + plane_rows
    onward_z = join_rows(plane_rows, (far,) * 4, None, "onward_z")
    z_pieces = swap_z((onward_z,) * 3)
    plane_pieces = swap_plane((onward_plane,) * 3)
    near, near_part, *kept = near_rows(
        groups, group, plane_rows, far_pieces, z_pieces[0], weights, partner_weights
    )
    parts = piece_rows(groups, group, z_pieces[1:] + plane_pieces, *kept)
    z_parts, plane_parts = swap_z((near_part,) + parts[:2]), swap_plane(parts[2:])
    first = first_sum(near, z_parts[0], half)
    plane_parts, first = barrier(plane_parts, first)
    far_sums = plane_sum(near, plane_parts)
    last_parts, far_sums = barrier(z_parts[1:], far_sums)
    own, *near_sums = column_sum(near, first, last_parts, half)
    total = total_rows(state, own, swap_z(far_sums))
    last_plane, total = barrier(swap_plane(near_sums), total)
    return final_rows(total, last_plane, last_gain)


def solution(mesh):
    dense = mesh.shape["req"] == 16 and mesh.shape["tp"] == 2
    return jax.shard_map(
        local_dense if dense else local_sparse,
        mesh=mesh,
        in_specs=(
            P("req", "tp"),
            P("req", "tp"),
            P("req", None, "tp"),
            P("req", None),
            P("req"),
            P("req", None),
            P("tp", None),
            P(),
            P("req", None),
            P("req", None),
            P(),
            P("req", None, "tp"),
            P("req", None, "tp"),
            P("req", "tp", None),
            P(),
        ),
        out_specs=P(("req", "tp"), None),
        check_vma=False,
    )
```

```python
import functools

import jax
import jax.numpy as jnp
from jax import lax
from jax.experimental import pallas as pl
from jax.experimental.pallas import tpu as pltpu
from jax.sharding import PartitionSpec as P

HEAD_WIDTH = 128
TOPK = 8
PRE_DEV = 56


EPSILON = 1e-06


def rms_scale(value_rows, gain_row):
    mean_square = jnp.mean(value_rows * value_rows, axis=-1, keepdims=True)
    return value_rows * lax.rsqrt(mean_square + EPSILON) * gain_row


def softmax_rounded(scores):
    row_peak = jnp.max(scores, axis=-1, keepdims=True)
    weights = jnp.exp(scores - row_peak)
    return (weights / jnp.sum(weights, axis=-1, keepdims=True)).astype(jnp.bfloat16)


def group_attention(queries, fresh_key_value, page_pool, page_rows, lengths):
    tokens_here = queries.shape[0]
    kv_heads = fresh_key_value.shape[1] // (2 * HEAD_WIDTH)
    group_size = queries.shape[1] // (HEAD_WIDTH * kv_heads)
    score_scale = HEAD_WIDTH ** (-0.5)
    split_query = queries.reshape(tokens_here, kv_heads, group_size, HEAD_WIDTH)
    fresh_kv = fresh_key_value.reshape(tokens_here, kv_heads, 2, HEAD_WIDTH)
    gathered_pages = page_pool[page_rows]
    cached = gathered_pages.reshape(page_rows.shape[0], -1, kv_heads, 2, HEAD_WIDTH)
    places = jnp.arange(cached.shape[1], dtype=jnp.int32)
    prefill_query = split_query[:PRE_DEV]
    prefill_fresh = fresh_kv[:PRE_DEV]
    cache_scores = (
        jnp.einsum(
            "ikgd,ckd->kgic", prefill_query, cached[0, :, :, 0], preferred_element_type=jnp.float32
        )
        * score_scale
    )
    cache_scores = jnp.where(places < lengths[0], cache_scores, -jnp.inf)
    block_scores = (
        jnp.einsum(
            "ikgd,jkd->kgij",
            prefill_query,
            prefill_fresh[:, :, 0],
            preferred_element_type=jnp.float32,
        )
        * score_scale
    )
    causal = jnp.arange(PRE_DEV)[:, None] >= jnp.arange(PRE_DEV)[None, :]
    block_scores = jnp.where(causal, block_scores, -jnp.inf)
    prefill_probs = softmax_rounded(jnp.concatenate([cache_scores, block_scores], axis=3))
    prefill_values = jnp.concatenate([cached[0, :, :, 1], prefill_fresh[:, :, 1]], axis=0)
    prefill_out = jnp.einsum(
        "kgic,ckd->ikgd", prefill_probs, prefill_values, preferred_element_type=jnp.float32
    )
    decode_query = split_query[PRE_DEV:]
    decode_fresh = fresh_kv[PRE_DEV:]
    decode_scores = (
        jnp.einsum(
            "rkgd,rckd->rkgc", decode_query, cached[1:, :, :, 0], preferred_element_type=jnp.float32
        )
        * score_scale
    )
    decode_scores = jnp.where(
        places[None, None, None, :] < lengths[1:, None, None, None], decode_scores, -jnp.inf
    )
    own_scores = (
        jnp.einsum(
            "rkgd,rkd->rkg", decode_query, decode_fresh[:, :, 0], preferred_element_type=jnp.float32
        )[..., None]
        * score_scale
    )
    decode_probs = softmax_rounded(jnp.concatenate([decode_scores, own_scores], axis=3))
    decode_values = jnp.concatenate([cached[1:, :, :, 1], decode_fresh[:, None, :, 1]], axis=1)
    decode_out = jnp.einsum(
        "rkgc,rckd->rkgd", decode_probs, decode_values, preferred_element_type=jnp.float32
    )
    joined = jnp.concatenate([prefill_out, decode_out], axis=0)
    return joined.reshape(tokens_here, -1).astype(jnp.bfloat16)


def slot_positions(block_owner, experts, capacity):
    flat_owner = block_owner.reshape(-1)
    onehot = (flat_owner[:, None] == jnp.arange(experts, dtype=jnp.int32)[None, :]).astype(
        jnp.int32
    )
    earlier = jnp.cumsum(onehot, axis=0) - onehot
    slot_index = jnp.sum(earlier * onehot, axis=1)
    return (flat_owner * capacity + slot_index).reshape(block_owner.shape)


def place_matrix(positions, slots_total):
    matches = positions[None, :, :] == jnp.arange(slots_total, dtype=jnp.int32)[:, None, None]
    return jnp.any(matches, axis=2).astype(jnp.bfloat16)


def local_sparse(
    queries,
    fresh_key_value,
    key_value_cache,
    request_page_index,
    cache_length_rows,
    residual,
    w_out,
    gain_in,
    route_ids,
    route_weights,
    expert_home,
    w_gate,
    w_up,
    w_down,
    gain_out,
):
    tp_size = lax.axis_size("tp")
    req_size = lax.axis_size("req")
    tp_index = lax.axis_index("tp")
    model_width = residual.shape[1]
    tokens_here = residual.shape[0]
    quarter = tokens_here // tp_size
    experts = expert_home.shape[0]
    capacity = min(quarter, max(2, 2 * quarter * TOPK // experts))
    context = group_attention(
        queries, fresh_key_value, key_value_cache, request_page_index, cache_length_rows
    )
    head_terms = jnp.dot(context, w_out, preferred_element_type=jnp.float32)
    state = residual.astype(jnp.float32) + lax.psum(head_terms, "tp")
    owners = jnp.sum(
        jnp.where(
            route_ids[:, :, None] == jnp.arange(experts, dtype=jnp.int32)[None, None, :],
            expert_home[None, None, :],
            0,
        ),
        axis=2,
    )
    shares = route_weights / jnp.sum(route_weights, axis=1, keepdims=True)
    own_start = tp_index * quarter
    own_state = lax.dynamic_slice_in_dim(state, own_start, quarter, 0)
    own_shares = lax.dynamic_slice_in_dim(shares, own_start, quarter, 0)
    normed_all = rms_scale(state, gain_in).astype(jnp.bfloat16)
    positions_all = jax.vmap(lambda block_owner: slot_positions(block_owner, experts, capacity))(
        owners.reshape(tp_size, quarter, TOPK)
    )
    placing = jax.vmap(lambda positions: place_matrix(positions, experts * capacity))(positions_all)
    outgoing = jnp.einsum(
        "qmi,qid->qmd",
        placing,
        normed_all.reshape(tp_size, quarter, model_width),
        preferred_element_type=jnp.float32,
    )
    outgoing = outgoing.astype(jnp.bfloat16).reshape(tp_size, experts, capacity, model_width)
    incoming = lax.all_to_all(outgoing, "req", split_axis=1, concat_axis=1, tiled=True)
    own_positions = lax.dynamic_index_in_dim(positions_all, tp_index, 0, keepdims=False)
    expert_rows = incoming.reshape(-1, model_width)
    gate_proj = jnp.dot(expert_rows, w_gate[0], preferred_element_type=jnp.float32)
    up_proj = jnp.dot(expert_rows, w_up[0], preferred_element_type=jnp.float32)
    inner_units = (jax.nn.silu(gate_proj) * up_proj).astype(jnp.bfloat16)
    summed = lax.psum_scatter(
        jnp.dot(inner_units, w_down[0], preferred_element_type=jnp.float32).astype(jnp.bfloat16),
        "tp",
        scatter_dimension=0,
        tiled=True,
    )
    results = summed.reshape(req_size, capacity, model_width)
    returned = lax.all_to_all(results, "req", split_axis=0, concat_axis=0, tiled=True).reshape(
        -1, model_width
    )
    picked = returned[own_positions]
    mixture = jnp.sum(own_shares[:, :, None] * picked.astype(jnp.float32), axis=1)
    return rms_scale(own_state + mixture, gain_out).astype(jnp.bfloat16)


ALL = ("req", "tp")
MASKED = -1e30
LANES = 128
MIB = 1024 * 1024
SMALL = pltpu.CompilerParams(vmem_limit_bytes=8 * MIB)


def vmem():
    return pl.BlockSpec(memory_space=pltpu.VMEM)


def smem():
    return pl.BlockSpec(memory_space=pltpu.SMEM)


def hbm():
    return pl.BlockSpec(memory_space=pltpu.HBM)


def stay(value):
    return pltpu.with_memory_space_constraint(value, pltpu.HBM)


def barrier(*values):
    return lax.optimization_barrier(values)


def multiplicity(page_rows, length, pool_pages, page_tokens):
    rows = page_rows[0].shape[0]
    lane = lax.broadcasted_iota(jnp.int32, (rows, page_tokens), 1)
    parts = []
    for page in range(pool_pages):
        count = jnp.zeros((rows, page_tokens), jnp.float32)
        for slot, named in enumerate(page_rows):
            hit = (named == page) & (lane + slot * page_tokens < length)
            count = count + jnp.where(hit, 1.0, 0.0)
        parts.append(count)
    return jnp.concatenate(parts, axis=1)


def pack_shares(ids, routed, home_ref):
    groups = home_ref.shape[0]
    choices, tokens = ids.shape
    spot = lax.broadcasted_iota(jnp.int32, (groups, tokens), 0)
    shares = routed / jnp.sum(routed, axis=0, keepdims=True)
    by_expert = jnp.zeros((groups, tokens), jnp.float32)
    for k in range(choices):
        by_expert = by_expert + jnp.where(spot == ids[k : k + 1, :], shares[k : k + 1, :], 0.0)
    by_home = jnp.zeros((groups, tokens), jnp.float32)
    for e in range(groups):
        by_home = by_home + jnp.where(spot == home_ref[e], by_expert[e : e + 1, :], 0.0)
    rounded = by_home.astype(jnp.bfloat16).astype(jnp.float32)
    tall = jnp.concatenate(
        [rounded, by_home - rounded, jnp.zeros((LANES - 2 * groups, tokens), jnp.float32)], axis=0
    )
    square = jnp.concatenate([tall, jnp.zeros((LANES, LANES - tokens), jnp.float32)], axis=1)
    return jnp.transpose(square)


def count_positions(pages_ref, lengths_ref, pool_pages, page_tokens, count_ref):
    slots, requests = pages_ref.shape
    decodes = requests - 1
    row = lax.broadcasted_iota(jnp.int32, (decodes, page_tokens), 0)

    def by_row(read):
        value = jnp.zeros((decodes, page_tokens), jnp.int32)
        for j in range(decodes):
            value = jnp.where(row == j, read(j + 1), value)
        return value

    full = lambda scalar: jnp.full((decodes, page_tokens), scalar, jnp.int32)
    first = multiplicity(
        [full(pages_ref[s, 0]) for s in range(slots)], full(lengths_ref[0]), pool_pages, page_tokens
    )
    later = multiplicity(
        [by_row(lambda j, s=s: pages_ref[s, j]) for s in range(slots)],
        by_row(lambda j: lengths_ref[j]),
        pool_pages,
        page_tokens,
    )
    count_ref[...] = jnp.concatenate([first] * (PRE_DEV // decodes) + [later], axis=0)


def attend(start, q_ref, fresh_ref, cache_ref, count_ref, context_ref):
    rows = context_ref.shape[0]
    tokens = q_ref.shape[0]
    kv_heads = fresh_ref.shape[1] // (2 * HEAD_WIDTH)
    group = q_ref.shape[1] // (HEAD_WIDTH * kv_heads)
    query_place = start + lax.broadcasted_iota(jnp.int32, (rows, tokens), 0)
    key_place = lax.broadcasted_iota(jnp.int32, (rows, tokens), 1)
    seen = (key_place == query_place) | ((key_place <= query_place) & (query_place < PRE_DEV))
    seen = jnp.concatenate([jnp.where(seen, 1.0, 0.0)] * group, axis=0)
    visible = jnp.concatenate([count_ref[pl.ds(start, rows), :]] * group, axis=0)
    scale = HEAD_WIDTH**-0.5
    contract_last = (((1,), (1,)), ((), ()))
    for k in range(kv_heads):
        key_at, value_at = 2 * k * HEAD_WIDTH, (2 * k + 1) * HEAD_WIDTH
        heads = [k * group + g for g in range(group)]
        query = jnp.concatenate(
            [q_ref[pl.ds(start, rows), h * HEAD_WIDTH : (h + 1) * HEAD_WIDTH] for h in heads],
            axis=0,
        )
        keys = cache_ref[:, :, key_at : key_at + HEAD_WIDTH].reshape(-1, HEAD_WIDTH)
        values = cache_ref[:, :, value_at : value_at + HEAD_WIDTH].reshape(-1, HEAD_WIDTH)
        old = lax.dot_general(query, keys, contract_last, preferred_element_type=jnp.float32)
        new = lax.dot_general(
            query,
            fresh_ref[:, key_at : key_at + HEAD_WIDTH],
            contract_last,
            preferred_element_type=jnp.float32,
        )
        old = jnp.where(visible > 0, old * scale, MASKED)
        new = jnp.where(seen > 0, new * scale, MASKED)
        peak = jnp.maximum(
            jnp.max(old, axis=1, keepdims=True), jnp.max(new, axis=1, keepdims=True)
        )
        old = jnp.exp(old - peak) * visible
        new = jnp.exp(new - peak) * seen
        inverse = 1.0 / (
            jnp.sum(old, axis=1, keepdims=True) + jnp.sum(new, axis=1, keepdims=True)
        )
        mixed = jnp.dot(
            (old * inverse).astype(jnp.bfloat16), values, preferred_element_type=jnp.float32
        ) + jnp.dot(
            (new * inverse).astype(jnp.bfloat16),
            fresh_ref[:, value_at : value_at + HEAD_WIDTH],
            preferred_element_type=jnp.float32,
        )
        mixed = mixed.astype(jnp.bfloat16)
        for g, h in enumerate(heads):
            context_ref[:, h * HEAD_WIDTH : (h + 1) * HEAD_WIDTH] = mixed[g * rows : (g + 1) * rows]


OUT_BLOCK = 512
W_PIECES = 4


def other_kernel(
    pages_ref, lengths_ref, tp_ref, group_ref, q_hbm, fresh_hbm, cache_hbm, w_hbm,
    send_ref, q_ref, fresh_ref, cache_ref, w_ref, count_ref, context_ref, terms_ref, sems,
):
    moves = [(q_hbm, q_ref), (fresh_hbm, fresh_ref), (cache_hbm, cache_ref)]
    depth = w_ref.shape[0] // W_PIECES
    parts = [slice(i * depth, (i + 1) * depth) for i in range(W_PIECES)]
    moves += [(w_hbm.at[part, :], w_ref.at[part, :]) for part in parts]
    fetches = [
        pltpu.make_async_copy(source, target, sems.at[i])
        for i, (source, target) in enumerate(moves)
    ]
    for fetch in fetches:
        fetch.start()
    half = context_ref.shape[0]
    start = pl.multiple_of((1 - tp_ref[0]) * half, half)
    count_positions(pages_ref, lengths_ref, cache_ref.shape[0], cache_ref.shape[1], count_ref)
    for fetch in fetches[:3]:
        fetch.wait()
    attend(start, q_ref, fresh_ref, cache_ref, count_ref, context_ref)
    for i, part in enumerate(parts):
        fetches[3 + i].wait()
        for at in range(0, w_ref.shape[1], OUT_BLOCK):
            cols = slice(at, at + OUT_BLOCK)
            terms = jnp.dot(
                context_ref[:, part], w_ref[part, cols], preferred_element_type=jnp.float32
            )
            terms_ref[:, cols] = terms if i == 0 else terms_ref[:, cols] + terms
    send_ref[...] = terms_ref[...].astype(jnp.bfloat16)


def other_terms(pages, lengths, tp_index, group, queries, fresh, cache, w_out):
    half = queries.shape[0] // 2
    moved = (queries, fresh, cache, w_out)
    return pl.pallas_call(
        other_kernel,
        out_shape=(jax.ShapeDtypeStruct((half, w_out.shape[1]), jnp.bfloat16),)
        + tuple(jax.ShapeDtypeStruct(v.shape, v.dtype) for v in moved),
        in_specs=[smem()] * 4 + [hbm()] * 4,
        out_specs=(vmem(),) * 5,
        scratch_shapes=[
            pltpu.VMEM((queries.shape[0], cache.shape[0] * cache.shape[1]), jnp.float32),
            pltpu.VMEM((half, queries.shape[1]), jnp.bfloat16),
            pltpu.VMEM((half, w_out.shape[1]), jnp.float32),
            pltpu.SemaphoreType.DMA((3 + W_PIECES,)),
        ],
        compiler_params=pltpu.CompilerParams(vmem_limit_bytes=16 * MIB),
        name="other_terms",
    )(stay(pages), stay(lengths), tp_index, group, *[stay(v) for v in moved])


def own_kernel(
    pages_ref, lengths_ref, tp_ref, home_ref, q_ref, fresh_ref, cache_ref, w_ref,
    residual_hbm, ids_hbm, routed_hbm, gain_hbm,
    own_ref, pack_ref, gain_ref, residual_ref, ids_ref, routed_ref, count_ref, context_ref, every_ref, sems,
):
    moves = (
        (ids_hbm, ids_ref), (routed_hbm, routed_ref), (residual_hbm, residual_ref),
        (gain_hbm, gain_ref),
    )
    fetches = [
        pltpu.make_async_copy(source, target, sems.at[i])
        for i, (source, target) in enumerate(moves)
    ]
    for fetch in fetches:
        fetch.start()
    half = context_ref.shape[0]
    start = pl.multiple_of(tp_ref[0] * half, half)
    count_positions(pages_ref, lengths_ref, cache_ref.shape[0], cache_ref.shape[1], count_ref)
    attend(start, q_ref, fresh_ref, cache_ref, count_ref, context_ref)
    for fetch in fetches:
        fetch.wait()
    every_ref[...] = pack_shares(ids_ref[...], routed_ref[...], home_ref)
    pack_ref[...] = every_ref[pl.ds(start, half), :].astype(jnp.bfloat16)
    for at in range(0, w_ref.shape[1], OUT_BLOCK):
        cols = slice(at, at + OUT_BLOCK)
        own_ref[:, cols] = residual_ref[pl.ds(start, half), cols].astype(jnp.float32) + jnp.dot(
            context_ref[...], w_ref[:, cols], preferred_element_type=jnp.float32
        )


def own_terms(pages, lengths, tp_index, home, kept, residual, ids, routed, gain):
    tokens, width = residual.shape
    half = tokens // 2
    queries, _, cache, _ = kept
    moved = (residual, ids, routed)
    return pl.pallas_call(
        own_kernel,
        out_shape=(
            jax.ShapeDtypeStruct((half, width), jnp.float32),
            jax.ShapeDtypeStruct((half, LANES), jnp.bfloat16),
            jax.ShapeDtypeStruct(gain.shape, gain.dtype),
        ),
        in_specs=[smem()] * 4 + [vmem()] * 4 + [hbm()] * 4,
        out_specs=(vmem(),) * 3,
        scratch_shapes=[pltpu.VMEM(v.shape, v.dtype) for v in moved]
        + [
            pltpu.VMEM((tokens, cache.shape[0] * cache.shape[1]), jnp.float32),
            pltpu.VMEM((half, queries.shape[1]), jnp.bfloat16),
            pltpu.VMEM((LANES, LANES), jnp.float32),
            pltpu.SemaphoreType.DMA((4,)),
        ],
        compiler_params=pltpu.CompilerParams(vmem_limit_bytes=16 * MIB),
        name="own_terms",
    )(stay(pages), stay(lengths), tp_index, stay(home), *kept, *[stay(v) for v in moved + (gain,)])


LATE = pl.CostEstimate(flops=3 * 10**10, bytes_accessed=1 << 20, transcendentals=0)


def norm_kernel(own_ref, got_ref, pack_ref, gain_ref, state_ref, far_ref, near_ref):
    state = own_ref[...] + got_ref[...].astype(jnp.float32)
    state_ref[...] = state
    normed = rms_scale(state, gain_ref[...]).astype(jnp.bfloat16)
    width = state.shape[1]
    far = far_ref.shape[0]
    far_ref[:, :width] = normed[:far]
    far_ref[:, width:] = pack_ref[:far, :]
    near_ref[:, :width] = normed[far:]
    near_ref[:, width:] = pack_ref[far:, :]


def norm_rows(own, got, pack, gain, far):
    rows, width = own.shape
    return pl.pallas_call(
        norm_kernel,
        out_shape=(
            jax.ShapeDtypeStruct((rows, width), jnp.float32),
            jax.ShapeDtypeStruct((far, width + LANES), jnp.bfloat16),
            jax.ShapeDtypeStruct((rows - far, width + LANES), jnp.bfloat16),
        ),
        in_specs=[vmem()] * 4,
        out_specs=(vmem(),) * 3,
        compiler_params=SMALL,
        name="norm_rows",
    )(own, got, pack, gain)


def join_kernel(starts, *refs):
    out_ref = refs[-1]
    at = 0
    for start, piece in zip(starts, refs[:-1]):
        height = piece.shape[0] - start
        out_ref[at : at + height, :] = piece[start:, :]
        at += height


def join_rows(pieces, starts, cost, name):
    height = sum(piece.shape[0] - start for piece, start in zip(pieces, starts))
    return pl.pallas_call(
        functools.partial(join_kernel, starts),
        out_shape=jax.ShapeDtypeStruct((height, pieces[0].shape[1]), jnp.bfloat16),
        in_specs=[vmem()] * len(pieces),
        out_specs=vmem(),
        compiler_params=SMALL,
        cost_estimate=cost,
        name=name,
    )(*pieces)


def hidden_units(groups, group_ref, x_ref, w_refs, h_ref, ready):
    rows = x_ref.shape[0]
    width = w_refs[0].shape[0]
    hidden = h_ref.shape[1] // 2
    lane = lax.broadcasted_iota(jnp.int32, (rows, LANES), 1)
    packed = x_ref[:, width:].astype(jnp.float32)
    for e in (1, 0):
        group = group_ref[0] ^ e
        share = jnp.sum(
            jnp.where((lane == group) | (lane == group + groups), packed, 0.0),
            axis=1,
            keepdims=True,
        )
        ready(e)
        both = jnp.dot(x_ref[:, :width], w_refs[e][...], preferred_element_type=jnp.float32)
        gate, up = both[:, :hidden], both[:, hidden:]
        h_ref[:, e * hidden : (e + 1) * hidden] = (
            share * up * (gate / (1.0 + jnp.exp(-gate)))
        ).astype(jnp.bfloat16)


DOWN_BLOCK = 512


def gather_pieces(pieces, x_ref):
    at = 0
    for piece in pieces:
        x_ref[at : at + piece.shape[0], :] = piece[...]
        at += piece.shape[0]
    if at < x_ref.shape[0]:
        x_ref[at:, :] = jnp.zeros((x_ref.shape[0] - at, x_ref.shape[1]), jnp.bfloat16)


def merge_kernel(wg1, wu1, wg0, wu0, wd0, wd1, w0_ref, w1_ref, down_ref, sems):
    hidden = wg0.shape[1]
    fetches = [
        pltpu.make_async_copy(source, target, sems.at[i])
        for i, (source, target) in enumerate(
            (
                (wg0, w0_ref.at[:, :hidden]),
                (wu0, w0_ref.at[:, hidden:]),
                (wd0, down_ref.at[:hidden, :]),
                (wd1, down_ref.at[hidden:, :]),
                (wg1, w1_ref.at[:, :hidden]),
                (wu1, w1_ref.at[:, hidden:]),
            )
        )
    ]
    for fetch in fetches:
        fetch.start()
    for fetch in fetches:
        fetch.wait()


def merge_weights(weights, partner_weights):
    wg0, wu0, wd0 = weights
    wg1, wu1, wd1 = partner_weights
    width, hidden = wg0.shape
    return pl.pallas_call(
        merge_kernel,
        out_shape=(
            jax.ShapeDtypeStruct((width, 2 * hidden), jnp.bfloat16),
            jax.ShapeDtypeStruct((width, 2 * hidden), jnp.bfloat16),
            jax.ShapeDtypeStruct((2 * hidden, width), jnp.bfloat16),
        ),
        in_specs=[pl.BlockSpec(memory_space=pl.ANY)] * 2 + [hbm()] * 4,
        out_specs=(vmem(),) * 3,
        scratch_shapes=[pltpu.SemaphoreType.DMA((6,))],
        compiler_params=SMALL,
        cost_estimate=pl.CostEstimate(
            flops=0, bytes_accessed=24 * width * hidden, transcendentals=0
        ),
        name="merge_weights",
    )(wg1, wu1, *[stay(w) for w in (wg0, wu0, wd0, wd1)])


def near_kernel(
    groups, group_ref, r0, r1, r2, r3, far_ref, z1_ref, w0_ref, w1_ref, down_ref,
    out_ref, z1_out_ref, x_ref, h_ref,
):
    gather_pieces((r0, r1, r2, r3, far_ref, z1_ref), x_ref)
    hidden_units(groups, group_ref, x_ref, (w0_ref, w1_ref), h_ref, lambda e: None)
    height = out_ref.shape[0]
    for col in range(0, down_ref.shape[1], DOWN_BLOCK):
        cols = slice(col, col + DOWN_BLOCK)
        down = jnp.dot(h_ref[...], down_ref[:, cols], preferred_element_type=jnp.float32)
        out_ref[:, cols] = down[:height]
        z1_out_ref[:, cols] = down[height : height + z1_ref.shape[0]].astype(jnp.bfloat16)


def expert_cost(rows, width, hidden):
    return pl.CostEstimate(
        flops=12 * rows * width * hidden,
        bytes_accessed=12 * width * hidden,
        transcendentals=2 * rows * hidden,
    )


def near_rows(groups, group, rows, far, near_z, w0, w1, down):
    height = 4 * rows[0].shape[0] + far.shape[0]
    padded = -(-(height + near_z.shape[0]) // 16) * 16
    width, hidden = w1.shape[0], w1.shape[1] // 2
    return pl.pallas_call(
        functools.partial(near_kernel, groups),
        out_shape=(
            jax.ShapeDtypeStruct((height, width), jnp.float32),
            jax.ShapeDtypeStruct((near_z.shape[0], width), jnp.bfloat16),
        ),
        in_specs=[smem()] + [vmem()] * 9,
        out_specs=(vmem(),) * 2,
        scratch_shapes=[
            pltpu.VMEM((padded, width + LANES), jnp.bfloat16),
            pltpu.VMEM((padded, 2 * hidden), jnp.bfloat16),
        ],
        compiler_params=pltpu.CompilerParams(vmem_limit_bytes=24 * MIB),
        cost_estimate=expert_cost(height, width, hidden),
        name="near_rows",
    )(group, *rows, far, near_z, w0, w1, down)


def piece_kernel(groups, count, group_ref, *refs):
    pieces, (w0_ref, w1_ref, down_ref) = refs[:count], refs[count : count + 3]
    outs, (x_ref, h_ref) = refs[count + 3 : 2 * count + 3], refs[2 * count + 3 :]
    gather_pieces(pieces, x_ref)
    hidden_units(groups, group_ref, x_ref, (w0_ref, w1_ref), h_ref, lambda e: None)
    for col in range(0, down_ref.shape[1], DOWN_BLOCK):
        cols = slice(col, col + DOWN_BLOCK)
        down = jnp.dot(h_ref[...], down_ref[:, cols], preferred_element_type=jnp.float32)
        at = 0
        for out in outs:
            out[:, cols] = down[at : at + out.shape[0]].astype(jnp.bfloat16)
            at += out.shape[0]


def piece_rows(groups, group, pieces, w0, w1, down):
    count = len(pieces)
    height = sum(piece.shape[0] for piece in pieces)
    padded = -(-height // 16) * 16
    width, hidden = w1.shape[0], w1.shape[1] // 2
    return pl.pallas_call(
        functools.partial(piece_kernel, groups, count),
        out_shape=tuple(
            jax.ShapeDtypeStruct((piece.shape[0], width), jnp.bfloat16) for piece in pieces
        ),
        in_specs=[smem()] + [vmem()] * (count + 3),
        out_specs=(vmem(),) * count,
        scratch_shapes=[
            pltpu.VMEM((padded, width + LANES), jnp.bfloat16),
            pltpu.VMEM((padded, 2 * hidden), jnp.bfloat16),
        ],
        compiler_params=pltpu.CompilerParams(vmem_limit_bytes=24 * MIB),
        cost_estimate=expert_cost(height, width, hidden),
        name="piece_rows",
    )(group, *pieces, w0, w1, down)


def plane_sum_kernel(near_ref, g1, g2, g3, m1, m2, m3):
    far = m1.shape[0]
    start = near_ref.shape[0] - 3 * far
    for j, out in enumerate((m1, m2, m3)):
        rows = slice(j * far, (j + 1) * far)
        total = near_ref[start + j * far : start + (j + 1) * far, :]
        for got in (g1, g2, g3):
            total = total + got[rows, :].astype(jnp.float32)
        out[...] = total.astype(jnp.bfloat16)


def plane_sum(near, got):
    far, width = got[0].shape[0] // 3, got[0].shape[1]
    return pl.pallas_call(
        plane_sum_kernel,
        out_shape=tuple(jax.ShapeDtypeStruct((far, width), jnp.bfloat16) for _ in range(3)),
        in_specs=[vmem()] * 4,
        out_specs=(vmem(),) * 3,
        compiler_params=SMALL,
        name="plane_sum",
    )(near, *got)


def first_sum_kernel(rows, near_ref, g1, out_ref):
    near = g1.shape[0] // 4
    for i in range(4):
        there = slice(i * near, (i + 1) * near)
        out_ref[there, :] = near_ref[(i + 1) * rows - near : (i + 1) * rows, :] + g1[
            there, :
        ].astype(jnp.float32)


def first_sum(near, got, rows):
    return pl.pallas_call(
        functools.partial(first_sum_kernel, rows),
        out_shape=jax.ShapeDtypeStruct(got.shape, jnp.float32),
        in_specs=[vmem()] * 2,
        out_specs=vmem(),
        compiler_params=SMALL,
        cost_estimate=LATE,
        name="first_sum",
    )(near, got)


def column_sum_kernel(near_ref, first_ref, g2, g3, own_ref, m1, m2, m3):
    rows = own_ref.shape[0]
    near = first_ref.shape[0] // 4
    far = rows - near
    for i, out in enumerate((own_ref, m1, m2, m3)):
        out[:far, :] = near_ref[i * rows : i * rows + far, :].astype(out.dtype)
        total = first_ref[i * near : (i + 1) * near, :]
        for got in (g2, g3):
            total = total + got[i * near : (i + 1) * near, :].astype(jnp.float32)
        out[far:, :] = total.astype(out.dtype)


def column_sum(near, first, got, rows):
    width = near.shape[1]
    kinds = (jnp.float32, jnp.bfloat16, jnp.bfloat16, jnp.bfloat16)
    return pl.pallas_call(
        column_sum_kernel,
        out_shape=tuple(jax.ShapeDtypeStruct((rows, width), kind) for kind in kinds),
        in_specs=[vmem()] * 4,
        out_specs=(vmem(),) * 4,
        compiler_params=SMALL,
        cost_estimate=LATE,
        name="column_sum",
    )(near, first, *got)


def total_kernel(state_ref, own_ref, z1, z2, z3, total_ref):
    total_ref[...] = state_ref[...] + own_ref[...]
    far = z1.shape[0]
    part = total_ref[:far, :]
    for got in (z1, z2, z3):
        part = part + got[...].astype(jnp.float32)
    total_ref[:far, :] = part


def total_rows(state, own, column):
    return pl.pallas_call(
        total_kernel,
        out_shape=jax.ShapeDtypeStruct(state.shape, jnp.float32),
        in_specs=[vmem()] * 5,
        out_specs=vmem(),
        compiler_params=SMALL,
        cost_estimate=LATE,
        name="total_rows",
    )(state, own, *column)


def final_kernel(total_ref, p1, p2, p3, gain_ref, out_ref):
    total = total_ref[...]
    for got in (p1, p2, p3):
        total = total + got[...].astype(jnp.float32)
    out_ref[...] = rms_scale(total, gain_ref[...]).astype(jnp.bfloat16)


def final_rows(total, plane, gain):
    return pl.pallas_call(
        final_kernel,
        out_shape=jax.ShapeDtypeStruct(total.shape, jnp.bfloat16),
        in_specs=[vmem()] * 5,
        out_specs=vmem(),
        compiler_params=SMALL,
        name="final_rows",
    )(total, *plane, gain)


def place(z, y, c, x):
    return ((z * 2 + y) * 2 + c) * 2 + x


def swap(value, dz, dy, dc, dx):
    pairs = [
        (place(z, y, c, x), place(z ^ dz, y ^ dy, c ^ dc, x ^ dx))
        for z in range(4)
        for y in range(2)
        for c in range(2)
        for x in range(2)
    ]
    return lax.ppermute(value, ALL, pairs)


PLANE = ((0, 0), (1, 1), (0, 1), (1, 0))


def swap_z(pieces):
    return tuple(swap(piece, d, 0, 0, 0) for d, piece in zip((1, 2, 3), pieces))


def swap_plane(pieces):
    return tuple(swap(piece, 0, dy, 0, dx) for (dy, dx), piece in zip(PLANE[1:], pieces))


def local_dense(
    queries, fresh_key_value, key_value_cache, request_page_index, cache_length_rows, residual,
    w_out, gain_in, route_ids, route_weights, expert_home, w_gate, w_up, w_down, gain_out,
):
    tp_index = lax.axis_index("tp")
    req_index = lax.axis_index("req")
    tokens, width = residual.shape
    half = tokens // 2
    far = half * 3 // 4
    groups = expert_home.shape[0]
    weights = (w_gate[0], w_up[0], w_down[0])
    partner_weights = tuple(swap(stay(w), 0, 0, 1, 0) for w in weights)
    group = req_index.reshape(1)
    tp_index, pages = tp_index.reshape(1), request_page_index.T
    sent, *kept = other_terms(
        pages, cache_length_rows, tp_index, group, queries, fresh_key_value, key_value_cache, w_out
    )
    own_state, pack, last_gain = own_terms(
        pages, cache_length_rows, tp_index, expert_home, kept, residual, route_ids.T,
        route_weights.T, gain_out[None, :],
    )
    got, partner_weights = barrier(swap(sent, 0, 0, 0, 1), partner_weights)
    state, far_rows, last_rows = norm_rows(own_state, got, pack, gain_in[None, :], far)
    rows = join_rows((far_rows, last_rows), (0, 0), LATE, "own_rows")
    z_rows = swap_z((far_rows,) * 3)
    nearest, partner_weights = barrier(z_rows[0], partner_weights)
    kept = merge_weights(weights, partner_weights)
    far_rows, kept = barrier(z_rows[1:], kept)
    z_rows = (nearest,) + far_rows
    onward_plane = join_rows(z_rows, (0, 0, 0), LATE, "onward_plane")
    plane_rows, far_pieces = barrier(swap_plane((rows,) * 3), onward_plane)
    plane_rows = (rows,) + plane_rows
    onward_z = join_rows(plane_rows, (far,) * 4, None, "onward_z")
    z_pieces = swap_z((onward_z,) * 3)
    plane_pieces = swap_plane((onward_plane,) * 3)
    near, near_part = near_rows(groups, group, plane_rows, far_pieces, z_pieces[0], *kept)
    parts = piece_rows(groups, group, z_pieces[1:] + plane_pieces, *kept)
    z_parts, plane_parts = swap_z((near_part,) + parts[:2]), swap_plane(parts[2:])
    first = first_sum(near, z_parts[0], half)
    plane_parts, first = barrier(plane_parts, first)
    far_sums = plane_sum(near, plane_parts)
    last_parts, far_sums = barrier(z_parts[1:], far_sums)
    own, *near_sums = column_sum(near, first, last_parts, half)
    total = total_rows(state, own, swap_z(far_sums))
    last_plane, total = barrier(swap_plane(near_sums), total)
    return final_rows(total, last_plane, last_gain)


def solution(mesh):
    dense = mesh.shape["req"] == 16 and mesh.shape["tp"] == 2
    return jax.shard_map(
        local_dense if dense else local_sparse,
        mesh=mesh,
        in_specs=(
            P("req", "tp"),
            P("req", "tp"),
            P("req", None, "tp"),
            P("req", None),
            P("req"),
            P("req", None),
            P("tp", None),
            P(),
            P("req", None),
            P("req", None),
            P(),
            P("req", None, "tp"),
            P("req", None, "tp"),
            P("req", "tp", None),
            P(),
        ),
        out_specs=P(("req", "tp"), None),
        check_vma=False,
    )
```

```python
import functools

import jax
import jax.numpy as jnp
from jax import lax
from jax.experimental import pallas as pl
from jax.experimental.pallas import tpu as pltpu
from jax.sharding import PartitionSpec as P

HEAD_WIDTH = 128
TOPK = 8
PRE_DEV = 56


EPSILON = 1e-06


def rms_scale(value_rows, gain_row):
    mean_square = jnp.mean(value_rows * value_rows, axis=-1, keepdims=True)
    return value_rows * lax.rsqrt(mean_square + EPSILON) * gain_row


def softmax_rounded(scores):
    row_peak = jnp.max(scores, axis=-1, keepdims=True)
    weights = jnp.exp(scores - row_peak)
    return (weights / jnp.sum(weights, axis=-1, keepdims=True)).astype(jnp.bfloat16)


def group_attention(queries, fresh_key_value, page_pool, page_rows, lengths):
    tokens_here = queries.shape[0]
    kv_heads = fresh_key_value.shape[1] // (2 * HEAD_WIDTH)
    group_size = queries.shape[1] // (HEAD_WIDTH * kv_heads)
    score_scale = HEAD_WIDTH ** (-0.5)
    split_query = queries.reshape(tokens_here, kv_heads, group_size, HEAD_WIDTH)
    fresh_kv = fresh_key_value.reshape(tokens_here, kv_heads, 2, HEAD_WIDTH)
    gathered_pages = page_pool[page_rows]
    cached = gathered_pages.reshape(page_rows.shape[0], -1, kv_heads, 2, HEAD_WIDTH)
    places = jnp.arange(cached.shape[1], dtype=jnp.int32)
    prefill_query = split_query[:PRE_DEV]
    prefill_fresh = fresh_kv[:PRE_DEV]
    cache_scores = (
        jnp.einsum(
            "ikgd,ckd->kgic", prefill_query, cached[0, :, :, 0], preferred_element_type=jnp.float32
        )
        * score_scale
    )
    cache_scores = jnp.where(places < lengths[0], cache_scores, -jnp.inf)
    block_scores = (
        jnp.einsum(
            "ikgd,jkd->kgij",
            prefill_query,
            prefill_fresh[:, :, 0],
            preferred_element_type=jnp.float32,
        )
        * score_scale
    )
    causal = jnp.arange(PRE_DEV)[:, None] >= jnp.arange(PRE_DEV)[None, :]
    block_scores = jnp.where(causal, block_scores, -jnp.inf)
    prefill_probs = softmax_rounded(jnp.concatenate([cache_scores, block_scores], axis=3))
    prefill_values = jnp.concatenate([cached[0, :, :, 1], prefill_fresh[:, :, 1]], axis=0)
    prefill_out = jnp.einsum(
        "kgic,ckd->ikgd", prefill_probs, prefill_values, preferred_element_type=jnp.float32
    )
    decode_query = split_query[PRE_DEV:]
    decode_fresh = fresh_kv[PRE_DEV:]
    decode_scores = (
        jnp.einsum(
            "rkgd,rckd->rkgc", decode_query, cached[1:, :, :, 0], preferred_element_type=jnp.float32
        )
        * score_scale
    )
    decode_scores = jnp.where(
        places[None, None, None, :] < lengths[1:, None, None, None], decode_scores, -jnp.inf
    )
    own_scores = (
        jnp.einsum(
            "rkgd,rkd->rkg", decode_query, decode_fresh[:, :, 0], preferred_element_type=jnp.float32
        )[..., None]
        * score_scale
    )
    decode_probs = softmax_rounded(jnp.concatenate([decode_scores, own_scores], axis=3))
    decode_values = jnp.concatenate([cached[1:, :, :, 1], decode_fresh[:, None, :, 1]], axis=1)
    decode_out = jnp.einsum(
        "rkgc,rckd->rkgd", decode_probs, decode_values, preferred_element_type=jnp.float32
    )
    joined = jnp.concatenate([prefill_out, decode_out], axis=0)
    return joined.reshape(tokens_here, -1).astype(jnp.bfloat16)


def slot_positions(block_owner, experts, capacity):
    flat_owner = block_owner.reshape(-1)
    onehot = (flat_owner[:, None] == jnp.arange(experts, dtype=jnp.int32)[None, :]).astype(
        jnp.int32
    )
    earlier = jnp.cumsum(onehot, axis=0) - onehot
    slot_index = jnp.sum(earlier * onehot, axis=1)
    return (flat_owner * capacity + slot_index).reshape(block_owner.shape)


def place_matrix(positions, slots_total):
    matches = positions[None, :, :] == jnp.arange(slots_total, dtype=jnp.int32)[:, None, None]
    return jnp.any(matches, axis=2).astype(jnp.bfloat16)


def local_sparse(
    queries,
    fresh_key_value,
    key_value_cache,
    request_page_index,
    cache_length_rows,
    residual,
    w_out,
    gain_in,
    route_ids,
    route_weights,
    expert_home,
    w_gate,
    w_up,
    w_down,
    gain_out,
):
    tp_size = lax.axis_size("tp")
    req_size = lax.axis_size("req")
    tp_index = lax.axis_index("tp")
    model_width = residual.shape[1]
    tokens_here = residual.shape[0]
    quarter = tokens_here // tp_size
    experts = expert_home.shape[0]
    capacity = min(quarter, max(2, 2 * quarter * TOPK // experts))
    context = group_attention(
        queries, fresh_key_value, key_value_cache, request_page_index, cache_length_rows
    )
    head_terms = jnp.dot(context, w_out, preferred_element_type=jnp.float32)
    state = residual.astype(jnp.float32) + lax.psum(head_terms, "tp")
    owners = jnp.sum(
        jnp.where(
            route_ids[:, :, None] == jnp.arange(experts, dtype=jnp.int32)[None, None, :],
            expert_home[None, None, :],
            0,
        ),
        axis=2,
    )
    shares = route_weights / jnp.sum(route_weights, axis=1, keepdims=True)
    own_start = tp_index * quarter
    own_state = lax.dynamic_slice_in_dim(state, own_start, quarter, 0)
    own_shares = lax.dynamic_slice_in_dim(shares, own_start, quarter, 0)
    normed_all = rms_scale(state, gain_in).astype(jnp.bfloat16)
    positions_all = jax.vmap(lambda block_owner: slot_positions(block_owner, experts, capacity))(
        owners.reshape(tp_size, quarter, TOPK)
    )
    placing = jax.vmap(lambda positions: place_matrix(positions, experts * capacity))(positions_all)
    outgoing = jnp.einsum(
        "qmi,qid->qmd",
        placing,
        normed_all.reshape(tp_size, quarter, model_width),
        preferred_element_type=jnp.float32,
    )
    outgoing = outgoing.astype(jnp.bfloat16).reshape(tp_size, experts, capacity, model_width)
    incoming = lax.all_to_all(outgoing, "req", split_axis=1, concat_axis=1, tiled=True)
    own_positions = lax.dynamic_index_in_dim(positions_all, tp_index, 0, keepdims=False)
    expert_rows = incoming.reshape(-1, model_width)
    gate_proj = jnp.dot(expert_rows, w_gate[0], preferred_element_type=jnp.float32)
    up_proj = jnp.dot(expert_rows, w_up[0], preferred_element_type=jnp.float32)
    inner_units = (jax.nn.silu(gate_proj) * up_proj).astype(jnp.bfloat16)
    summed = lax.psum_scatter(
        jnp.dot(inner_units, w_down[0], preferred_element_type=jnp.float32).astype(jnp.bfloat16),
        "tp",
        scatter_dimension=0,
        tiled=True,
    )
    results = summed.reshape(req_size, capacity, model_width)
    returned = lax.all_to_all(results, "req", split_axis=0, concat_axis=0, tiled=True).reshape(
        -1, model_width
    )
    picked = returned[own_positions]
    mixture = jnp.sum(own_shares[:, :, None] * picked.astype(jnp.float32), axis=1)
    return rms_scale(own_state + mixture, gain_out).astype(jnp.bfloat16)


ALL = ("req", "tp")
MASKED = -1e30
LANES = 128
MIB = 1024 * 1024
SMALL = pltpu.CompilerParams(vmem_limit_bytes=8 * MIB)


def vmem():
    return pl.BlockSpec(memory_space=pltpu.VMEM)


def smem():
    return pl.BlockSpec(memory_space=pltpu.SMEM)


def hbm():
    return pl.BlockSpec(memory_space=pltpu.HBM)


def stay(value):
    return pltpu.with_memory_space_constraint(value, pltpu.HBM)


def barrier(*values):
    return lax.optimization_barrier(values)


def multiplicity(page_rows, length, pool_pages, page_tokens):
    rows = page_rows[0].shape[0]
    lane = lax.broadcasted_iota(jnp.int32, (rows, page_tokens), 1)
    parts = []
    for page in range(pool_pages):
        count = jnp.zeros((rows, page_tokens), jnp.float32)
        for slot, named in enumerate(page_rows):
            hit = (named == page) & (lane + slot * page_tokens < length)
            count = count + jnp.where(hit, 1.0, 0.0)
        parts.append(count)
    return jnp.concatenate(parts, axis=1)


def pack_shares(ids, routed, home_ref):
    groups = home_ref.shape[0]
    choices, tokens = ids.shape
    spot = lax.broadcasted_iota(jnp.int32, (groups, tokens), 0)
    shares = routed / jnp.sum(routed, axis=0, keepdims=True)
    by_expert = jnp.zeros((groups, tokens), jnp.float32)
    for k in range(choices):
        by_expert = by_expert + jnp.where(spot == ids[k : k + 1, :], shares[k : k + 1, :], 0.0)
    by_home = jnp.zeros((groups, tokens), jnp.float32)
    for e in range(groups):
        by_home = by_home + jnp.where(spot == home_ref[e], by_expert[e : e + 1, :], 0.0)
    rounded = by_home.astype(jnp.bfloat16).astype(jnp.float32)
    tall = jnp.concatenate(
        [rounded, by_home - rounded, jnp.zeros((LANES - 2 * groups, tokens), jnp.float32)], axis=0
    )
    square = jnp.concatenate([tall, jnp.zeros((LANES, LANES - tokens), jnp.float32)], axis=1)
    return jnp.transpose(square)


def count_positions(pages_ref, lengths_ref, pool_pages, page_tokens, count_ref):
    slots, requests = pages_ref.shape
    decodes = requests - 1
    row = lax.broadcasted_iota(jnp.int32, (decodes, page_tokens), 0)

    def by_row(read):
        value = jnp.zeros((decodes, page_tokens), jnp.int32)
        for j in range(decodes):
            value = jnp.where(row == j, read(j + 1), value)
        return value

    full = lambda scalar: jnp.full((decodes, page_tokens), scalar, jnp.int32)
    first = multiplicity(
        [full(pages_ref[s, 0]) for s in range(slots)], full(lengths_ref[0]), pool_pages, page_tokens
    )
    later = multiplicity(
        [by_row(lambda j, s=s: pages_ref[s, j]) for s in range(slots)],
        by_row(lambda j: lengths_ref[j]),
        pool_pages,
        page_tokens,
    )
    count_ref[...] = jnp.concatenate([first] * (PRE_DEV // decodes) + [later], axis=0)


def attend(start, q_ref, fresh_ref, cache_ref, count_ref, context_ref):
    rows = context_ref.shape[0]
    tokens = q_ref.shape[0]
    kv_heads = fresh_ref.shape[1] // (2 * HEAD_WIDTH)
    group = q_ref.shape[1] // (HEAD_WIDTH * kv_heads)
    query_place = start + lax.broadcasted_iota(jnp.int32, (rows, tokens), 0)
    key_place = lax.broadcasted_iota(jnp.int32, (rows, tokens), 1)
    seen = (key_place == query_place) | ((key_place <= query_place) & (query_place < PRE_DEV))
    seen = jnp.concatenate([jnp.where(seen, 1.0, 0.0)] * group, axis=0)
    visible = jnp.concatenate([count_ref[pl.ds(start, rows), :]] * group, axis=0)
    scale = HEAD_WIDTH**-0.5
    contract_last = (((1,), (1,)), ((), ()))
    for k in range(kv_heads):
        key_at, value_at = 2 * k * HEAD_WIDTH, (2 * k + 1) * HEAD_WIDTH
        heads = [k * group + g for g in range(group)]
        query = jnp.concatenate(
            [q_ref[pl.ds(start, rows), h * HEAD_WIDTH : (h + 1) * HEAD_WIDTH] for h in heads],
            axis=0,
        )
        keys = cache_ref[:, :, key_at : key_at + HEAD_WIDTH].reshape(-1, HEAD_WIDTH)
        values = cache_ref[:, :, value_at : value_at + HEAD_WIDTH].reshape(-1, HEAD_WIDTH)
        old = lax.dot_general(query, keys, contract_last, preferred_element_type=jnp.float32)
        new = lax.dot_general(
            query,
            fresh_ref[:, key_at : key_at + HEAD_WIDTH],
            contract_last,
            preferred_element_type=jnp.float32,
        )
        old = jnp.where(visible > 0, old * scale, MASKED)
        new = jnp.where(seen > 0, new * scale, MASKED)
        peak = jnp.maximum(
            jnp.max(old, axis=1, keepdims=True), jnp.max(new, axis=1, keepdims=True)
        )
        old = jnp.exp(old - peak) * visible
        new = jnp.exp(new - peak) * seen
        inverse = 1.0 / (
            jnp.sum(old, axis=1, keepdims=True) + jnp.sum(new, axis=1, keepdims=True)
        )
        mixed = jnp.dot(
            (old * inverse).astype(jnp.bfloat16), values, preferred_element_type=jnp.float32
        ) + jnp.dot(
            (new * inverse).astype(jnp.bfloat16),
            fresh_ref[:, value_at : value_at + HEAD_WIDTH],
            preferred_element_type=jnp.float32,
        )
        mixed = mixed.astype(jnp.bfloat16)
        for g, h in enumerate(heads):
            context_ref[:, h * HEAD_WIDTH : (h + 1) * HEAD_WIDTH] = mixed[g * rows : (g + 1) * rows]


OUT_BLOCK = 512
W_PIECES = 8


def other_kernel(
    pages_ref, lengths_ref, tp_ref, group_ref, q_hbm, fresh_hbm, cache_hbm, w_hbm,
    send_ref, q_ref, fresh_ref, cache_ref, w_ref, count_ref, context_ref, terms_ref, sems,
):
    moves = [(q_hbm, q_ref), (fresh_hbm, fresh_ref), (cache_hbm, cache_ref)]
    depth = w_ref.shape[0] // W_PIECES
    parts = [slice(i * depth, (i + 1) * depth) for i in range(W_PIECES)]
    moves += [(w_hbm.at[part, :], w_ref.at[part, :]) for part in parts]
    fetches = [
        pltpu.make_async_copy(source, target, sems.at[i])
        for i, (source, target) in enumerate(moves)
    ]
    for fetch in fetches:
        fetch.start()
    half = context_ref.shape[0]
    start = pl.multiple_of((1 - tp_ref[0]) * half, half)
    count_positions(pages_ref, lengths_ref, cache_ref.shape[0], cache_ref.shape[1], count_ref)
    for fetch in fetches[:3]:
        fetch.wait()
    attend(start, q_ref, fresh_ref, cache_ref, count_ref, context_ref)
    for i, part in enumerate(parts):
        fetches[3 + i].wait()
        for at in range(0, w_ref.shape[1], OUT_BLOCK):
            cols = slice(at, at + OUT_BLOCK)
            terms = jnp.dot(
                context_ref[:, part], w_ref[part, cols], preferred_element_type=jnp.float32
            )
            terms_ref[:, cols] = terms if i == 0 else terms_ref[:, cols] + terms
    send_ref[...] = terms_ref[...].astype(jnp.bfloat16)


def other_terms(pages, lengths, tp_index, group, queries, fresh, cache, w_out):
    half = queries.shape[0] // 2
    moved = (queries, fresh, cache, w_out)
    return pl.pallas_call(
        other_kernel,
        out_shape=(jax.ShapeDtypeStruct((half, w_out.shape[1]), jnp.bfloat16),)
        + tuple(jax.ShapeDtypeStruct(v.shape, v.dtype) for v in moved),
        in_specs=[smem()] * 4 + [hbm()] * 4,
        out_specs=(vmem(),) * 5,
        scratch_shapes=[
            pltpu.VMEM((queries.shape[0], cache.shape[0] * cache.shape[1]), jnp.float32),
            pltpu.VMEM((half, queries.shape[1]), jnp.bfloat16),
            pltpu.VMEM((half, w_out.shape[1]), jnp.float32),
            pltpu.SemaphoreType.DMA((3 + W_PIECES,)),
        ],
        compiler_params=pltpu.CompilerParams(vmem_limit_bytes=16 * MIB),
        name="other_terms",
    )(stay(pages), stay(lengths), tp_index, group, *[stay(v) for v in moved])


def own_kernel(
    pages_ref, lengths_ref, tp_ref, home_ref, q_ref, fresh_ref, cache_ref, w_ref,
    residual_hbm, ids_hbm, routed_hbm, gain_hbm,
    own_ref, pack_ref, gain_ref, residual_ref, ids_ref, routed_ref, count_ref, context_ref, every_ref, sems,
):
    moves = (
        (ids_hbm, ids_ref), (routed_hbm, routed_ref), (residual_hbm, residual_ref),
        (gain_hbm, gain_ref),
    )
    fetches = [
        pltpu.make_async_copy(source, target, sems.at[i])
        for i, (source, target) in enumerate(moves)
    ]
    for fetch in fetches:
        fetch.start()
    half = context_ref.shape[0]
    start = pl.multiple_of(tp_ref[0] * half, half)
    count_positions(pages_ref, lengths_ref, cache_ref.shape[0], cache_ref.shape[1], count_ref)
    attend(start, q_ref, fresh_ref, cache_ref, count_ref, context_ref)
    for fetch in fetches:
        fetch.wait()
    every_ref[...] = pack_shares(ids_ref[...], routed_ref[...], home_ref)
    pack_ref[...] = every_ref[pl.ds(start, half), :].astype(jnp.bfloat16)
    for at in range(0, w_ref.shape[1], OUT_BLOCK):
        cols = slice(at, at + OUT_BLOCK)
        own_ref[:, cols] = residual_ref[pl.ds(start, half), cols].astype(jnp.float32) + jnp.dot(
            context_ref[...], w_ref[:, cols], preferred_element_type=jnp.float32
        )


def own_terms(pages, lengths, tp_index, home, kept, residual, ids, routed, gain):
    tokens, width = residual.shape
    half = tokens // 2
    queries, _, cache, _ = kept
    moved = (residual, ids, routed)
    return pl.pallas_call(
        own_kernel,
        out_shape=(
            jax.ShapeDtypeStruct((half, width), jnp.float32),
            jax.ShapeDtypeStruct((half, LANES), jnp.bfloat16),
            jax.ShapeDtypeStruct(gain.shape, gain.dtype),
        ),
        in_specs=[smem()] * 4 + [vmem()] * 4 + [hbm()] * 4,
        out_specs=(vmem(),) * 3,
        scratch_shapes=[pltpu.VMEM(v.shape, v.dtype) for v in moved]
        + [
            pltpu.VMEM((tokens, cache.shape[0] * cache.shape[1]), jnp.float32),
            pltpu.VMEM((half, queries.shape[1]), jnp.bfloat16),
            pltpu.VMEM((LANES, LANES), jnp.float32),
            pltpu.SemaphoreType.DMA((4,)),
        ],
        compiler_params=pltpu.CompilerParams(vmem_limit_bytes=16 * MIB),
        name="own_terms",
    )(stay(pages), stay(lengths), tp_index, stay(home), *kept, *[stay(v) for v in moved + (gain,)])


LATE = pl.CostEstimate(flops=3 * 10**10, bytes_accessed=1 << 20, transcendentals=0)


def norm_kernel(own_ref, got_ref, pack_ref, gain_ref, state_ref, far_ref, near_ref):
    state = own_ref[...] + got_ref[...].astype(jnp.float32)
    state_ref[...] = state
    normed = rms_scale(state, gain_ref[...]).astype(jnp.bfloat16)
    width = state.shape[1]
    far = far_ref.shape[0]
    far_ref[:, :width] = normed[:far]
    far_ref[:, width:] = pack_ref[:far, :]
    near_ref[:, :width] = normed[far:]
    near_ref[:, width:] = pack_ref[far:, :]


def norm_rows(own, got, pack, gain, far):
    rows, width = own.shape
    return pl.pallas_call(
        norm_kernel,
        out_shape=(
            jax.ShapeDtypeStruct((rows, width), jnp.float32),
            jax.ShapeDtypeStruct((far, width + LANES), jnp.bfloat16),
            jax.ShapeDtypeStruct((rows - far, width + LANES), jnp.bfloat16),
        ),
        in_specs=[vmem()] * 4,
        out_specs=(vmem(),) * 3,
        compiler_params=SMALL,
        name="norm_rows",
    )(own, got, pack, gain)


def join_kernel(starts, *refs):
    out_ref = refs[-1]
    at = 0
    for start, piece in zip(starts, refs[:-1]):
        height = piece.shape[0] - start
        out_ref[at : at + height, :] = piece[start:, :]
        at += height


def join_rows(pieces, starts, cost, name):
    height = sum(piece.shape[0] - start for piece, start in zip(pieces, starts))
    return pl.pallas_call(
        functools.partial(join_kernel, starts),
        out_shape=jax.ShapeDtypeStruct((height, pieces[0].shape[1]), jnp.bfloat16),
        in_specs=[vmem()] * len(pieces),
        out_specs=vmem(),
        compiler_params=SMALL,
        cost_estimate=cost,
        name=name,
    )(*pieces)


def hidden_units(groups, group_ref, x_ref, w_refs, h_ref, ready):
    rows = x_ref.shape[0]
    width = w_refs[0].shape[0]
    hidden = h_ref.shape[1] // 2
    lane = lax.broadcasted_iota(jnp.int32, (rows, LANES), 1)
    packed = x_ref[:, width:].astype(jnp.float32)
    for e in (1, 0):
        group = group_ref[0] ^ e
        share = jnp.sum(
            jnp.where((lane == group) | (lane == group + groups), packed, 0.0),
            axis=1,
            keepdims=True,
        )
        ready(e)
        both = jnp.dot(x_ref[:, :width], w_refs[e][...], preferred_element_type=jnp.float32)
        gate, up = both[:, :hidden], both[:, hidden:]
        h_ref[:, e * hidden : (e + 1) * hidden] = (
            share * up * (gate / (1.0 + jnp.exp(-gate)))
        ).astype(jnp.bfloat16)


DOWN_BLOCK = 512


def gather_pieces(pieces, x_ref):
    at = 0
    for piece in pieces:
        x_ref[at : at + piece.shape[0], :] = piece[...]
        at += piece.shape[0]
    if at < x_ref.shape[0]:
        x_ref[at:, :] = jnp.zeros((x_ref.shape[0] - at, x_ref.shape[1]), jnp.bfloat16)


def near_kernel(
    groups, group_ref, r0, r1, r2, r3, far_ref, z1_ref, wg1, wu1, wg0, wu0, wd0, wd1,
    out_ref, z1_out_ref, w0_ref, w1_ref, down_ref, x_ref, h_ref, sems,
):
    hidden = wg0.shape[1]
    fetches = [
        pltpu.make_async_copy(source, target, sems.at[i])
        for i, (source, target) in enumerate(
            (
                (wg0, w0_ref.at[:, :hidden]),
                (wu0, w0_ref.at[:, hidden:]),
                (wd0, down_ref.at[:hidden, :]),
                (wd1, down_ref.at[hidden:, :]),
                (wg1, w1_ref.at[:, :hidden]),
                (wu1, w1_ref.at[:, hidden:]),
            )
        )
    ]
    for fetch in fetches:
        fetch.start()
    gather_pieces((r0, r1, r2, r3, far_ref, z1_ref), x_ref)

    def ready(e):
        for fetch in fetches[4:] if e else fetches[:2]:
            fetch.wait()

    hidden_units(groups, group_ref, x_ref, (w0_ref, w1_ref), h_ref, ready)
    fetches[2].wait()
    fetches[3].wait()
    height = out_ref.shape[0]
    for col in range(0, down_ref.shape[1], DOWN_BLOCK):
        cols = slice(col, col + DOWN_BLOCK)
        down = jnp.dot(h_ref[...], down_ref[:, cols], preferred_element_type=jnp.float32)
        out_ref[:, cols] = down[:height]
        z1_out_ref[:, cols] = down[height : height + z1_ref.shape[0]].astype(jnp.bfloat16)


def expert_cost(rows, width, hidden):
    return pl.CostEstimate(
        flops=12 * rows * width * hidden,
        bytes_accessed=12 * width * hidden,
        transcendentals=2 * rows * hidden,
    )


def near_rows(groups, group, rows, far, near_z, weights, partner_weights):
    height = 4 * rows[0].shape[0] + far.shape[0]
    padded = -(-(height + near_z.shape[0]) // 16) * 16
    width, hidden = weights[0].shape
    wg0, wu0, wd0 = weights
    wg1, wu1, wd1 = partner_weights
    return pl.pallas_call(
        functools.partial(near_kernel, groups),
        out_shape=(
            jax.ShapeDtypeStruct((height, width), jnp.float32),
            jax.ShapeDtypeStruct((near_z.shape[0], width), jnp.bfloat16),
            jax.ShapeDtypeStruct((width, 2 * hidden), jnp.bfloat16),
            jax.ShapeDtypeStruct((width, 2 * hidden), jnp.bfloat16),
            jax.ShapeDtypeStruct((2 * hidden, width), jnp.bfloat16),
        ),
        in_specs=[smem()] + [vmem()] * 8 + [hbm()] * 4,
        out_specs=(vmem(),) * 5,
        scratch_shapes=[
            pltpu.VMEM((padded, width + LANES), jnp.bfloat16),
            pltpu.VMEM((padded, 2 * hidden), jnp.bfloat16),
            pltpu.SemaphoreType.DMA((6,)),
        ],
        compiler_params=pltpu.CompilerParams(vmem_limit_bytes=24 * MIB),
        cost_estimate=expert_cost(height, width, hidden),
        name="near_rows",
    )(group, *rows, far, near_z, wg1, wu1, *[stay(w) for w in (wg0, wu0, wd0, wd1)])


def piece_kernel(groups, count, group_ref, *refs):
    pieces, (w0_ref, w1_ref, down_ref) = refs[:count], refs[count : count + 3]
    outs, (x_ref, h_ref) = refs[count + 3 : 2 * count + 3], refs[2 * count + 3 :]
    gather_pieces(pieces, x_ref)
    hidden_units(groups, group_ref, x_ref, (w0_ref, w1_ref), h_ref, lambda e: None)
    for col in range(0, down_ref.shape[1], DOWN_BLOCK):
        cols = slice(col, col + DOWN_BLOCK)
        down = jnp.dot(h_ref[...], down_ref[:, cols], preferred_element_type=jnp.float32)
        at = 0
        for out in outs:
            out[:, cols] = down[at : at + out.shape[0]].astype(jnp.bfloat16)
            at += out.shape[0]


def piece_rows(groups, group, pieces, w0, w1, down):
    count = len(pieces)
    height = sum(piece.shape[0] for piece in pieces)
    padded = -(-height // 16) * 16
    width, hidden = w1.shape[0], w1.shape[1] // 2
    return pl.pallas_call(
        functools.partial(piece_kernel, groups, count),
        out_shape=tuple(
            jax.ShapeDtypeStruct((piece.shape[0], width), jnp.bfloat16) for piece in pieces
        ),
        in_specs=[smem()] + [vmem()] * (count + 3),
        out_specs=(vmem(),) * count,
        scratch_shapes=[
            pltpu.VMEM((padded, width + LANES), jnp.bfloat16),
            pltpu.VMEM((padded, 2 * hidden), jnp.bfloat16),
        ],
        compiler_params=pltpu.CompilerParams(vmem_limit_bytes=24 * MIB),
        cost_estimate=expert_cost(height, width, hidden),
        name="piece_rows",
    )(group, *pieces, w0, w1, down)


def plane_sum_kernel(near_ref, g1, g2, g3, m1, m2, m3):
    far = m1.shape[0]
    start = near_ref.shape[0] - 3 * far
    for j, out in enumerate((m1, m2, m3)):
        rows = slice(j * far, (j + 1) * far)
        total = near_ref[start + j * far : start + (j + 1) * far, :]
        for got in (g1, g2, g3):
            total = total + got[rows, :].astype(jnp.float32)
        out[...] = total.astype(jnp.bfloat16)


def plane_sum(near, got):
    far, width = got[0].shape[0] // 3, got[0].shape[1]
    return pl.pallas_call(
        plane_sum_kernel,
        out_shape=tuple(jax.ShapeDtypeStruct((far, width), jnp.bfloat16) for _ in range(3)),
        in_specs=[vmem()] * 4,
        out_specs=(vmem(),) * 3,
        compiler_params=SMALL,
        name="plane_sum",
    )(near, *got)


def first_sum_kernel(rows, near_ref, g1, out_ref):
    near = g1.shape[0] // 4
    for i in range(4):
        there = slice(i * near, (i + 1) * near)
        out_ref[there, :] = near_ref[(i + 1) * rows - near : (i + 1) * rows, :] + g1[
            there, :
        ].astype(jnp.float32)


def first_sum(near, got, rows):
    return pl.pallas_call(
        functools.partial(first_sum_kernel, rows),
        out_shape=jax.ShapeDtypeStruct(got.shape, jnp.float32),
        in_specs=[vmem()] * 2,
        out_specs=vmem(),
        compiler_params=SMALL,
        cost_estimate=LATE,
        name="first_sum",
    )(near, got)


def column_sum_kernel(near_ref, first_ref, g2, g3, own_ref, m1, m2, m3):
    rows = own_ref.shape[0]
    near = first_ref.shape[0] // 4
    far = rows - near
    for i, out in enumerate((own_ref, m1, m2, m3)):
        out[:far, :] = near_ref[i * rows : i * rows + far, :].astype(out.dtype)
        total = first_ref[i * near : (i + 1) * near, :]
        for got in (g2, g3):
            total = total + got[i * near : (i + 1) * near, :].astype(jnp.float32)
        out[far:, :] = total.astype(out.dtype)


def column_sum(near, first, got, rows):
    width = near.shape[1]
    kinds = (jnp.float32, jnp.bfloat16, jnp.bfloat16, jnp.bfloat16)
    return pl.pallas_call(
        column_sum_kernel,
        out_shape=tuple(jax.ShapeDtypeStruct((rows, width), kind) for kind in kinds),
        in_specs=[vmem()] * 4,
        out_specs=(vmem(),) * 4,
        compiler_params=SMALL,
        cost_estimate=LATE,
        name="column_sum",
    )(near, first, *got)


def total_kernel(state_ref, own_ref, z1, z2, z3, total_ref):
    total_ref[...] = state_ref[...] + own_ref[...]
    far = z1.shape[0]
    part = total_ref[:far, :]
    for got in (z1, z2, z3):
        part = part + got[...].astype(jnp.float32)
    total_ref[:far, :] = part


def total_rows(state, own, column):
    return pl.pallas_call(
        total_kernel,
        out_shape=jax.ShapeDtypeStruct(state.shape, jnp.float32),
        in_specs=[vmem()] * 5,
        out_specs=vmem(),
        compiler_params=SMALL,
        cost_estimate=LATE,
        name="total_rows",
    )(state, own, *column)


def final_kernel(total_ref, p1, p2, p3, gain_ref, out_ref):
    total = total_ref[...]
    for got in (p1, p2, p3):
        total = total + got[...].astype(jnp.float32)
    out_ref[...] = rms_scale(total, gain_ref[...]).astype(jnp.bfloat16)


def final_rows(total, plane, gain):
    return pl.pallas_call(
        final_kernel,
        out_shape=jax.ShapeDtypeStruct(total.shape, jnp.bfloat16),
        in_specs=[vmem()] * 5,
        out_specs=vmem(),
        compiler_params=SMALL,
        name="final_rows",
    )(total, *plane, gain)


def place(z, y, c, x):
    return ((z * 2 + y) * 2 + c) * 2 + x


def swap(value, dz, dy, dc, dx):
    pairs = [
        (place(z, y, c, x), place(z ^ dz, y ^ dy, c ^ dc, x ^ dx))
        for z in range(4)
        for y in range(2)
        for c in range(2)
        for x in range(2)
    ]
    return lax.ppermute(value, ALL, pairs)


PLANE = ((0, 0), (1, 1), (0, 1), (1, 0))


def swap_z(pieces):
    return tuple(swap(piece, d, 0, 0, 0) for d, piece in zip((1, 2, 3), pieces))


def swap_plane(pieces):
    return tuple(swap(piece, 0, dy, 0, dx) for (dy, dx), piece in zip(PLANE[1:], pieces))


def local_dense(
    queries, fresh_key_value, key_value_cache, request_page_index, cache_length_rows, residual,
    w_out, gain_in, route_ids, route_weights, expert_home, w_gate, w_up, w_down, gain_out,
):
    tp_index = lax.axis_index("tp")
    req_index = lax.axis_index("req")
    tokens, width = residual.shape
    half = tokens // 2
    far = half * 3 // 4
    groups = expert_home.shape[0]
    weights = (w_gate[0], w_up[0], w_down[0])
    partner_weights = tuple(swap(stay(w), 0, 0, 1, 0) for w in weights)
    group = req_index.reshape(1)
    tp_index, pages = tp_index.reshape(1), request_page_index.T
    sent, *kept = other_terms(
        pages, cache_length_rows, tp_index, group, queries, fresh_key_value, key_value_cache, w_out
    )
    own_state, pack, last_gain = own_terms(
        pages, cache_length_rows, tp_index, expert_home, kept, residual, route_ids.T,
        route_weights.T, gain_out[None, :],
    )
    got, partner_weights = barrier(swap(sent, 0, 0, 0, 1), partner_weights)
    state, far_rows, last_rows = norm_rows(own_state, got, pack, gain_in[None, :], far)
    rows = join_rows((far_rows, last_rows), (0, 0), LATE, "own_rows")
    z_rows = swap_z((far_rows,) * 3)
    onward_plane = join_rows(z_rows, (0, 0, 0), LATE, "onward_plane")
    plane_rows, far_pieces = barrier(swap_plane((rows,) * 3), onward_plane)
    plane_rows = (rows,) + plane_rows
    onward_z = join_rows(plane_rows, (far,) * 4, None, "onward_z")
    z_pieces = swap_z((onward_z,) * 3)
    plane_pieces = swap_plane((onward_plane,) * 3)
    near, near_part, *kept = near_rows(
        groups, group, plane_rows, far_pieces, z_pieces[0], weights, partner_weights
    )
    parts = piece_rows(groups, group, z_pieces[1:] + plane_pieces, *kept)
    z_parts, plane_parts = swap_z((near_part,) + parts[:2]), swap_plane(parts[2:])
    first = first_sum(near, z_parts[0], half)
    plane_parts, first = barrier(plane_parts, first)
    far_sums = plane_sum(near, plane_parts)
    last_parts, far_sums = barrier(z_parts[1:], far_sums)
    own, *near_sums = column_sum(near, first, last_parts, half)
    total = total_rows(state, own, swap_z(far_sums))
    last_plane, total = barrier(swap_plane(near_sums), total)
    return final_rows(total, last_plane, last_gain)


def solution(mesh):
    dense = mesh.shape["req"] == 16 and mesh.shape["tp"] == 2
    return jax.shard_map(
        local_dense if dense else local_sparse,
        mesh=mesh,
        in_specs=(
            P("req", "tp"),
            P("req", "tp"),
            P("req", None, "tp"),
            P("req", None),
            P("req"),
            P("req", None),
            P("tp", None),
            P(),
            P("req", None),
            P("req", None),
            P(),
            P("req", None, "tp"),
            P("req", None, "tp"),
            P("req", "tp", None),
            P(),
        ),
        out_specs=P(("req", "tp"), None),
        check_vma=False,
    )
```
